32 devices in a mesh: grp: 2 (over y), blk: 4 (over z), head: 4 (over x, core).
Axes of the slice: x: 2, y: 2, z: 4, core: 2. Of those that a mesh axis runs over, the one named last changes fastest.
Arguments:
- queries: bfloat16 [8, 576, 4096], P('grp', None, ('head', 'blk')), parts along dimension 0, may hold values from -8 to 8
- tree_keys: bfloat16 [8, 32, 576], P('grp'), parts along dimension 0, may hold values from -8 to 8
- parents: int32 [8, 32], P('grp'), parts along dimension 0, may hold values from 0 to 30, as said below
- node_live: int32 [8, 32], P('grp'), parts along dimension 0, may hold values 0 or 1
- lengths: int32 [8], P('grp'), parts along dimension 0, may hold values from 1 to 6144, 15360 in all
- start_device: int32 [8], P('grp'), parts along dimension 0, may hold values from 0 to 3
- cache_latent: bfloat16 [8, 6144, 512], P('grp', 'blk'), parts along dimension 0, may hold values from -8 to 8
- cache_rope: bfloat16 [8, 64, 6144], P('grp', None, 'blk'), parts along dimension 0, may hold values from -8 to 8
- up_weight: bfloat16 [128, 512, 128], P('head'), may hold values from -1 to 1
Outputs:
- verified: bfloat16 [8, 32, 16384], P('grp', None, ('head', 'blk')), parts along dimension 0
The draws below stay inside these ranges and needn't reach their ends.
There are 2 independent parts, one for each index of `grp`. The reference program is written for one: setup_inputs(seed, part) draws one part's arguments, and reference() takes and returns one part's arrays. A program takes and returns all parts, laid end to end along the dimension named above; an argument that names none is the same for every part. Nothing has to cross between parts.
Inputs may be any that keep to these rules, and one draw needn't show every extreme that they name: Together the lengths fill 5/8 of the cycle's slots; one request has exactly 6144 tokens. parents[r, 0] = 0; every other node's parent has a lower index.
All inputs are finite; a program needn't handle non-finite values.
Results may differ from the reference program's by a relative error of at most 0.012.
Values may be sent and summed in bfloat16 or wider, within the bound.
No kernel may reach another device: no remote copies, remote signals or barrier semaphores. Data moves between devices by JAX's collectives and lax.ppermute only.
A program may use at most 128 MiB of HBM per device.

```python
import math
import jax
import jax.numpy as jnp
import numpy as np
from jax import lax

DL = 512
DR = 64
DN = 128
DV = 128
HEADS = 128
NODES = 32
REQS = 4
SEG = 1536
CTX = 6144
N_BLK = 4


def draw_pair(key):
    base_key = jax.random.fold_in(key, 11)
    subkeys = jax.random.split(base_key, 3)
    query_shape = (REQS, DL + DR, HEADS * NODES)
    tree_shape = (REQS, NODES, DL + DR)
    query_vals = jnp.clip(jax.random.normal(subkeys[1], query_shape), -8.0, 8.0)
    tree_vals = jnp.clip(4.0 * jax.random.normal(subkeys[2], tree_shape), -8.0, 8.0)
    return (query_vals, tree_vals)


def draw_queries(key, part):
    return draw_pair(key)[0].astype(jnp.bfloat16)


def draw_tree_keys(key, part):
    return draw_pair(key)[1].astype(jnp.bfloat16)


def draw_parents(key, part):
    parent_key = jax.random.fold_in(key, 23)
    upper_bound = jnp.maximum(jnp.arange(NODES, dtype=jnp.int32), 1)
    drawn = jax.random.randint(parent_key, (REQS, NODES), 0, upper_bound[None, :], dtype=jnp.int32)
    return drawn.at[0, NODES - 1].set(NODES - 2)


def draw_cache_latent(key, part):
    latent_key = jax.random.fold_in(key, 41)
    base = jnp.clip(1.5 * jax.random.normal(latent_key, (REQS, CTX, DL)), -8.0, 8.0)
    return base.astype(jnp.bfloat16)


def draw_cache_rope(key, part):
    rope_key = jax.random.fold_in(key, 43)
    base = jnp.clip(1.5 * jax.random.normal(rope_key, (REQS, DR, CTX)), -8.0, 8.0)
    return base.astype(jnp.bfloat16)


def touch_ends(values, stream_key, low, largest):
    index_at = [jax.random.randint(jax.random.fold_in(stream_key, axis), (), 0, length) for axis, length in enumerate(values.shape)]
    main_axis = values.shape.index(max(values.shape))
    beside = index_at[:main_axis] + [(index_at[main_axis] + 1) % values.shape[main_axis]] + index_at[main_axis + 1:]
    return values.at[tuple(index_at)].set(low).at[tuple(beside)].set(largest)


def block_levels(key, dims, pieces, low, largest):
    factor_of, own = 1.0, jax.random.fold_in(key, 6)
    for position, blocks in pieces:
        heights = jnp.exp(jax.random.uniform(jax.random.fold_in(own, position), (blocks,), jnp.float32, low / len(pieces), largest / len(pieces)))
        factor_of = factor_of * jnp.repeat(heights, dims[position] // blocks).reshape([-1 if axis == position else 1 for axis in range(len(dims))])
    return factor_of


def profile(count, total, reach, skew):
    loads = [(1 << 20) // math.isqrt(grade ** skew) + 1 for grade in range(2, count + 1)]
    spare, given = total - reach - (count - 1), [1] * (count - 1)
    while spare > 0:
        movable = [i for i in range(count - 1) if given[i] < reach]
        whole, budget = sum([loads[i] for i in movable]), spare
        for i in movable:
            more = min(reach - given[i], max(1, budget * loads[i] // whole), spare)
            given[i] = given[i] + more
            spare = spare - more
    return np.array([reach] + given)


def ragged(key, count, total, bound, skew):
    if count == 2:
        one = jax.random.randint(key, (), max(1, total - bound), min(bound, total - 1) + 1)
        return jnp.stack([one, total - one])
    tallies = jnp.asarray(profile(count, total, bound, skew), jnp.int32)
    pairs = (count - 1) // 2
    source_of, taker = tallies[1:1 + 2 * pairs:2], tallies[2:2 + 2 * pairs:2]
    margin = jnp.minimum(source_of - 1, bound - taker)
    moved = jax.random.randint(jax.random.fold_in(key, 1), (pairs,), 0, 1 << 20) % (margin + 1)
    tallies = tallies.at[1:1 + 2 * pairs:2].set(source_of - moved).at[2:2 + 2 * pairs:2].set(taker + moved)
    return tallies[jax.random.permutation(jax.random.fold_in(key, 2), count)]


def noise(stream_key, shape, spread, bound, cuts=(), held_as=jnp.bfloat16):
    result = spread * jax.random.normal(stream_key, shape, jnp.float32)
    if cuts:
        result = result * block_levels(stream_key, shape, cuts, -0.22, 0.18)
    return jnp.clip(result, -bound, bound).astype(held_as)


def setup_inputs(seed: int = 0, part: int = 0) -> dict:
    splits = jax.random.split(jax.random.key(seed), 10)
    part_keys = jax.random.split(jax.random.fold_in(splits[9], part), 10)
    queries = draw_queries(jax.random.fold_in(jax.random.fold_in(splits[9], part), 71), part)
    tree_keys = draw_tree_keys(jax.random.fold_in(jax.random.fold_in(splits[9], part), 71), part)
    parents = draw_parents(jax.random.fold_in(jax.random.fold_in(splits[9], part), 71), part)
    node_live = touch_ends((jax.random.randint(part_keys[3], (REQS, NODES), 0, 8) < 7).astype(jnp.int32), jax.random.fold_in(part_keys[3], 1), 0, 1)
    lengths = ragged(part_keys[4], REQS, REQS * N_BLK * SEG * 5 // 8, N_BLK * SEG, 2).astype(jnp.int32)
    start_device = touch_ends(jax.random.randint(part_keys[5], (REQS,), 0, N_BLK), jax.random.fold_in(part_keys[5], 1), 0, N_BLK - 1).astype(jnp.int32)
    cache_latent = draw_cache_latent(jax.random.fold_in(jax.random.fold_in(splits[9], part), 71), part)
    cache_rope = draw_cache_rope(jax.random.fold_in(jax.random.fold_in(splits[9], part), 71), part)
    up_weight = noise(splits[8], (HEADS, DL, DV), (DL // 16) ** -0.5, 1.0, ((0, 4),))
    return {"queries": queries, "tree_keys": tree_keys, "parents": parents, "node_live": node_live, "lengths": lengths, "start_device": start_device, "cache_latent": cache_latent, "cache_rope": cache_rope, "up_weight": up_weight}


def ancestor_matrix(parent_list):
    node_count = parent_list.shape[0]
    ordering = jnp.arange(node_count, dtype=jnp.int32)
    one_hop = (parent_list[:, None] == ordering[None, :]).astype(jnp.float32)
    reached = jnp.maximum(one_hop, jnp.eye(node_count, dtype=jnp.float32))
    for repeat in range(max(node_count - 1, 1).bit_length()):
        reached = jnp.minimum(jnp.dot(reached, reached, precision=lax.Precision.HIGHEST), 1.0)
    return reached

def reference(queries, tree_keys, parents, node_live, lengths, start_device, cache_latent, cache_rope, up_weight):
    score_scale = 1.0 / math.sqrt(DN + DR)
    head_group = 8
    cycle_pages = jnp.arange(N_BLK, dtype=jnp.int32)
    key_count = N_BLK * SEG
    positions = jnp.arange(key_count, dtype=jnp.int32)
    weight_full = up_weight.astype(jnp.float32)

    def one_request(packed):
        query_all, tree_rows, parent_list, live_row, length_one, start_one, latent_all, rope_all = packed
        page_order = ((start_one + cycle_pages) % N_BLK).astype(jnp.int32)
        lat_keys = jnp.take(latent_all.reshape(N_BLK, SEG, DL), page_order, axis=0).reshape(key_count, DL)
        rope_keys = jnp.take(rope_all.reshape(DR, N_BLK, SEG), page_order, axis=1).reshape(DR, key_count)
        in_range = positions < length_one
        reached = ancestor_matrix(parent_list) > 0.5
        tree_visible = jnp.tile(reached, (head_group, 1))
        values = jnp.concatenate([tree_rows[:, :DL], lat_keys], axis=0)

        def head_block(first_col):
            query_cols = lax.dynamic_slice_in_dim(query_all, first_col, head_group * NODES, 1)
            tree_scores = jnp.dot(query_cols.T, tree_rows.T, preferred_element_type=jnp.float32) * score_scale
            ctx_scores = jnp.dot(query_cols[:DL].T, lat_keys.T, preferred_element_type=jnp.float32)
            ctx_scores = (ctx_scores + jnp.dot(query_cols[DL:].T, rope_keys, preferred_element_type=jnp.float32)) * score_scale
            scores = jnp.concatenate([jnp.where(tree_visible, tree_scores, -jnp.inf), jnp.where(in_range[None, :], ctx_scores, -jnp.inf)], axis=1)
            top_row = lax.optimization_barrier(jnp.max(scores, axis=1, keepdims=True))
            exp_scores = jnp.exp(scores - top_row)
            denominator = lax.optimization_barrier(jnp.sum(exp_scores, axis=1, keepdims=True))
            latent_out = jnp.dot(exp_scores.astype(jnp.bfloat16), values, preferred_element_type=jnp.float32)
            return latent_out / denominator
        starts = jnp.arange(HEADS // head_group, dtype=jnp.int32) * (head_group * NODES)
        latent_heads = lax.map(head_block, starts).reshape(HEADS, NODES, DL)
        projected = jnp.einsum('hnd,hdv->nhv', latent_heads, weight_full, precision=lax.Precision.HIGHEST)
        masked = projected * live_row.astype(jnp.float32)[:, None, None]
        return masked.reshape(NODES, HEADS * DV).astype(jnp.bfloat16)
    return lax.map(one_request, (queries, tree_keys, parents, node_live, lengths, start_device, cache_latent, cache_rope))
```

```python
import functools
import math

import jax
import jax.numpy as jnp
from jax import lax
from jax.experimental import pallas as pl
from jax.experimental.pallas import tpu as pltpu
from jax.sharding import PartitionSpec as P

DN = 128

NEGATIVE = -1e30
STAT_ROWS = 16


def merged(value, axis, join):
    pieces = jax.tree.map(lambda part: lax.all_gather(part, axis), value)
    head = jax.tree.map(lambda part: part[0], pieces)
    tail = jax.tree.map(lambda part: part[1:], pieces)
    subtotal, _ = lax.scan(lambda subtotal, slab: (join(subtotal, slab), None), head, tail)
    return subtotal


def ancestor_matrix(parent_list):
    node_count = parent_list.shape[0]
    ordering = jnp.arange(node_count, dtype=jnp.int32)
    one_hop = (parent_list[:, None] == ordering[None, :]).astype(jnp.float32)
    reached = jnp.maximum(one_hop, jnp.eye(node_count, dtype=jnp.float32))
    for repeat in range(max(node_count - 1, 1).bit_length()):
        reached = jnp.minimum(jnp.dot(reached, reached, precision=lax.Precision.HIGHEST), 1.0)
    return reached


def softmax_update(running, scores, visible, values):
    top_score, weight_sum, summed = running
    masked = jnp.where(visible, scores, -jnp.inf)
    new_top = jnp.maximum(top_score, jnp.max(masked, axis=1))
    factor = jnp.exp(top_score - new_top)
    expweights = jnp.exp(masked - new_top[:, None])
    summed = summed * factor[:, None] + jnp.dot(
        expweights.astype(jnp.bfloat16), values, preferred_element_type=jnp.float32
    )
    return (new_top, weight_sum * factor + jnp.sum(expweights, axis=1), summed)


def join_stats(first_stats, second_stats):
    top_one, sum_one = first_stats
    top_two, sum_two = second_stats
    top_both = jnp.maximum(top_one, top_two)
    return (top_both, sum_one * jnp.exp(top_one - top_both) + sum_two * jnp.exp(top_two - top_both))


def attend_page(running, query_block, lat_page, rope_page, live_count, score_scale):
    dim_lat = lat_page.shape[1]
    query_lat = query_block[:dim_lat]
    query_rope = query_block[dim_lat:]
    key_block = math.gcd(lat_page.shape[0], 512)

    def block_step(block_index, carried):
        first_key = block_index * key_block
        lat_rows = lax.dynamic_slice_in_dim(lat_page, first_key, key_block, 0)
        rope_rows = lax.dynamic_slice_in_dim(rope_page, first_key, key_block, 1)
        scores = lax.dot_general(
            query_lat, lat_rows, (((0,), (1,)), ((), ())), preferred_element_type=jnp.float32
        )
        scores = scores + lax.dot_general(
            query_rope, rope_rows, (((0,), (0,)), ((), ())), preferred_element_type=jnp.float32
        )
        scores = scores * score_scale
        visible = first_key + jnp.arange(key_block, dtype=jnp.int32) < live_count
        return softmax_update(carried, scores, visible[None, :], lat_rows)

    block_count = (live_count + key_block - 1) // key_block
    return lax.fori_loop(0, block_count, block_step, running)


def fresh_state(columns, dim_lat):
    return (
        jnp.full((columns,), NEGATIVE, jnp.float32),
        jnp.zeros((columns,), jnp.float32),
        jnp.zeros((columns, dim_lat), jnp.float32),
    )


def gathered_shards(
    queries,
    tree_keys,
    parents,
    node_live,
    lengths,
    start_device,
    cache_latent,
    cache_rope,
    up_weight,
):
    cycle_size = lax.axis_size("blk")
    position = lax.axis_index("blk")
    request_count = queries.shape[0]
    local_cols = queries.shape[2]
    node_count = tree_keys.shape[1]
    dim_lat = cache_latent.shape[2]
    dim_rope = cache_rope.shape[1]
    dim_value = up_weight.shape[2]
    page_rows = cache_latent.shape[1]
    own_heads = local_cols // node_count
    score_scale = 1.0 / math.sqrt(DN + dim_rope)
    page_index = (position - start_device) % cycle_size
    live_keys = jnp.clip(lengths - page_index * page_rows, 0, page_rows)
    piece = lax.all_gather(queries, "blk", axis=2, tiled=True)
    piece_cols = piece.shape[2]
    tops = []
    sums = []
    accs = []
    for fold_request in range(request_count):
        fold_outcome = attend_page(
            fresh_state(piece_cols, dim_lat),
            piece[fold_request],
            cache_latent[fold_request],
            cache_rope[fold_request],
            live_keys[fold_request],
            score_scale,
        )
        tops.append(fold_outcome[0])
        sums.append(fold_outcome[1])
        accs.append(fold_outcome[2])
    top_all = jnp.stack(tops)
    sum_all = jnp.stack(sums)
    acc_all = jnp.stack(accs)
    reached = jax.vmap(ancestor_matrix)(parents) > 0.5
    tree_tops, tree_sums, tree_accs = ([], [], [])
    for request in range(request_count):
        tree_scores = (
            lax.dot_general(
                queries[request],
                tree_keys[request],
                (((0,), (1,)), ((), ())),
                preferred_element_type=jnp.float32,
            )
            * score_scale
        )
        visible = jnp.tile(reached[request], (own_heads, 1))
        outcome = softmax_update(
            fresh_state(local_cols, dim_lat), tree_scores, visible, tree_keys[request][:, :dim_lat]
        )
        tree_tops.append(outcome[0])
        tree_sums.append(outcome[1])
        tree_accs.append(outcome[2])
    tree_top = jnp.stack(tree_tops)
    tree_sum = jnp.stack(tree_sums)
    tree_acc = jnp.stack(tree_accs)
    own_start = position * local_cols
    own_top = lax.dynamic_slice_in_dim(top_all, own_start, local_cols, 1)
    own_sum = lax.dynamic_slice_in_dim(sum_all, own_start, local_cols, 1)
    own_acc = lax.dynamic_slice_in_dim(acc_all, own_start, local_cols, 1)
    joined = jnp.maximum(own_top, tree_top)
    first_factor = jnp.exp(own_top - joined)
    second_factor = jnp.exp(tree_top - joined)
    top_all = lax.dynamic_update_slice_in_dim(top_all, joined, own_start, 1)
    sum_all = lax.dynamic_update_slice_in_dim(
        sum_all, own_sum * first_factor + tree_sum * second_factor, own_start, 1
    )
    acc_all = lax.dynamic_update_slice_in_dim(
        acc_all,
        own_acc * first_factor[:, :, None] + tree_acc * second_factor[:, :, None],
        own_start,
        1,
    )
    merged_top, merged_sum = merged((top_all, sum_all), "blk", join_stats)
    scaling = jnp.exp(top_all - merged_top) / merged_sum
    normed = acc_all * scaling[:, :, None]
    head_rows = lax.psum_scatter(
        normed.astype(jnp.bfloat16), "blk", scatter_dimension=1, tiled=True
    ).astype(jnp.float32)
    weight_own = lax.dynamic_slice_in_dim(up_weight, position * own_heads, own_heads, 0).astype(
        jnp.float32
    )
    projected = jnp.einsum(
        "rhnd,hdv->rnhv",
        head_rows.reshape(request_count, own_heads, node_count, dim_lat),
        weight_own,
        precision=lax.Precision.HIGHEST,
    )
    verified = projected.reshape(request_count, node_count, own_heads * dim_value)
    live_nodes = node_live.astype(jnp.float32)[:, :, None]
    return (verified * live_nodes).astype(jnp.bfloat16)


def dot_nt(left, right):
    return lax.dot_general(
        left, right, (((1,), (1,)), ((), ())), preferred_element_type=jnp.float32
    )


def dot_nn(left, right):
    return jnp.dot(left, right, preferred_element_type=jnp.float32)


def fold_scores(scores, values, top_ref, sum_ref, acc_ref):
    old_top = top_ref[...]
    new_top = jnp.maximum(old_top, jnp.max(scores, axis=1, keepdims=True))
    factor = jnp.exp(old_top - new_top)
    weights = jnp.exp(scores - new_top)
    sum_ref[...] = sum_ref[...] * factor + jnp.sum(weights, axis=1, keepdims=True)
    acc_ref[...] = acc_ref[...] * factor + dot_nn(weights.astype(jnp.bfloat16), values)
    top_ref[...] = new_top


def page_kernel(
    request_count, slot_count, own, key_block, score_scale, table_ref, *refs
):
    refs = list(refs)
    query_refs = [refs.pop(0) for _ in range(slot_count)]
    lat_ref, rope_ref = refs.pop(0), refs.pop(0)
    weight_refs = [refs.pop(0) for _ in range(slot_count)]
    if own:
        tree_ref, reach_ref = refs.pop(0), refs.pop(0)
        part_ref, stat_ref = refs.pop(0), refs.pop(0)
    else:
        out_refs = [refs.pop(0) for _ in range(slot_count)]
    rows_ref, level_ref, top_ref, sum_ref, acc_ref = refs
    request = pl.program_id(0)
    live = table_ref[request]
    dim_lat = lat_ref.shape[2]
    heads, _, dim_value = weight_refs[0].shape
    columns = query_refs[0].shape[2]
    nodes = columns // heads

    for slot in range(slot_count):
        keys = live * table_ref[request_count + slot]

        @pl.when(keys + int(own) > 0)
        def _():
            query = query_refs[slot][0].T
            query_lat, query_rope = query[:, :dim_lat], query[:, dim_lat:]
            top_ref[...] = jnp.full_like(top_ref, NEGATIVE)
            sum_ref[...] = jnp.zeros_like(sum_ref)
            acc_ref[...] = jnp.zeros_like(acc_ref)
            if own:
                tree = tree_ref[0]
                scores = dot_nt(query, tree) * score_scale
                visible = jnp.tile(reach_ref[0], (heads, 1)) > 0.5
                fold_scores(
                    jnp.where(visible, scores, NEGATIVE), tree[:, :dim_lat], top_ref, sum_ref, acc_ref
                )

            def block_step(index, carry):
                first = pl.multiple_of(index * key_block, key_block)
                lat = lat_ref[0, pl.ds(first, key_block), :]
                scores = dot_nt(query_lat, lat) + dot_nn(
                    query_rope, rope_ref[0, :, pl.ds(first, key_block)]
                )
                place = first + lax.broadcasted_iota(jnp.int32, scores.shape, 1)
                scores = jnp.where(place < keys, scores * score_scale, NEGATIVE)
                fold_scores(scores, lat, top_ref, sum_ref, acc_ref)
                return carry

            lax.fori_loop(0, pl.cdiv(keys, key_block), block_step, 0)
            normed = acc_ref[...] / sum_ref[...]
            rows_ref[slot, :, pl.ds(pl.multiple_of(request * nodes, nodes), nodes), :] = (
                normed.astype(jnp.bfloat16).reshape(heads, nodes, dim_lat)
            )
            level_ref[slot, request] = top_ref[...] + jnp.log(sum_ref[...])

        @pl.when(keys + int(own) <= 0)
        def _():
            rows_ref[slot, :, pl.ds(pl.multiple_of(request * nodes, nodes), nodes), :] = jnp.zeros(
                (heads, nodes, dim_lat), jnp.bfloat16
            )
            level_ref[slot, request] = jnp.full((columns, 1), NEGATIVE, jnp.float32)

    @pl.when(request == request_count - 1)
    def _():
        for slot in range(slot_count):

            @pl.when(table_ref[request_count + slot] > 0)
            def _():
                for head in range(heads):
                    value = dot_nn(rows_ref[slot, head], weight_refs[slot][head])
                    for each in range(request_count):
                        piece = value[each * nodes : (each + 1) * nodes]
                        if own:
                            part_ref[each, head * nodes : (head + 1) * nodes, :] = piece
                        else:
                            out_refs[slot][each, head * nodes : (head + 1) * nodes, :] = piece.astype(
                                jnp.bfloat16
                            )
                for each in range(request_count):
                    if own:
                        stat_ref[each] = level_ref[slot, each]
                    else:
                        out_refs[slot][each, columns:, :] = level_rows(
                            level_ref[slot, each], dim_value
                        )


def diagonal(lanes):
    return lax.broadcasted_iota(jnp.int32, (lanes, lanes), 0) == lax.broadcasted_iota(
        jnp.int32, (lanes, lanes), 1
    )


def level_rows(level, lanes):
    pieces = []
    rest = level
    for _ in range(3):
        piece = rest.astype(jnp.bfloat16).astype(jnp.float32)
        rest = rest - piece
        pieces.append(piece)
    rows = []
    for piece in pieces:
        for first in range(0, level.shape[0], lanes):
            spread = jnp.where(diagonal(lanes), piece[first : first + lanes], 0.0)
            rows.append(jnp.sum(spread, axis=0, keepdims=True))
    filled = jnp.concatenate(
        rows + [jnp.zeros((STAT_ROWS - len(rows), lanes), jnp.float32)], axis=0
    )
    return filled.astype(jnp.bfloat16)


def level_column(block, columns):
    lanes = block.shape[1]
    block = block.astype(jnp.float32)
    per = columns // lanes
    parts = []
    for index in range(per):
        total = block[index : index + 1]
        total = total + block[per + index : per + index + 1]
        total = total + block[2 * per + index : 2 * per + index + 1]
        parts.append(jnp.sum(jnp.where(diagonal(lanes), total, 0.0), axis=1, keepdims=True))
    return jnp.concatenate(parts, axis=0)


def merge_kernel(remote_count, heads, valid_ref, part_ref, stat_ref, live_ref, *refs):
    remote_refs, out_ref = refs[:remote_count], refs[remote_count]
    columns, dim_value = part_ref.shape[1:]
    nodes = columns // heads
    levels = [stat_ref[0]]
    for index, ref in enumerate(remote_refs):
        level = level_column(ref[0, columns:, :], columns)
        levels.append(jnp.where(valid_ref[index] > 0, level, NEGATIVE))
    top = functools.reduce(jnp.maximum, levels)
    weights = [jnp.exp(level - top) for level in levels]
    total = functools.reduce(jnp.add, weights)
    value = part_ref[0] * weights[0]
    for ref, weight in zip(remote_refs, weights[1:]):
        value = value + ref[0, :columns, :].astype(jnp.float32) * weight
    value = value / total
    keep = live_ref[0]
    for head in range(heads):
        rows = value[head * nodes : (head + 1) * nodes] * keep
        out_ref[0, :, head * dim_value : (head + 1) * dim_value] = rows.astype(jnp.bfloat16)


def run_pages(table, query_slots, cache_latent, cache_rope, up_weight, tree=None):
    request_count, width, columns = query_slots[0].shape
    slot_count = len(query_slots)
    page_rows, dim_lat = cache_latent.shape[1:]
    dim_rope = cache_rope.shape[1]
    dim_value = up_weight.shape[2]
    own = tree is not None
    heads = up_weight.shape[0] // lax.axis_size("blk")
    nodes = columns // heads
    key_block = math.gcd(page_rows, 512)
    in_specs = [pl.BlockSpec((1, width, columns), lambda r, t: (r, 0, 0))] * slot_count
    in_specs += [
        pl.BlockSpec((1, page_rows, dim_lat), lambda r, t: (r, 0, 0)),
        pl.BlockSpec((1, dim_rope, page_rows), lambda r, t: (r, 0, 0)),
    ]
    for slot in range(slot_count):
        at = request_count + slot_count + slot
        in_specs.append(
            pl.BlockSpec((heads, dim_lat, dim_value), lambda r, t, at=at: (t[at], 0, 0))
        )
    operands = list(query_slots) + [cache_latent, cache_rope] + [up_weight] * slot_count
    if own:
        tree_keys, reached = tree
        in_specs += [
            pl.BlockSpec((1, nodes, width), lambda r, t: (r, 0, 0)),
            pl.BlockSpec((1, nodes, nodes), lambda r, t: (r, 0, 0)),
        ]
        operands += [tree_keys, reached]
        out_shape = [
            jax.ShapeDtypeStruct((request_count, columns, dim_value), jnp.float32),
            jax.ShapeDtypeStruct((request_count, columns, 1), jnp.float32),
        ]
        out_specs = [
            pl.BlockSpec((request_count, columns, dim_value), lambda r, t: (0, 0, 0)),
            pl.BlockSpec((request_count, columns, 1), lambda r, t: (0, 0, 0)),
        ]
    else:
        rows = columns + STAT_ROWS
        out_shape = [
            jax.ShapeDtypeStruct((request_count, rows, dim_value), jnp.bfloat16)
        ] * slot_count
        out_specs = [
            pl.BlockSpec((request_count, rows, dim_value), lambda r, t: (0, 0, 0))
        ] * slot_count
    return pl.pallas_call(
        functools.partial(
            page_kernel,
            request_count,
            slot_count,
            own,
            key_block,
            1.0 / math.sqrt(DN + dim_rope),
        ),
        grid_spec=pltpu.PrefetchScalarGridSpec(
            num_scalar_prefetch=1,
            grid=(request_count,),
            in_specs=in_specs,
            out_specs=out_specs,
            scratch_shapes=[
                pltpu.VMEM((slot_count, heads, request_count * nodes, dim_lat), jnp.bfloat16),
                pltpu.VMEM((slot_count, request_count, columns, 1), jnp.float32),
                pltpu.VMEM((columns, 1), jnp.float32),
                pltpu.VMEM((columns, 1), jnp.float32),
                pltpu.VMEM((columns, dim_lat), jnp.float32),
            ],
        ),
        out_shape=out_shape,
        compiler_params=pltpu.CompilerParams(dimension_semantics=("arbitrary",)),
        cost_estimate=pl.CostEstimate(
            flops=2 * request_count * columns * page_rows * (width + dim_lat),
            bytes_accessed=request_count * page_rows * (width) * 2,
            transcendentals=request_count * columns * page_rows,
        ),
        name=f"pages_{slot_count}_{int(own)}",
    )(table, *operands)


def chained_shards(
    queries,
    tree_keys,
    parents,
    node_live,
    lengths,
    start_device,
    cache_latent,
    cache_rope,
    up_weight,
):
    size = lax.axis_size("blk")
    position = lax.axis_index("blk")
    request_count, _, columns = queries.shape
    page_rows = cache_latent.shape[1]
    dim_value = up_weight.shape[2]
    heads = up_weight.shape[0] // size
    nodes = columns // heads
    page_index = (position - start_device) % size
    live_keys = jnp.clip(lengths - page_index * page_rows, 0, page_rows).astype(jnp.int32)

    def table(slots):
        shards = jnp.stack([jnp.clip(position + step, 0, size - 1) for step in slots])
        valid = jnp.stack([(position + step >= 0) & (position + step < size) for step in slots])
        return jnp.concatenate([live_keys, valid.astype(jnp.int32), shards.astype(jnp.int32)])

    def moved(value, step, pairs):
        return lax.ppermute(value, "blk", pairs)

    right = left = queries
    arrived = []
    for hop in range(1, size):
        right = lax.ppermute(right, "blk", [(i, i + 1) for i in range(hop - 1, size - 1)])
        left = lax.ppermute(left, "blk", [(i, i - 1) for i in range(1, size - hop + 1)])
        arrived.append((right, left))
    reached = jax.vmap(ancestor_matrix)(parents)
    part, stat = run_pages(
        table([0]), [queries], cache_latent, cache_rope, up_weight, (tree_keys, reached)
    )
    remote = []
    valid = []
    for hop in range(1, size):
        for_left, for_right = run_pages(
            table([-hop, hop]), list(arrived[hop - 1]), cache_latent, cache_rope, up_weight
        )
        remote.append(lax.ppermute(for_left, "blk", [(i, i - hop) for i in range(hop, size)]))
        valid.append(position + hop < size)
        remote.append(lax.ppermute(for_right, "blk", [(i, i + hop) for i in range(size - hop)]))
        valid.append(position - hop >= 0)
    live_nodes = node_live.astype(jnp.float32)[:, :, None]
    block = lambda *shape: pl.BlockSpec((1,) + shape, lambda r, t: (r, 0, 0))
    return pl.pallas_call(
        functools.partial(merge_kernel, len(remote), heads),
        grid_spec=pltpu.PrefetchScalarGridSpec(
            num_scalar_prefetch=1,
            grid=(request_count,),
            in_specs=[block(columns, dim_value), block(columns, 1), block(nodes, 1)]
            + [block(columns + STAT_ROWS, dim_value)] * len(remote),
            out_specs=block(nodes, heads * dim_value),
        ),
        out_shape=jax.ShapeDtypeStruct((request_count, nodes, heads * dim_value), jnp.bfloat16),
        name="merge_parts",
    )(jnp.stack(valid).astype(jnp.int32), part, stat, live_nodes, *remote)


def solution(mesh):
    size = mesh.shape["blk"]

    def shards(queries, *rest):
        columns = queries.shape[2]
        wide = columns % rest[-1].shape[2] == 0
        plan = chained_shards if wide and 1 < size <= 8 else gathered_shards
        return plan(queries, *rest)

    return jax.shard_map(
        shards,
        mesh=mesh,
        in_specs=(
            P("grp", None, ("head", "blk")),
            P("grp", None, None),
            P("grp", None),
            P("grp", None),
            P("grp"),
            P("grp"),
            P("grp", "blk", None),
            P("grp", None, "blk"),
            P("head", None, None),
        ),
        out_specs=P("grp", None, ("head", "blk")),
        check_vma=False,
    )
```

```python
import functools
import math

import jax
import jax.numpy as jnp
from jax import lax
from jax.experimental import pallas as pl
from jax.experimental.pallas import tpu as pltpu
from jax.sharding import PartitionSpec as P

DN = 128

NEGATIVE = -1e30
STAT_ROWS = 16


def merged(value, axis, join):
    pieces = jax.tree.map(lambda part: lax.all_gather(part, axis), value)
    head = jax.tree.map(lambda part: part[0], pieces)
    tail = jax.tree.map(lambda part: part[1:], pieces)
    subtotal, _ = lax.scan(lambda subtotal, slab: (join(subtotal, slab), None), head, tail)
    return subtotal


def ancestor_matrix(parent_list):
    node_count = parent_list.shape[0]
    ordering = jnp.arange(node_count, dtype=jnp.int32)
    one_hop = (parent_list[:, None] == ordering[None, :]).astype(jnp.float32)
    reached = jnp.maximum(one_hop, jnp.eye(node_count, dtype=jnp.float32))
    for repeat in range(max(node_count - 1, 1).bit_length()):
        reached = jnp.minimum(jnp.dot(reached, reached, precision=lax.Precision.HIGHEST), 1.0)
    return reached


def softmax_update(running, scores, visible, values):
    top_score, weight_sum, summed = running
    masked = jnp.where(visible, scores, -jnp.inf)
    new_top = jnp.maximum(top_score, jnp.max(masked, axis=1))
    factor = jnp.exp(top_score - new_top)
    expweights = jnp.exp(masked - new_top[:, None])
    summed = summed * factor[:, None] + jnp.dot(
        expweights.astype(jnp.bfloat16), values, preferred_element_type=jnp.float32
    )
    return (new_top, weight_sum * factor + jnp.sum(expweights, axis=1), summed)


def join_stats(first_stats, second_stats):
    top_one, sum_one = first_stats
    top_two, sum_two = second_stats
    top_both = jnp.maximum(top_one, top_two)
    return (top_both, sum_one * jnp.exp(top_one - top_both) + sum_two * jnp.exp(top_two - top_both))


def attend_page(running, query_block, lat_page, rope_page, live_count, score_scale):
    dim_lat = lat_page.shape[1]
    query_lat = query_block[:dim_lat]
    query_rope = query_block[dim_lat:]
    key_block = math.gcd(lat_page.shape[0], 512)

    def block_step(block_index, carried):
        first_key = block_index * key_block
        lat_rows = lax.dynamic_slice_in_dim(lat_page, first_key, key_block, 0)
        rope_rows = lax.dynamic_slice_in_dim(rope_page, first_key, key_block, 1)
        scores = lax.dot_general(
            query_lat, lat_rows, (((0,), (1,)), ((), ())), preferred_element_type=jnp.float32
        )
        scores = scores + lax.dot_general(
            query_rope, rope_rows, (((0,), (0,)), ((), ())), preferred_element_type=jnp.float32
        )
        scores = scores * score_scale
        visible = first_key + jnp.arange(key_block, dtype=jnp.int32) < live_count
        return softmax_update(carried, scores, visible[None, :], lat_rows)

    block_count = (live_count + key_block - 1) // key_block
    return lax.fori_loop(0, block_count, block_step, running)


def fresh_state(columns, dim_lat):
    return (
        jnp.full((columns,), NEGATIVE, jnp.float32),
        jnp.zeros((columns,), jnp.float32),
        jnp.zeros((columns, dim_lat), jnp.float32),
    )


def gathered_shards(
    queries,
    tree_keys,
    parents,
    node_live,
    lengths,
    start_device,
    cache_latent,
    cache_rope,
    up_weight,
):
    cycle_size = lax.axis_size("blk")
    position = lax.axis_index("blk")
    request_count = queries.shape[0]
    local_cols = queries.shape[2]
    node_count = tree_keys.shape[1]
    dim_lat = cache_latent.shape[2]
    dim_rope = cache_rope.shape[1]
    dim_value = up_weight.shape[2]
    page_rows = cache_latent.shape[1]
    own_heads = local_cols // node_count
    score_scale = 1.0 / math.sqrt(DN + dim_rope)
    page_index = (position - start_device) % cycle_size
    live_keys = jnp.clip(lengths - page_index * page_rows, 0, page_rows)
    piece = lax.all_gather(queries, "blk", axis=2, tiled=True)
    piece_cols = piece.shape[2]
    tops = []
    sums = []
    accs = []
    for fold_request in range(request_count):
        fold_outcome = attend_page(
            fresh_state(piece_cols, dim_lat),
            piece[fold_request],
            cache_latent[fold_request],
            cache_rope[fold_request],
            live_keys[fold_request],
            score_scale,
        )
        tops.append(fold_outcome[0])
        sums.append(fold_outcome[1])
        accs.append(fold_outcome[2])
    top_all = jnp.stack(tops)
    sum_all = jnp.stack(sums)
    acc_all = jnp.stack(accs)
    reached = jax.vmap(ancestor_matrix)(parents) > 0.5
    tree_tops, tree_sums, tree_accs = ([], [], [])
    for request in range(request_count):
        tree_scores = (
            lax.dot_general(
                queries[request],
                tree_keys[request],
                (((0,), (1,)), ((), ())),
                preferred_element_type=jnp.float32,
            )
            * score_scale
        )
        visible = jnp.tile(reached[request], (own_heads, 1))
        outcome = softmax_update(
            fresh_state(local_cols, dim_lat), tree_scores, visible, tree_keys[request][:, :dim_lat]
        )
        tree_tops.append(outcome[0])
        tree_sums.append(outcome[1])
        tree_accs.append(outcome[2])
    tree_top = jnp.stack(tree_tops)
    tree_sum = jnp.stack(tree_sums)
    tree_acc = jnp.stack(tree_accs)
    own_start = position * local_cols
    own_top = lax.dynamic_slice_in_dim(top_all, own_start, local_cols, 1)
    own_sum = lax.dynamic_slice_in_dim(sum_all, own_start, local_cols, 1)
    own_acc = lax.dynamic_slice_in_dim(acc_all, own_start, local_cols, 1)
    joined = jnp.maximum(own_top, tree_top)
    first_factor = jnp.exp(own_top - joined)
    second_factor = jnp.exp(tree_top - joined)
    top_all = lax.dynamic_update_slice_in_dim(top_all, joined, own_start, 1)
    sum_all = lax.dynamic_update_slice_in_dim(
        sum_all, own_sum * first_factor + tree_sum * second_factor, own_start, 1
    )
    acc_all = lax.dynamic_update_slice_in_dim(
        acc_all,
        own_acc * first_factor[:, :, None] + tree_acc * second_factor[:, :, None],
        own_start,
        1,
    )
    merged_top, merged_sum = merged((top_all, sum_all), "blk", join_stats)
    scaling = jnp.exp(top_all - merged_top) / merged_sum
    normed = acc_all * scaling[:, :, None]
    head_rows = lax.psum_scatter(
        normed.astype(jnp.bfloat16), "blk", scatter_dimension=1, tiled=True
    ).astype(jnp.float32)
    weight_own = lax.dynamic_slice_in_dim(up_weight, position * own_heads, own_heads, 0).astype(
        jnp.float32
    )
    projected = jnp.einsum(
        "rhnd,hdv->rnhv",
        head_rows.reshape(request_count, own_heads, node_count, dim_lat),
        weight_own,
        precision=lax.Precision.HIGHEST,
    )
    verified = projected.reshape(request_count, node_count, own_heads * dim_value)
    live_nodes = node_live.astype(jnp.float32)[:, :, None]
    return (verified * live_nodes).astype(jnp.bfloat16)


def dot_nn(left, right):
    return jnp.dot(left, right, preferred_element_type=jnp.float32)


def dot_tn(left, right):
    return lax.dot_general(
        left, right, (((0,), (0,)), ((), ())), preferred_element_type=jnp.float32
    )


def reach_closure(parent_row):
    count = parent_row.shape[1]
    row = lax.broadcasted_iota(jnp.int32, (count, count), 0)
    lane = lax.broadcasted_iota(jnp.int32, (count, count), 1)
    reached = jnp.where((row == parent_row) | (row == lane), 1.0, 0.0).astype(jnp.bfloat16)
    return reached


def page_softmax(query, lat_ref, rope_ref, request, keys, blocks, block, scale, score_ref, tree):
    dim_lat = lat_ref.shape[2]
    query_lat, query_rope = query[:dim_lat], query[dim_lat:]
    tops = []
    for index in range(blocks):
        span = slice(index * block, (index + 1) * block)
        scores = dot_nn(lat_ref[request, span, :], query_lat)
        scores = (scores + dot_tn(rope_ref[request, :, span], query_rope)) * scale
        place = index * block + lax.broadcasted_iota(jnp.int32, scores.shape, 0)
        scores = jnp.where(place < keys, scores, NEGATIVE)
        score_ref[span, :] = scores
        tops.append(jnp.max(scores, axis=0, keepdims=True))
    if tree is not None:
        tree_keys, visible = tree
        tree_scores = jnp.where(visible > 0.5, dot_nn(tree_keys, query) * scale, NEGATIVE)
        tops.append(jnp.max(tree_scores, axis=0, keepdims=True))
    top = functools.reduce(jnp.maximum, tops)
    total = summed = None
    for index in range(blocks):
        span = slice(index * block, (index + 1) * block)
        weights = jnp.exp(score_ref[span, :] - top)
        weight_sum = jnp.sum(weights, axis=0, keepdims=True)
        values = dot_tn(lat_ref[request, span, :], weights.astype(jnp.bfloat16))
        total = weight_sum if total is None else total + weight_sum
        summed = values if summed is None else summed + values
    if tree is not None:
        weights = jnp.exp(tree_scores - top)
        weight_sum = jnp.sum(weights, axis=0, keepdims=True)
        values = dot_tn(tree_keys[:, :dim_lat], weights.astype(jnp.bfloat16))
        total = weight_sum if total is None else total + weight_sum
        summed = values if summed is None else summed + values
    return summed, total, top


def page_kernel(request_count, heads, slot_count, own, joint, block, scale, table_ref, *refs):
    refs = list(refs)
    query_refs = [refs.pop(0) for _ in range(slot_count)]
    lat_ref, rope_ref, weight_ref = refs.pop(0), refs.pop(0), refs.pop(0)
    if own:
        tree_ref, parent_ref, part_ref, stat_ref = [refs.pop(0) for _ in range(4)]
    else:
        out_refs = [refs.pop(0) for _ in range(1 if joint else slot_count)]
    rows_ref, level_ref, score_ref, reach_ref = refs
    page_rows, dim_lat = lat_ref.shape[1:]
    dim_value = weight_ref.shape[2]
    columns = query_refs[0].shape[2]
    nodes = columns // heads
    block_count = page_rows // block
    step = 2 if block_count % 2 == 0 else 1

    if own:
        reached = reach_closure(parent_ref[...])
        for _ in range(max(nodes - 1, 1).bit_length()):
            reached = jnp.minimum(dot_nn(reached, reached), 1.0).astype(jnp.bfloat16)
        reach_ref[...] = reached.astype(jnp.float32)

    for slot in range(slot_count):
        out_ref = None if own else out_refs[0 if joint else slot]
        active = table_ref[request_count + slot]
        shard = table_ref[request_count + slot_count + slot]

        @pl.when(active > 0)
        def _():
            def request_step(request, carry):
                keys = table_ref[request]
                base = pl.multiple_of(request * nodes, nodes)

                def finish(summed, total, top):
                    normed = (summed * (1.0 / total)).astype(jnp.bfloat16)
                    rows_ref[:, pl.ds(base, nodes), :] = normed.T.reshape(heads, nodes, dim_lat)
                    level_ref[pl.ds(request, 1), :] = top + jnp.log(total)

                def attend(blocks):
                    tree = None
                    if own:
                        row = lax.broadcasted_iota(jnp.int32, (reach_ref.shape[1], columns), 0)
                        lane = lax.broadcasted_iota(jnp.int32, (reach_ref.shape[1], columns), 1)
                        pick = jnp.where(row == base + lane % nodes, 1.0, 0.0).astype(jnp.bfloat16)
                        near = reach_ref[pl.ds(base, nodes), :].astype(jnp.bfloat16)
                        tree = (tree_ref[request], dot_nn(near, pick))
                    finish(
                        *page_softmax(
                            query_refs[slot][request], lat_ref, rope_ref, request, keys, blocks, block,
                            scale, score_ref, tree,
                        )
                    )

                for blocks in range(step, block_count + 1, step):

                    @pl.when((keys > (blocks - step) * block) & (keys <= blocks * block))
                    def _():
                        attend(blocks)

                @pl.when(keys <= 0)
                def _():
                    if own:
                        attend(0)
                    else:
                        rows_ref[:, pl.ds(base, nodes), :] = jnp.zeros(
                            (heads, nodes, dim_lat), jnp.bfloat16
                        )
                        level_ref[pl.ds(request, 1), :] = jnp.full((1, columns), NEGATIVE, jnp.float32)

                return carry

            lax.fori_loop(0, request_count, request_step, 0)
            for head in range(heads):
                value = dot_nn(rows_ref[head], weight_ref[shard * heads + head])
                for each in range(request_count):
                    piece = value[each * nodes : (each + 1) * nodes]
                    if own:
                        part_ref[each, head * nodes : (head + 1) * nodes, :] = piece
                    else:
                        out_ref[each, head * nodes : (head + 1) * nodes, :] = piece.astype(jnp.bfloat16)
            if own:
                stat_ref[...] = level_ref[...]
            else:
                for each in range(request_count):
                    out_ref[each, columns:, :] = level_rows(level_ref[each : each + 1, :], dim_value)


def level_rows(level, lanes):
    pieces = []
    rest = level
    for _ in range(3):
        piece = rest.astype(jnp.bfloat16).astype(jnp.float32)
        rest = rest - piece
        pieces.append(piece)
    rows = [
        piece[:, first : first + lanes] for piece in pieces for first in range(0, level.shape[1], lanes)
    ]
    rows.append(jnp.zeros((STAT_ROWS - len(rows), lanes), jnp.float32))
    return jnp.concatenate(rows, axis=0).astype(jnp.bfloat16)


def level_row(block, columns):
    per = columns // block.shape[1]
    block = block.astype(jnp.float32)
    return jnp.concatenate(
        [block[i : i + 1] + block[per + i : per + i + 1] + block[2 * per + i : 2 * per + i + 1] for i in range(per)],
        axis=1,
    )


def merge_kernel(remote_count, heads, valid_ref, part_ref, stat_ref, live_ref, *refs):
    remote_refs, out_ref = refs[:remote_count], refs[remote_count]
    request_count, columns, dim_value = part_ref.shape
    nodes = columns // heads
    levels = [stat_ref[...]]
    for index, ref in enumerate(remote_refs):
        level = jnp.concatenate(
            [level_row(ref[each, columns:, :], columns) for each in range(request_count)], axis=0
        )
        levels.append(jnp.where(valid_ref[index] > 0, level, NEGATIVE))
    top = functools.reduce(jnp.maximum, levels)
    weights = [jnp.exp(level - top) for level in levels]
    total = 1.0 / functools.reduce(jnp.add, weights)
    stacked = [weight * total for weight in weights]
    filler = -len(stacked) * request_count % 8
    if filler:
        stacked.append(jnp.zeros((filler, columns), jnp.float32))
    shares = jnp.concatenate(stacked, axis=0).T
    for each in range(request_count):
        value = part_ref[each] * shares[:, each : each + 1]
        for index, ref in enumerate(remote_refs):
            at = (index + 1) * request_count + each
            value = value + ref[each, :columns, :].astype(jnp.float32) * shares[:, at : at + 1]
        keep = live_ref[each]
        for head in range(heads):
            rows = value[head * nodes : (head + 1) * nodes] * keep
            out_ref[each, :, head * dim_value : (head + 1) * dim_value] = rows.astype(jnp.bfloat16)


VMEM = pl.BlockSpec(memory_space=pltpu.VMEM)
SMEM = pl.BlockSpec(memory_space=pltpu.SMEM)


def run_pages(table, query_slots, cache_latent, cache_rope, up_weight, joint=False, tree=None):
    request_count, width, columns = query_slots[0].shape
    slot_count = len(query_slots)
    page_rows, dim_lat = cache_latent.shape[1:]
    dim_rope = cache_rope.shape[1]
    dim_value = up_weight.shape[2]
    own = tree is not None
    heads = up_weight.shape[0] // lax.axis_size("blk")
    nodes = columns // heads
    block = math.gcd(page_rows, 256)
    operands = list(query_slots) + [cache_latent, cache_rope, up_weight]
    if own:
        operands += list(tree)
        out_shape = [
            jax.ShapeDtypeStruct((request_count, columns, dim_value), jnp.float32),
            jax.ShapeDtypeStruct((request_count, columns), jnp.float32),
        ]
    else:
        rows = columns + STAT_ROWS
        out_shape = [jax.ShapeDtypeStruct((request_count, rows, dim_value), jnp.bfloat16)] * (
            1 if joint else slot_count
        )
    return pl.pallas_call(
        functools.partial(
            page_kernel,
            request_count,
            heads,
            slot_count,
            own,
            joint,
            block,
            1.0 / math.sqrt(DN + dim_rope),
        ),
        in_specs=[SMEM] + [VMEM] * len(operands),
        out_specs=[VMEM] * len(out_shape),
        scratch_shapes=[
            pltpu.VMEM((heads, request_count * nodes, dim_lat), jnp.bfloat16),
            pltpu.VMEM((request_count, columns), jnp.float32),
            pltpu.VMEM((page_rows, columns), jnp.float32),
            pltpu.VMEM((request_count * nodes, request_count * nodes), jnp.float32),
        ],
        out_shape=out_shape,
        compiler_params=pltpu.CompilerParams(vmem_limit_bytes=VMEM_LIMIT),
        cost_estimate=pl.CostEstimate(
            flops=2 * request_count * columns * page_rows * (width + dim_lat),
            bytes_accessed=request_count * page_rows * width * 2,
            transcendentals=request_count * columns * page_rows,
        ),
        name=f"pages_{slot_count}_{int(own)}",
    )(table, *operands)


VMEM_LIMIT = 10 << 20


def after(value, *others):
    return lax.optimization_barrier((value, *others))[0]


def chained_shards(
    queries,
    tree_keys,
    parents,
    node_live,
    lengths,
    start_device,
    cache_latent,
    cache_rope,
    up_weight,
):
    size = lax.axis_size("blk")
    position = lax.axis_index("blk")
    request_count, _, columns = queries.shape
    page_rows = cache_latent.shape[1]
    dim_value = up_weight.shape[2]
    heads = up_weight.shape[0] // size
    nodes = columns // heads
    page_index = (position - start_device) % size
    live_keys = jnp.clip(lengths - page_index * page_rows, 0, page_rows).astype(jnp.int32)

    def table(steps):
        place = position + jnp.array(steps, jnp.int32)
        valid = ((place >= 0) & (place < size)).astype(jnp.int32)
        return jnp.concatenate([live_keys, valid, jnp.clip(place, 0, size - 1).astype(jnp.int32)])

    parent_row = (parents + nodes * jnp.arange(request_count, dtype=jnp.int32)[:, None]).reshape(1, -1)
    done = [queries]
    right = left = queries
    outcome = []
    for hop in range(1, size):
        if outcome:
            right, left = after(right, *outcome[-1]), after(left, *outcome[-1])
        right = lax.ppermute(right, "blk", [(i, i + 1) for i in range(hop - 1, size - 1)])
        left = lax.ppermute(left, "blk", [(i, i - 1) for i in range(1, size - hop + 1)])
        if hop == 1:
            outcome.append(
                run_pages(
                    table([0]), [queries], cache_latent, cache_rope, up_weight,
                    tree=(tree_keys, parent_row),
                )
            )
        else:
            outcome.append(
                run_pages(
                    table([1 - hop, hop - 1]), slots, cache_latent, cache_rope, up_weight,
                    joint=2 * (hop - 1) >= size,
                )
            )
        slots = [right, left]
    outcome.append(
        run_pages(
            table([1 - size, size - 1]), slots, cache_latent, cache_rope, up_weight, joint=True
        )
    )
    part, stat = outcome[0]
    remote = []
    valid = []
    for hop in range(1, size):
        to_left = [(i, i - hop) for i in range(hop, size)]
        to_right = [(i, i + hop) for i in range(size - hop)]
        if len(outcome[hop]) == 1:
            remote.append(lax.ppermute(outcome[hop][0], "blk", to_left + to_right))
            valid.append((position + hop < size) | (position >= hop))
        else:
            remote.append(lax.ppermute(outcome[hop][0], "blk", to_left))
            valid.append(position + hop < size)
            remote.append(lax.ppermute(outcome[hop][1], "blk", to_right))
            valid.append(position >= hop)
    live_nodes = node_live.astype(jnp.float32)[:, :, None]
    return pl.pallas_call(
        functools.partial(merge_kernel, len(remote), heads),
        in_specs=[SMEM] + [VMEM] * (3 + len(remote)),
        out_specs=VMEM,
        out_shape=jax.ShapeDtypeStruct((request_count, nodes, heads * dim_value), jnp.bfloat16),
        compiler_params=pltpu.CompilerParams(vmem_limit_bytes=VMEM_LIMIT),
        name="merge_parts",
    )(jnp.stack(valid).astype(jnp.int32), part, stat, live_nodes, *remote)


def solution(mesh):
    size = mesh.shape["blk"]

    def shards(queries, *rest):
        columns = queries.shape[2]
        wide = columns % rest[-1].shape[2] == 0
        plan = chained_shards if wide and 1 < size <= 8 else gathered_shards
        return plan(queries, *rest)

    return jax.shard_map(
        shards,
        mesh=mesh,
        in_specs=(
            P("grp", None, ("head", "blk")),
            P("grp", None, None),
            P("grp", None),
            P("grp", None),
            P("grp"),
            P("grp"),
            P("grp", "blk", None),
            P("grp", None, "blk"),
            P("head", None, None),
        ),
        out_specs=P("grp", None, ("head", "blk")),
        check_vma=False,
    )
```

```python
import functools
import math

import jax
import jax.numpy as jnp
from jax import lax
from jax.experimental import pallas as pl
from jax.experimental.pallas import tpu as pltpu
from jax.sharding import PartitionSpec as P

DN = 128

NEGATIVE = -1e30
STAT_ROWS = 16


def merged(value, axis, join):
    pieces = jax.tree.map(lambda part: lax.all_gather(part, axis), value)
    head = jax.tree.map(lambda part: part[0], pieces)
    tail = jax.tree.map(lambda part: part[1:], pieces)
    subtotal, _ = lax.scan(lambda subtotal, slab: (join(subtotal, slab), None), head, tail)
    return subtotal


def ancestor_matrix(parent_list):
    node_count = parent_list.shape[0]
    ordering = jnp.arange(node_count, dtype=jnp.int32)
    one_hop = (parent_list[:, None] == ordering[None, :]).astype(jnp.float32)
    reached = jnp.maximum(one_hop, jnp.eye(node_count, dtype=jnp.float32))
    for repeat in range(max(node_count - 1, 1).bit_length()):
        reached = jnp.minimum(jnp.dot(reached, reached, precision=lax.Precision.HIGHEST), 1.0)
    return reached


def softmax_update(running, scores, visible, values):
    top_score, weight_sum, summed = running
    masked = jnp.where(visible, scores, -jnp.inf)
    new_top = jnp.maximum(top_score, jnp.max(masked, axis=1))
    factor = jnp.exp(top_score - new_top)
    expweights = jnp.exp(masked - new_top[:, None])
    summed = summed * factor[:, None] + jnp.dot(
        expweights.astype(jnp.bfloat16), values, preferred_element_type=jnp.float32
    )
    return (new_top, weight_sum * factor + jnp.sum(expweights, axis=1), summed)


def join_stats(first_stats, second_stats):
    top_one, sum_one = first_stats
    top_two, sum_two = second_stats
    top_both = jnp.maximum(top_one, top_two)
    return (top_both, sum_one * jnp.exp(top_one - top_both) + sum_two * jnp.exp(top_two - top_both))


def attend_page(running, query_block, lat_page, rope_page, live_count, score_scale):
    dim_lat = lat_page.shape[1]
    query_lat = query_block[:dim_lat]
    query_rope = query_block[dim_lat:]
    key_block = math.gcd(lat_page.shape[0], 512)

    def block_step(block_index, carried):
        first_key = block_index * key_block
        lat_rows = lax.dynamic_slice_in_dim(lat_page, first_key, key_block, 0)
        rope_rows = lax.dynamic_slice_in_dim(rope_page, first_key, key_block, 1)
        scores = lax.dot_general(
            query_lat, lat_rows, (((0,), (1,)), ((), ())), preferred_element_type=jnp.float32
        )
        scores = scores + lax.dot_general(
            query_rope, rope_rows, (((0,), (0,)), ((), ())), preferred_element_type=jnp.float32
        )
        scores = scores * score_scale
        visible = first_key + jnp.arange(key_block, dtype=jnp.int32) < live_count
        return softmax_update(carried, scores, visible[None, :], lat_rows)

    block_count = (live_count + key_block - 1) // key_block
    return lax.fori_loop(0, block_count, block_step, running)


def fresh_state(columns, dim_lat):
    return (
        jnp.full((columns,), NEGATIVE, jnp.float32),
        jnp.zeros((columns,), jnp.float32),
        jnp.zeros((columns, dim_lat), jnp.float32),
    )


def gathered_shards(
    queries,
    tree_keys,
    parents,
    node_live,
    lengths,
    start_device,
    cache_latent,
    cache_rope,
    up_weight,
):
    cycle_size = lax.axis_size("blk")
    position = lax.axis_index("blk")
    request_count = queries.shape[0]
    local_cols = queries.shape[2]
    node_count = tree_keys.shape[1]
    dim_lat = cache_latent.shape[2]
    dim_rope = cache_rope.shape[1]
    dim_value = up_weight.shape[2]
    page_rows = cache_latent.shape[1]
    own_heads = local_cols // node_count
    score_scale = 1.0 / math.sqrt(DN + dim_rope)
    page_index = (position - start_device) % cycle_size
    live_keys = jnp.clip(lengths - page_index * page_rows, 0, page_rows)
    piece = lax.all_gather(queries, "blk", axis=2, tiled=True)
    piece_cols = piece.shape[2]
    tops = []
    sums = []
    accs = []
    for fold_request in range(request_count):
        fold_outcome = attend_page(
            fresh_state(piece_cols, dim_lat),
            piece[fold_request],
            cache_latent[fold_request],
            cache_rope[fold_request],
            live_keys[fold_request],
            score_scale,
        )
        tops.append(fold_outcome[0])
        sums.append(fold_outcome[1])
        accs.append(fold_outcome[2])
    top_all = jnp.stack(tops)
    sum_all = jnp.stack(sums)
    acc_all = jnp.stack(accs)
    reached = jax.vmap(ancestor_matrix)(parents) > 0.5
    tree_tops, tree_sums, tree_accs = ([], [], [])
    for request in range(request_count):
        tree_scores = (
            lax.dot_general(
                queries[request],
                tree_keys[request],
                (((0,), (1,)), ((), ())),
                preferred_element_type=jnp.float32,
            )
            * score_scale
        )
        visible = jnp.tile(reached[request], (own_heads, 1))
        outcome = softmax_update(
            fresh_state(local_cols, dim_lat), tree_scores, visible, tree_keys[request][:, :dim_lat]
        )
        tree_tops.append(outcome[0])
        tree_sums.append(outcome[1])
        tree_accs.append(outcome[2])
    tree_top = jnp.stack(tree_tops)
    tree_sum = jnp.stack(tree_sums)
    tree_acc = jnp.stack(tree_accs)
    own_start = position * local_cols
    own_top = lax.dynamic_slice_in_dim(top_all, own_start, local_cols, 1)
    own_sum = lax.dynamic_slice_in_dim(sum_all, own_start, local_cols, 1)
    own_acc = lax.dynamic_slice_in_dim(acc_all, own_start, local_cols, 1)
    joined = jnp.maximum(own_top, tree_top)
    first_factor = jnp.exp(own_top - joined)
    second_factor = jnp.exp(tree_top - joined)
    top_all = lax.dynamic_update_slice_in_dim(top_all, joined, own_start, 1)
    sum_all = lax.dynamic_update_slice_in_dim(
        sum_all, own_sum * first_factor + tree_sum * second_factor, own_start, 1
    )
    acc_all = lax.dynamic_update_slice_in_dim(
        acc_all,
        own_acc * first_factor[:, :, None] + tree_acc * second_factor[:, :, None],
        own_start,
        1,
    )
    merged_top, merged_sum = merged((top_all, sum_all), "blk", join_stats)
    scaling = jnp.exp(top_all - merged_top) / merged_sum
    normed = acc_all * scaling[:, :, None]
    head_rows = lax.psum_scatter(
        normed.astype(jnp.bfloat16), "blk", scatter_dimension=1, tiled=True
    ).astype(jnp.float32)
    weight_own = lax.dynamic_slice_in_dim(up_weight, position * own_heads, own_heads, 0).astype(
        jnp.float32
    )
    projected = jnp.einsum(
        "rhnd,hdv->rnhv",
        head_rows.reshape(request_count, own_heads, node_count, dim_lat),
        weight_own,
        precision=lax.Precision.HIGHEST,
    )
    verified = projected.reshape(request_count, node_count, own_heads * dim_value)
    live_nodes = node_live.astype(jnp.float32)[:, :, None]
    return (verified * live_nodes).astype(jnp.bfloat16)


def dot_nn(left, right):
    return jnp.dot(left, right, preferred_element_type=jnp.float32)


def dot_tn(left, right):
    return lax.dot_general(
        left, right, (((0,), (0,)), ((), ())), preferred_element_type=jnp.float32
    )


def reach_closure(parent_row):
    count = parent_row.shape[1]
    row = lax.broadcasted_iota(jnp.int32, (count, count), 0)
    lane = lax.broadcasted_iota(jnp.int32, (count, count), 1)
    reached = jnp.where((row == parent_row) | (row == lane), 1.0, 0.0).astype(jnp.bfloat16)
    return reached


def page_softmax(query, lat_ref, rope_ref, request, keys, blocks, block, scale, score_ref, tree):
    dim_lat = lat_ref.shape[2]
    query_lat, query_rope = query[:dim_lat], query[dim_lat:]
    tops = []
    for index in range(blocks):
        span = slice(index * block, (index + 1) * block)
        scores = dot_nn(lat_ref[request, span, :], query_lat)
        scores = (scores + dot_tn(rope_ref[request, :, span], query_rope)) * scale
        place = index * block + lax.broadcasted_iota(jnp.int32, scores.shape, 0)
        scores = jnp.where(place < keys, scores, NEGATIVE)
        score_ref[span, :] = scores
        tops.append(jnp.max(scores, axis=0, keepdims=True))
    if tree is not None:
        tree_keys, visible = tree
        tree_scores = jnp.where(visible > 0.5, dot_nn(tree_keys, query) * scale, NEGATIVE)
        tops.append(jnp.max(tree_scores, axis=0, keepdims=True))
    top = functools.reduce(jnp.maximum, tops)
    total = summed = None
    for index in range(blocks):
        span = slice(index * block, (index + 1) * block)
        weights = jnp.exp(score_ref[span, :] - top)
        weight_sum = jnp.sum(weights, axis=0, keepdims=True)
        values = dot_tn(lat_ref[request, span, :], weights.astype(jnp.bfloat16))
        total = weight_sum if total is None else total + weight_sum
        summed = values if summed is None else summed + values
    if tree is not None:
        weights = jnp.exp(tree_scores - top)
        weight_sum = jnp.sum(weights, axis=0, keepdims=True)
        values = dot_tn(tree_keys[:, :dim_lat], weights.astype(jnp.bfloat16))
        total = weight_sum if total is None else total + weight_sum
        summed = values if summed is None else summed + values
    return summed, total, top


def page_kernel(
    first, request_count, chunk_sizes, heads, slot_count, own, joint, block, scale, table_ref, *refs
):
    refs = list(refs)
    query_refs = [[refs.pop(0) for _ in chunk_sizes] for _ in range(slot_count)]
    lat_ref, rope_ref, weight_ref = refs.pop(0), refs.pop(0), refs.pop(0)
    if own:
        tree_ref, parent_ref, part_ref, stat_ref = [refs.pop(0) for _ in range(4)]
    else:
        out_refs = [refs.pop(0) for _ in range(1 if joint else slot_count)]
    query_ref, rows_ref, level_ref, score_ref, reach_ref = refs
    total_requests = lat_ref.shape[0]
    page_rows, dim_lat = lat_ref.shape[1:]
    dim_value = weight_ref.shape[2]
    columns = query_ref.shape[1]
    nodes = columns // heads
    block_count = page_rows // block
    step = 2 if block_count % 2 == 0 else 1
    active = [table_ref[total_requests + slot] for slot in range(slot_count)]
    shards = [table_ref[total_requests + slot_count + slot] for slot in range(slot_count)]

    if own:
        reached = reach_closure(parent_ref[...])
        for _ in range(max(nodes - 1, 1).bit_length()):
            reached = jnp.minimum(dot_nn(reached, reached), 1.0).astype(jnp.bfloat16)
        reach_ref[...] = reached.astype(jnp.float32)

    def item_step(item, carry):
        place = lax.rem(item, request_count)
        lane_slot = lax.div(item, request_count)
        request = first + place
        usable = 0
        for slot in range(slot_count):
            here = active[slot] if joint else active[slot] * (lane_slot == slot).astype(jnp.int32)
            usable = usable + here
            offset = 0
            for ref, size in zip(query_refs[slot], chunk_sizes):

                @pl.when((here > 0) & (place >= offset) & (place < offset + size))
                def _():
                    query_ref[...] = ref[place - offset]

                offset += size
        keys = table_ref[request] * usable
        base = pl.multiple_of(place * nodes, nodes)

        def attend(blocks):
            tree = None
            if own:
                row = lax.broadcasted_iota(jnp.int32, (reach_ref.shape[1], columns), 0)
                lane = lax.broadcasted_iota(jnp.int32, (reach_ref.shape[1], columns), 1)
                pick = jnp.where(row == base + lane % nodes, 1.0, 0.0).astype(jnp.bfloat16)
                near = reach_ref[pl.ds(base, nodes), :].astype(jnp.bfloat16)
                tree = (tree_ref[request], dot_nn(near, pick))
            summed, total, top = page_softmax(
                query_ref[...], lat_ref, rope_ref, request, keys, blocks, block, scale, score_ref, tree
            )
            normed = (summed * (1.0 / total)).astype(jnp.bfloat16)
            rows_ref[lane_slot, :, pl.ds(base, nodes), :] = normed.T.reshape(heads, nodes, dim_lat)
            level_ref[lane_slot, pl.ds(place, 1), :] = top + jnp.log(total)

        for blocks in range(step, block_count + 1, step):

            @pl.when((keys > (blocks - step) * block) & (keys <= blocks * block))
            def _():
                attend(blocks)

        @pl.when(keys <= 0)
        def _():
            if own:
                attend(0)
            else:
                rows_ref[lane_slot, :, pl.ds(base, nodes), :] = jnp.zeros(
                    (heads, nodes, dim_lat), jnp.bfloat16
                )
                level_ref[lane_slot, pl.ds(place, 1), :] = jnp.full((1, columns), NEGATIVE, jnp.float32)

        return carry

    lanes = 1 if joint else slot_count
    if joint:
        flags = functools.reduce(jnp.add, active)
        shard = functools.reduce(jnp.add, [a * s for a, s in zip(active, shards)])
        lax.fori_loop(0, request_count * jnp.minimum(flags, 1), item_step, 0)
        flags, shards = [flags], [shard]
    else:
        flags = active
        lax.fori_loop(0, request_count * slot_count, item_step, 0)
    for lane_slot in range(lanes):

        @pl.when(flags[lane_slot] > 0)
        def _():
            for head in range(heads):
                value = dot_nn(rows_ref[lane_slot, head], weight_ref[shards[lane_slot] * heads + head])
                for each in range(request_count):
                    piece = value[each * nodes : (each + 1) * nodes]
                    if own:
                        part_ref[each, head * nodes : (head + 1) * nodes, :] = piece
                    else:
                        out_refs[lane_slot][each, head * nodes : (head + 1) * nodes, :] = piece.astype(
                            jnp.bfloat16
                        )
            if own:
                stat_ref[...] = level_ref[lane_slot]
            else:
                for each in range(request_count):
                    out_refs[lane_slot][each, columns:, :] = level_rows(
                        level_ref[lane_slot, each : each + 1, :], dim_value
                    )


def level_rows(level, lanes):
    pieces = []
    rest = level
    for _ in range(3):
        piece = rest.astype(jnp.bfloat16).astype(jnp.float32)
        rest = rest - piece
        pieces.append(piece)
    rows = [
        piece[:, first : first + lanes] for piece in pieces for first in range(0, level.shape[1], lanes)
    ]
    rows.append(jnp.zeros((STAT_ROWS - len(rows), lanes), jnp.float32))
    return jnp.concatenate(rows, axis=0).astype(jnp.bfloat16)


def level_row(block, columns):
    per = columns // block.shape[1]
    block = block.astype(jnp.float32)
    return jnp.concatenate(
        [block[i : i + 1] + block[per + i : per + i + 1] + block[2 * per + i : 2 * per + i + 1] for i in range(per)],
        axis=1,
    )


def merge_kernel(layout, heads, valid_ref, part_ref, stat_ref, live_ref, *refs):
    request_count, columns, dim_value = part_ref.shape
    nodes = columns // heads
    refs = list(refs)
    sources = []
    for sizes in layout:
        places = []
        for size in sizes:
            ref = refs.pop(0)
            places += [(ref, each) for each in range(size)]
        sources.append(places)
    out_ref = refs.pop(0)
    levels = [stat_ref[...]]
    for index, places in enumerate(sources):
        level = jnp.concatenate(
            [level_row(ref[each, columns:, :], columns) for ref, each in places], axis=0
        )
        levels.append(jnp.where(valid_ref[index] > 0, level, NEGATIVE))
    top = functools.reduce(jnp.maximum, levels)
    weights = [jnp.exp(level - top) for level in levels]
    total = live_ref[...] / functools.reduce(jnp.add, weights)
    stacked = [weight * total for weight in weights]
    filler = -len(stacked) * request_count % 8
    if filler:
        stacked.append(jnp.zeros((filler, columns), jnp.float32))
    shares = jnp.concatenate(stacked, axis=0).T
    for request in range(request_count):
        value = part_ref[request] * shares[:, request : request + 1]
        for index, places in enumerate(sources):
            at = (index + 1) * request_count + request
            ref, each = places[request]
            value = value + ref[each, :columns, :].astype(jnp.float32) * shares[:, at : at + 1]
        for head in range(heads):
            rows = value[head * nodes : (head + 1) * nodes]
            out_ref[request, :, head * dim_value : (head + 1) * dim_value] = rows.astype(jnp.bfloat16)


VMEM = pl.BlockSpec(memory_space=pltpu.VMEM)
SMEM = pl.BlockSpec(memory_space=pltpu.SMEM)
VMEM_LIMIT = 10 << 20


def run_pages(table, query_slots, first, pages, joint=False, tree=None):
    cache_latent, cache_rope, up_weight = pages
    _, width, columns = query_slots[0][0].shape
    chunk_sizes = [chunk.shape[0] for chunk in query_slots[0]]
    request_count = sum(chunk_sizes)
    slot_count = len(query_slots)
    page_rows, dim_lat = cache_latent.shape[1:]
    dim_rope = cache_rope.shape[1]
    dim_value = up_weight.shape[2]
    own = tree is not None
    heads = up_weight.shape[0] // lax.axis_size("blk")
    nodes = columns // heads
    block = math.gcd(page_rows, 256)
    lanes = 1 if joint else slot_count
    operands = [chunk for slot in query_slots for chunk in slot] + [cache_latent, cache_rope, up_weight]
    reach_size = 8
    if own:
        operands += list(tree)
        reach_size = request_count * nodes
        out_shape = [
            jax.ShapeDtypeStruct((request_count, columns, dim_value), jnp.float32),
            jax.ShapeDtypeStruct((request_count, columns), jnp.float32),
        ]
    else:
        rows = columns + STAT_ROWS
        out_shape = [jax.ShapeDtypeStruct((request_count, rows, dim_value), jnp.bfloat16)] * lanes
    return pl.pallas_call(
        functools.partial(
            page_kernel,
            first,
            request_count,
            chunk_sizes,
            heads,
            slot_count,
            own,
            joint,
            block,
            1.0 / math.sqrt(DN + dim_rope),
        ),
        in_specs=[SMEM] + [VMEM] * len(operands),
        out_specs=[VMEM] * len(out_shape),
        scratch_shapes=[
            pltpu.VMEM((width, columns), jnp.bfloat16),
            pltpu.VMEM((lanes, heads, request_count * nodes, dim_lat), jnp.bfloat16),
            pltpu.VMEM((lanes, request_count, columns), jnp.float32),
            pltpu.VMEM((page_rows, columns), jnp.float32),
            pltpu.VMEM((reach_size, reach_size), jnp.float32),
        ],
        out_shape=out_shape,
        compiler_params=pltpu.CompilerParams(vmem_limit_bytes=VMEM_LIMIT),
        cost_estimate=pl.CostEstimate(
            flops=2 * request_count * columns * page_rows * (width + dim_lat),
            bytes_accessed=request_count * page_rows * width * 2,
            transcendentals=request_count * columns * page_rows,
        ),
        name=f"pages_{slot_count}_{first}_{request_count}",
    )(table, *operands)


def after(value, *others):
    return lax.optimization_barrier((value, *others))[0]


def chained_shards(
    queries,
    tree_keys,
    parents,
    node_live,
    lengths,
    start_device,
    cache_latent,
    cache_rope,
    up_weight,
):
    size = lax.axis_size("blk")
    position = lax.axis_index("blk")
    request_count, _, columns = queries.shape
    page_rows = cache_latent.shape[1]
    dim_value = up_weight.shape[2]
    heads = up_weight.shape[0] // size
    nodes = columns // heads
    pages = (cache_latent, cache_rope, up_weight)
    page_index = (position - start_device) % size
    live_keys = jnp.clip(lengths - page_index * page_rows, 0, page_rows).astype(jnp.int32)

    def table(steps):
        place = position + jnp.array(steps, jnp.int32)
        valid = ((place >= 0) & (place < size)).astype(jnp.int32)
        return jnp.concatenate([live_keys, valid, jnp.clip(place, 0, size - 1).astype(jnp.int32)])

    half = request_count // 2
    bounds = [(0, half), (half, request_count)] if half else [(0, request_count)]
    parent_row = (parents + nodes * jnp.arange(request_count, dtype=jnp.int32)[:, None]).reshape(1, -1)
    right = [queries[low:high] for low, high in bounds]
    left = list(right)
    sources = []
    valid = []
    outcome = None
    for hop in range(1, size):
        rightward = [(i, i + 1) for i in range(hop - 1, size - 1)]
        leftward = [(i, i - 1) for i in range(1, size - hop + 1)]
        came = (right, left)
        for index in range(len(bounds)):
            if outcome:
                right[index] = after(right[index], *outcome)
                left[index] = after(left[index], *outcome)
        right, left = list(right), list(left)
        sent = [
            (lax.ppermute(right[index], "blk", rightward), lax.ppermute(left[index], "blk", leftward))
            for index in range(len(bounds))
        ]
        if hop == 1:
            outcome = part, stat = run_pages(
                table([0]), [[queries]], 0, pages, tree=(tree_keys, parent_row)
            )
        else:
            back = hop - 1
            outcome = run_pages(
                table([-back, back]), came, 0, pages, joint=2 * back >= size
            )
            send_back(outcome, back, size, position, sources, valid)
        right = [pair[0] for pair in sent]
        left = [pair[1] for pair in sent]
    last = []
    for index, (low, high) in enumerate(bounds):
        answer = run_pages(
            table([1 - size, size - 1]), [[right[index]], [left[index]]], low, pages, joint=True
        )
        last.append((answer, size - 1))
    gathered = []
    for answer, back in last:
        send_back(answer, back, size, position, gathered, [])
    sources.append([piece for source in gathered for piece in source])
    valid.append((position + size - 1 < size) | (position >= size - 1))
    live_rows = jnp.tile(node_live.astype(jnp.float32), (1, heads))
    arrays = [piece for source in sources for piece in source]
    layout = [[piece.shape[0] for piece in source] for source in sources]
    return pl.pallas_call(
        functools.partial(merge_kernel, layout, heads),
        in_specs=[SMEM] + [VMEM] * (3 + len(arrays)),
        out_specs=VMEM,
        out_shape=jax.ShapeDtypeStruct((request_count, nodes, heads * dim_value), jnp.bfloat16),
        compiler_params=pltpu.CompilerParams(vmem_limit_bytes=VMEM_LIMIT),
        name="merge_parts",
    )(jnp.stack(valid).astype(jnp.int32), part, stat, live_rows, *arrays)


def send_back(answer, back, size, position, sources, valid):
    to_left = [(i, i - back) for i in range(back, size)]
    to_right = [(i, i + back) for i in range(size - back)]
    if len(answer) == 1:
        sources.append([lax.ppermute(answer[0], "blk", to_left + to_right)])
        valid.append((position + back < size) | (position >= back))
    else:
        sources.append([lax.ppermute(answer[0], "blk", to_left)])
        valid.append(position + back < size)
        sources.append([lax.ppermute(answer[1], "blk", to_right)])
        valid.append(position >= back)


def solution(mesh):
    size = mesh.shape["blk"]

    def shards(queries, *rest):
        columns = queries.shape[2]
        wide = columns % rest[-1].shape[2] == 0
        plan = chained_shards if wide and 1 < size <= 8 else gathered_shards
        return plan(queries, *rest)

    return jax.shard_map(
        shards,
        mesh=mesh,
        in_specs=(
            P("grp", None, ("head", "blk")),
            P("grp", None, None),
            P("grp", None),
            P("grp", None),
            P("grp"),
            P("grp"),
            P("grp", "blk", None),
            P("grp", None, "blk"),
            P("head", None, None),
        ),
        out_specs=P("grp", None, ("head", "blk")),
        check_vma=False,
    )
```

```python
import functools
import math

import jax
import jax.numpy as jnp
from jax import lax
from jax.experimental import pallas as pl
from jax.experimental.pallas import tpu as pltpu
from jax.sharding import PartitionSpec as P

DN = 128

NEGATIVE = -1e30
STAT_ROWS = 16


def merged(value, axis, join):
    pieces = jax.tree.map(lambda part: lax.all_gather(part, axis), value)
    head = jax.tree.map(lambda part: part[0], pieces)
    tail = jax.tree.map(lambda part: part[1:], pieces)
    subtotal, _ = lax.scan(lambda subtotal, slab: (join(subtotal, slab), None), head, tail)
    return subtotal


def ancestor_matrix(parent_list):
    node_count = parent_list.shape[0]
    ordering = jnp.arange(node_count, dtype=jnp.int32)
    one_hop = (parent_list[:, None] == ordering[None, :]).astype(jnp.float32)
    reached = jnp.maximum(one_hop, jnp.eye(node_count, dtype=jnp.float32))
    for repeat in range(max(node_count - 1, 1).bit_length()):
        reached = jnp.minimum(jnp.dot(reached, reached, precision=lax.Precision.HIGHEST), 1.0)
    return reached


def softmax_update(running, scores, visible, values):
    top_score, weight_sum, summed = running
    masked = jnp.where(visible, scores, -jnp.inf)
    new_top = jnp.maximum(top_score, jnp.max(masked, axis=1))
    factor = jnp.exp(top_score - new_top)
    expweights = jnp.exp(masked - new_top[:, None])
    summed = summed * factor[:, None] + jnp.dot(
        expweights.astype(jnp.bfloat16), values, preferred_element_type=jnp.float32
    )
    return (new_top, weight_sum * factor + jnp.sum(expweights, axis=1), summed)


def join_stats(first_stats, second_stats):
    top_one, sum_one = first_stats
    top_two, sum_two = second_stats
    top_both = jnp.maximum(top_one, top_two)
    return (top_both, sum_one * jnp.exp(top_one - top_both) + sum_two * jnp.exp(top_two - top_both))


def attend_page(running, query_block, lat_page, rope_page, live_count, score_scale):
    dim_lat = lat_page.shape[1]
    query_lat = query_block[:dim_lat]
    query_rope = query_block[dim_lat:]
    key_block = math.gcd(lat_page.shape[0], 512)

    def block_step(block_index, carried):
        first_key = block_index * key_block
        lat_rows = lax.dynamic_slice_in_dim(lat_page, first_key, key_block, 0)
        rope_rows = lax.dynamic_slice_in_dim(rope_page, first_key, key_block, 1)
        scores = lax.dot_general(
            query_lat, lat_rows, (((0,), (1,)), ((), ())), preferred_element_type=jnp.float32
        )
        scores = scores + lax.dot_general(
            query_rope, rope_rows, (((0,), (0,)), ((), ())), preferred_element_type=jnp.float32
        )
        scores = scores * score_scale
        visible = first_key + jnp.arange(key_block, dtype=jnp.int32) < live_count
        return softmax_update(carried, scores, visible[None, :], lat_rows)

    block_count = (live_count + key_block - 1) // key_block
    return lax.fori_loop(0, block_count, block_step, running)


def fresh_state(columns, dim_lat):
    return (
        jnp.full((columns,), NEGATIVE, jnp.float32),
        jnp.zeros((columns,), jnp.float32),
        jnp.zeros((columns, dim_lat), jnp.float32),
    )


def gathered_shards(
    queries,
    tree_keys,
    parents,
    node_live,
    lengths,
    start_device,
    cache_latent,
    cache_rope,
    up_weight,
):
    cycle_size = lax.axis_size("blk")
    position = lax.axis_index("blk")
    request_count = queries.shape[0]
    local_cols = queries.shape[2]
    node_count = tree_keys.shape[1]
    dim_lat = cache_latent.shape[2]
    dim_rope = cache_rope.shape[1]
    dim_value = up_weight.shape[2]
    page_rows = cache_latent.shape[1]
    own_heads = local_cols // node_count
    score_scale = 1.0 / math.sqrt(DN + dim_rope)
    page_index = (position - start_device) % cycle_size
    live_keys = jnp.clip(lengths - page_index * page_rows, 0, page_rows)
    piece = lax.all_gather(queries, "blk", axis=2, tiled=True)
    piece_cols = piece.shape[2]
    tops = []
    sums = []
    accs = []
    for fold_request in range(request_count):
        fold_outcome = attend_page(
            fresh_state(piece_cols, dim_lat),
            piece[fold_request],
            cache_latent[fold_request],
            cache_rope[fold_request],
            live_keys[fold_request],
            score_scale,
        )
        tops.append(fold_outcome[0])
        sums.append(fold_outcome[1])
        accs.append(fold_outcome[2])
    top_all = jnp.stack(tops)
    sum_all = jnp.stack(sums)
    acc_all = jnp.stack(accs)
    reached = jax.vmap(ancestor_matrix)(parents) > 0.5
    tree_tops, tree_sums, tree_accs = ([], [], [])
    for request in range(request_count):
        tree_scores = (
            lax.dot_general(
                queries[request],
                tree_keys[request],
                (((0,), (1,)), ((), ())),
                preferred_element_type=jnp.float32,
            )
            * score_scale
        )
        visible = jnp.tile(reached[request], (own_heads, 1))
        outcome = softmax_update(
            fresh_state(local_cols, dim_lat), tree_scores, visible, tree_keys[request][:, :dim_lat]
        )
        tree_tops.append(outcome[0])
        tree_sums.append(outcome[1])
        tree_accs.append(outcome[2])
    tree_top = jnp.stack(tree_tops)
    tree_sum = jnp.stack(tree_sums)
    tree_acc = jnp.stack(tree_accs)
    own_start = position * local_cols
    own_top = lax.dynamic_slice_in_dim(top_all, own_start, local_cols, 1)
    own_sum = lax.dynamic_slice_in_dim(sum_all, own_start, local_cols, 1)
    own_acc = lax.dynamic_slice_in_dim(acc_all, own_start, local_cols, 1)
    joined = jnp.maximum(own_top, tree_top)
    first_factor = jnp.exp(own_top - joined)
    second_factor = jnp.exp(tree_top - joined)
    top_all = lax.dynamic_update_slice_in_dim(top_all, joined, own_start, 1)
    sum_all = lax.dynamic_update_slice_in_dim(
        sum_all, own_sum * first_factor + tree_sum * second_factor, own_start, 1
    )
    acc_all = lax.dynamic_update_slice_in_dim(
        acc_all,
        own_acc * first_factor[:, :, None] + tree_acc * second_factor[:, :, None],
        own_start,
        1,
    )
    merged_top, merged_sum = merged((top_all, sum_all), "blk", join_stats)
    scaling = jnp.exp(top_all - merged_top) / merged_sum
    normed = acc_all * scaling[:, :, None]
    head_rows = lax.psum_scatter(
        normed.astype(jnp.bfloat16), "blk", scatter_dimension=1, tiled=True
    ).astype(jnp.float32)
    weight_own = lax.dynamic_slice_in_dim(up_weight, position * own_heads, own_heads, 0).astype(
        jnp.float32
    )
    projected = jnp.einsum(
        "rhnd,hdv->rnhv",
        head_rows.reshape(request_count, own_heads, node_count, dim_lat),
        weight_own,
        precision=lax.Precision.HIGHEST,
    )
    verified = projected.reshape(request_count, node_count, own_heads * dim_value)
    live_nodes = node_live.astype(jnp.float32)[:, :, None]
    return (verified * live_nodes).astype(jnp.bfloat16)


def dot_nn(left, right):
    return jnp.dot(left, right, preferred_element_type=jnp.float32)


def dot_tn(left, right):
    return lax.dot_general(
        left, right, (((0,), (0,)), ((), ())), preferred_element_type=jnp.float32
    )


def reach_closure(parent_row):
    count = parent_row.shape[1]
    row = lax.broadcasted_iota(jnp.int32, (count, count), 0)
    lane = lax.broadcasted_iota(jnp.int32, (count, count), 1)
    reached = jnp.where((row == parent_row) | (row == lane), 1.0, 0.0).astype(jnp.bfloat16)
    return reached


def page_softmax(query, lat_ref, rope_ref, request, keys, blocks, block, scale, score_ref, tree):
    dim_lat = lat_ref.shape[2]
    query_lat, query_rope = query[:dim_lat], query[dim_lat:]
    tops = []
    for index in range(blocks):
        span = slice(index * block, (index + 1) * block)
        scores = dot_nn(lat_ref[request, span, :], query_lat)
        scores = (scores + dot_tn(rope_ref[request, :, span], query_rope)) * scale
        place = index * block + lax.broadcasted_iota(jnp.int32, scores.shape, 0)
        scores = jnp.where(place < keys, scores, NEGATIVE)
        score_ref[span, :] = scores
        tops.append(jnp.max(scores, axis=0, keepdims=True))
    if tree is not None:
        tree_keys, visible = tree
        tree_scores = jnp.where(visible > 0.5, dot_nn(tree_keys, query) * scale, NEGATIVE)
        tops.append(jnp.max(tree_scores, axis=0, keepdims=True))
    top = functools.reduce(jnp.maximum, tops)
    total = summed = None
    for index in range(blocks):
        span = slice(index * block, (index + 1) * block)
        weights = jnp.exp(score_ref[span, :] - top)
        weight_sum = jnp.sum(weights, axis=0, keepdims=True)
        values = dot_tn(lat_ref[request, span, :], weights.astype(jnp.bfloat16))
        total = weight_sum if total is None else total + weight_sum
        summed = values if summed is None else summed + values
    if tree is not None:
        weights = jnp.exp(tree_scores - top)
        weight_sum = jnp.sum(weights, axis=0, keepdims=True)
        values = dot_tn(tree_keys[:, :dim_lat], weights.astype(jnp.bfloat16))
        total = weight_sum if total is None else total + weight_sum
        summed = values if summed is None else summed + values
    return summed, total, top


class Book:
    def __init__(self, place_ref, length_ref, start_ref, page_rows):
        self.position, self.half = place_ref[0], place_ref[1]
        self.size = place_ref[2]
        self.lengths, self.starts = length_ref, start_ref
        self.page_rows = page_rows
        self.count = length_ref.shape[0]
        self.apart = shortest(length_ref)
        self.hub = ((self.position > 0) & (self.position < self.size - 1)).astype(jnp.int32)

    def request(self, place):
        moved = place + (place >= self.apart).astype(jnp.int32)
        return jnp.where(place == self.count - 1, self.apart, moved)

    def live(self, request, position):
        page = lax.rem(position - self.starts[request] + self.size, self.size)
        return jnp.clip(self.lengths[request] - page * self.page_rows, 0, self.page_rows)


def shortest(length_ref):
    best, index = length_ref[0], jnp.int32(0)
    for each in range(1, length_ref.shape[0]):
        less = length_ref[each] < best
        index = jnp.where(less, each, index)
        best = jnp.minimum(best, length_ref[each])
    return index


def sort_kernel(length_ref, query_ref, long_ref, apart_ref, sems):
    apart = shortest(length_ref)
    copies = [pltpu.make_async_copy(query_ref.at[apart], apart_ref.at[0], sems.at[0])]
    for place in range(long_ref.shape[0]):
        request = place + (place >= apart).astype(jnp.int32)
        copies.append(
            pltpu.make_async_copy(query_ref.at[request], long_ref.at[place], sems.at[place + 1])
        )
    for copy in copies:
        copy.start()
    for copy in copies:
        copy.wait()


def rope_pieces(half, width):
    return [(low, min(width, half - low)) for low in range(0, half, width)]


def pack_kernel(place_ref, length_ref, lat_ref, rope_ref, out_ref, sems):
    apart = shortest(length_ref)
    half = lat_ref.shape[1] // 2
    dim_rope = rope_ref.shape[1]
    width = lat_ref.shape[2]
    low = pl.multiple_of(place_ref[1] * half, 128)
    copies = [
        pltpu.make_async_copy(
            lat_ref.at[apart, pl.ds(low, half), :], out_ref.at[pl.ds(0, half), :], sems.at[0]
        )
    ]
    for index, (at, size) in enumerate(rope_pieces(half, width)):
        copies.append(
            pltpu.make_async_copy(
                rope_ref.at[apart, :, pl.ds(pl.multiple_of(low + at, 128), size)],
                out_ref.at[pl.ds(half + index * dim_rope, dim_rope), pl.ds(0, size)],
                sems.at[index + 1],
            )
        )
    for copy in copies:
        copy.start()
    for copy in copies:
        copy.wait()


def variants(keys, block_count, block, action):
    step = 2 if block_count % 2 == 0 else 1
    for blocks in range(step, block_count + 1, step):

        @pl.when((keys > (blocks - step) * block) & (keys <= blocks * block))
        def _():
            action(blocks)


def spans(place, nodes):
    if isinstance(place, int):
        return slice(place * nodes, (place + 1) * nodes), slice(place, place + 1)
    return pl.ds(pl.multiple_of(place * nodes, nodes), nodes), pl.ds(place, 1)


def store_value(rows_ref, level_ref, lane, place, nodes, summed, total, top):
    heads, _, dim_lat = rows_ref.shape[1:]
    span, line = spans(place, nodes)
    normed = (summed * (1.0 / total)).astype(jnp.bfloat16)
    rows_ref[lane, :, span, :] = normed.T.reshape(heads, nodes, dim_lat)
    level_ref[lane, line, :] = top + jnp.log(total)


def store_nothing(rows_ref, level_ref, lane, place, nodes):
    heads, _, dim_lat = rows_ref.shape[1:]
    span, line = spans(place, nodes)
    rows_ref[lane, :, span, :] = jnp.zeros((heads, nodes, dim_lat), jnp.bfloat16)
    level_ref[lane, line, :] = jnp.full((1, level_ref.shape[2]), NEGATIVE, jnp.float32)


def project(rows_ref, level_ref, weight_ref, lane, count, nodes, out_ref, stat_ref=None):
    heads = rows_ref.shape[1]
    columns, dim_value = level_ref.shape[2], weight_ref.shape[3]
    for head in range(heads):
        value = dot_nn(rows_ref[lane, head], weight_ref[lane, head])
        for each in range(count):
            piece = value[each * nodes : (each + 1) * nodes].astype(out_ref.dtype)
            out_ref[each, head * nodes : (head + 1) * nodes, :] = piece
    if stat_ref is not None:
        stat_ref[...] = level_ref[lane]
        return
    for each in range(count):
        out_ref[each, columns:, :] = level_rows(level_ref[lane, each : each + 1, :], dim_value)


def page_kernel(steps, own, block, scale, place_ref, length_ref, start_ref, *refs):
    refs = list(refs)
    query_refs = [[refs.pop(0) for _ in group] for group in steps]
    if own:
        apart_query_ref = refs.pop(0)
    lat_hbm, rope_hbm, weight_hbm = refs.pop(0), refs.pop(0), refs.pop(0)
    if own:
        tree_ref, parent_ref, part_ref, stat_ref = [refs.pop(0) for _ in range(4)]
        out_refs = [part_ref]
    else:
        out_refs = [refs.pop(0) for _ in steps]
    query_ref, lat_ref, rope_ref, weight_ref, rows_ref, level_ref, score_ref, reach_ref = refs[:8]
    page_sems, weight_sems = refs[8:]
    page_rows = lat_ref.shape[1]
    book = Book(place_ref, length_ref, start_ref, page_rows)
    heads = weight_ref.shape[1]
    columns = query_ref.shape[1]
    nodes = columns // heads
    lanes = len(steps)
    count = book.count - (0 if own else 1)
    block_count = page_rows // block

    flags = []
    shards = []
    for group in steps:
        flag = shard = jnp.int32(0)
        for step in group:
            there = book.position + step
            exists = ((there >= 0) & (there < book.size)).astype(jnp.int32)
            flag = flag + exists
            shard = shard + exists * there
        flags.append(flag)
        shards.append(shard)
    any_flag = jnp.minimum(functools.reduce(jnp.add, flags), 1)

    def keys_at(place):
        request = book.request(place)
        keys = book.live(request, book.position) * any_flag
        if own:
            keys = keys * jnp.where(place == count - 1, book.hub, 1)
        return request, keys

    def page_copies(place):
        request, keys = keys_at(place)
        return keys, [
            pltpu.make_async_copy(lat_hbm.at[request], lat_ref.at[place], page_sems.at[place, 0]),
            pltpu.make_async_copy(rope_hbm.at[request], rope_ref.at[place], page_sems.at[place, 1]),
        ]

    def weight_copy(lane):
        low = pl.multiple_of(shards[lane] * heads, heads)
        return pltpu.make_async_copy(
            weight_hbm.at[pl.ds(low, heads)], weight_ref.at[lane], weight_sems.at[lane]
        )

    for place in range(count):
        keys, copies = page_copies(jnp.int32(place))

        @pl.when(keys > 0)
        def _():
            for copy in copies:
                copy.start()

    for lane in range(lanes):

        @pl.when(flags[lane] > 0)
        def _():
            weight_copy(lane).start()

    if own:
        reached = reach_closure(parent_ref[...])
        for _ in range(max(nodes - 1, 1).bit_length()):
            reached = jnp.minimum(dot_nn(reached, reached), 1.0).astype(jnp.bfloat16)
        reach_ref[...] = reached.astype(jnp.float32)

    def item_step(item, carry):
        place = lax.div(item, lanes)
        lane = lax.rem(item, lanes)
        request, keys = keys_at(place)
        keys_here = keys
        if lanes > 1:
            here = functools.reduce(
                jnp.add, [flags[each] * (lane == each).astype(jnp.int32) for each in range(lanes)]
            )
            keys_here = keys * here

        @pl.when((keys > 0) & (lane == 0))
        def _():
            for copy in page_copies(place)[1]:
                copy.wait()

        for each, group in enumerate(steps):
            for step, ref in zip(group, query_refs[each]):
                there = book.position + step
                chosen = (there >= 0) & (there < book.size) & (lane == each) & (keys_here + int(own) > 0)
                if own:
                    chosen = chosen & (place < count - 1)

                @pl.when(chosen)
                def _():
                    query_ref[...] = ref[place]

        if own:

            @pl.when(place == count - 1)
            def _():
                query_ref[...] = apart_query_ref[0]

        def attend(blocks):
            tree = None
            if own:
                base = pl.multiple_of(request * nodes, nodes)
                row = lax.broadcasted_iota(jnp.int32, (reach_ref.shape[1], columns), 0)
                along = lax.broadcasted_iota(jnp.int32, (reach_ref.shape[1], columns), 1)
                pick = jnp.where(row == base + along % nodes, 1.0, 0.0).astype(jnp.bfloat16)
                near = reach_ref[pl.ds(base, nodes), :].astype(jnp.bfloat16)
                tree = (tree_ref[request], dot_nn(near, pick))
            outcome = page_softmax(
                query_ref[...], lat_ref, rope_ref, place, keys, blocks, block, scale, score_ref, tree
            )
            store_value(rows_ref, level_ref, lane, place, nodes, *outcome)

        variants(keys_here, block_count, block, attend)

        @pl.when(keys_here <= 0)
        def _():
            if own:
                attend(0)
            else:
                store_nothing(rows_ref, level_ref, lane, place, nodes)

        return carry

    lax.fori_loop(0, count * lanes * any_flag, item_step, 0)
    for lane in range(lanes):

        @pl.when(flags[lane] > 0)
        def _():
            weight_copy(lane).wait()
            project(
                rows_ref, level_ref, weight_ref, lane, count, nodes, out_refs[lane],
                stat_ref if own else None,
            )


def hub_kernel(block, scale, place_ref, length_ref, start_ref, *refs):
    refs = list(refs)
    left_ref, right_ref, far_ref, own_ref, mine_ref, other_ref = [refs.pop(0) for _ in range(6)]
    lat_hbm, rope_hbm, weight_hbm = [refs.pop(0) for _ in range(3)]
    held_refs = [refs.pop(0) for _ in range(3)]
    out_refs = [refs.pop(0) for _ in range(3)]
    part_ref, stat_ref = refs.pop(0), refs.pop(0)
    query_ref, lat_ref, rope_ref, weight_ref, rows_ref, level_ref, score_ref = refs[:7]
    sum_ref, acc_ref, page_sems, weight_sems = refs[7:]
    page_rows, dim_lat = lat_ref.shape[1:]
    dim_rope = rope_ref.shape[1]
    book = Book(place_ref, length_ref, start_ref, page_rows)
    heads, columns = weight_ref.shape[1], query_ref.shape[1]
    nodes = columns // heads
    half = page_rows // 2
    block_count = page_rows // block
    request = book.apart
    low_side = book.position * 2 < book.size
    end = jnp.where(low_side, 0, book.size - 1)
    far = jnp.where(low_side, book.position + 2, book.position - 2)
    shards = [book.position - 1, book.position + 1, far, book.position]
    live = [book.live(request, book.position), book.live(request, end)]
    query_refs = [left_ref, right_ref, far_ref, own_ref]

    for out_ref, held_ref in zip(out_refs, held_refs):
        out_ref[: held_ref.shape[0]] = held_ref[...]

    @pl.when(book.hub == 0)
    def _():
        for out_ref in out_refs:
            last = out_ref.shape[0] - 1
            out_ref[last, :columns, :] = jnp.zeros((columns, out_ref.shape[2]), out_ref.dtype)
            nothing = jnp.full((1, columns), NEGATIVE, jnp.float32)
            out_ref[last, columns:, :] = level_rows(nothing, out_ref.shape[2])
        part_ref[...] = jnp.zeros_like(part_ref)
        stat_ref[...] = jnp.full_like(stat_ref, NEGATIVE)

    @pl.when(book.hub > 0)
    def _():
        page_copies = [
            pltpu.make_async_copy(lat_hbm.at[request], lat_ref.at[0], page_sems.at[0]),
            pltpu.make_async_copy(rope_hbm.at[request], rope_ref.at[0], page_sems.at[1]),
        ]
        weight_copies = [
            pltpu.make_async_copy(
                weight_hbm.at[pl.ds(pl.multiple_of(shard * heads, heads), heads)],
                weight_ref.at[lane],
                weight_sems.at[lane],
            )
            for lane, shard in enumerate(shards)
        ]
        for copy in page_copies + weight_copies:
            copy.start()
        for side in range(2):

            @pl.when(book.half == side)
            def _():
                for ref, part in ((mine_ref, side), (other_ref, 1 - side)):
                    lat_ref[1, part * half : (part + 1) * half, :] = ref[:half, :]
                    for index, (at, size) in enumerate(rope_pieces(half, dim_lat)):
                        top = half + index * dim_rope
                        rope_ref[1, :, part * half + at : part * half + at + size] = ref[
                            top : top + dim_rope, :size
                        ]

        for copy in page_copies:
            copy.wait()

        def item_step(item, carry):
            lane, page = lax.div(item, 2), lax.rem(item, 2)
            keys = jnp.where(page == 0, jnp.where(lane == 3, 0, live[0]), live[1])

            @pl.when(page == 0)
            def _():
                for each, ref in enumerate(query_refs):

                    @pl.when(lane == each)
                    def _():
                        query_ref[...] = ref[0]

                sum_ref[0:1, :] = jnp.zeros((1, columns), jnp.float32)
                sum_ref[1:2, :] = jnp.full((1, columns), NEGATIVE, jnp.float32)
                acc_ref[...] = jnp.zeros_like(acc_ref)

            def attend(blocks):
                summed, total, top = page_softmax(
                    query_ref[...], lat_ref, rope_ref, page, keys, blocks, block, scale, score_ref, None
                )
                old_top = sum_ref[1:2, :]
                new_top = jnp.maximum(old_top, top)
                old_share, new_share = jnp.exp(old_top - new_top), jnp.exp(top - new_top)
                sum_ref[0:1, :] = sum_ref[0:1, :] * old_share + total * new_share
                sum_ref[1:2, :] = new_top
                acc_ref[...] = acc_ref[...] * old_share + summed * new_share

            variants(keys, block_count, block, attend)
            some = jnp.where(lane == 3, 0, live[0]) + live[1]

            @pl.when((page == 1) & (some > 0))
            def _():
                outcome = acc_ref[...], sum_ref[0:1, :], sum_ref[1:2, :]
                store_value(rows_ref, level_ref, lane, 0, nodes, *outcome)

            @pl.when((page == 1) & (some <= 0))
            def _():
                store_nothing(rows_ref, level_ref, lane, 0, nodes)

            return carry

        lax.fori_loop(0, 8, item_step, 0)
        for copy in weight_copies:
            copy.wait()
        for lane, out_ref in enumerate(out_refs):
            last = out_ref.shape[0] - 1
            project(rows_ref, level_ref, weight_ref, lane, 1, nodes, out_ref.at[last : last + 1])
        project(rows_ref, level_ref, weight_ref, 3, 1, nodes, part_ref, stat_ref)


def level_rows(level, lanes):
    pieces = []
    rest = level
    for _ in range(3):
        piece = rest.astype(jnp.bfloat16).astype(jnp.float32)
        rest = rest - piece
        pieces.append(piece)
    rows = [
        piece[:, first : first + lanes] for piece in pieces for first in range(0, level.shape[1], lanes)
    ]
    rows.append(jnp.zeros((STAT_ROWS - len(rows), lanes), jnp.float32))
    return jnp.concatenate(rows, axis=0).astype(jnp.bfloat16)


def level_row(block, columns):
    per = columns // block.shape[1]
    block = block.astype(jnp.float32)
    return jnp.concatenate(
        [block[i : i + 1] + block[per + i : per + i + 1] + block[2 * per + i : 2 * per + i + 1] for i in range(per)],
        axis=1,
    )


def merge_kernel(layout, heads, place_ref, length_ref, start_ref, part_ref, stat_ref, live_ref,
                 apart_ref, apart_stat_ref, *refs):
    book = Book(place_ref, length_ref, start_ref, 1)
    request_count, columns, dim_value = part_ref.shape
    nodes = columns // heads
    remote_refs, out_ref = refs[: len(layout)], refs[len(layout)]
    nothing = jnp.full((1, columns), NEGATIVE, jnp.float32)
    requests = [book.request(jnp.int32(place)) for place in range(request_count)]
    levels = [stat_ref[...]]
    for steps, ref in zip(layout, remote_refs):
        held = ref.shape[0]
        level = jnp.concatenate(
            [level_row(ref[each, columns:, :], columns) for each in range(held)]
            + [nothing] * (request_count - held),
            axis=0,
        )
        exists = functools.reduce(
            jnp.logical_or,
            [(book.position + step >= 0) & (book.position + step < book.size) for step in steps],
        )
        levels.append(jnp.where(exists, level, NEGATIVE))
    levels.append(jnp.concatenate([nothing] * (request_count - 1) + [apart_stat_ref[...]], axis=0))
    top = functools.reduce(jnp.maximum, levels)
    weights = [jnp.exp(level - top) for level in levels]
    keep = jnp.concatenate([live_ref[pl.ds(request, 1), :] for request in requests], axis=0)
    total = keep / functools.reduce(jnp.add, weights)
    stacked = [weight * total for weight in weights]
    filler = -len(stacked) * request_count % 8
    if filler:
        stacked.append(jnp.zeros((filler, columns), jnp.float32))
    shares = jnp.concatenate(stacked, axis=0).T
    for place in range(request_count):
        value = part_ref[place] * shares[:, place : place + 1]
        for index, ref in enumerate(remote_refs):
            if place >= ref.shape[0]:
                continue
            at = (index + 1) * request_count + place
            value = value + ref[place, :columns, :].astype(jnp.float32) * shares[:, at : at + 1]
        if place == request_count - 1:
            at = (len(layout) + 1) * request_count + place
            value = value + apart_ref[0] * shares[:, at : at + 1]
        for head in range(heads):
            rows = value[head * nodes : (head + 1) * nodes].astype(jnp.bfloat16)
            out_ref[requests[place], :, head * dim_value : (head + 1) * dim_value] = rows


VMEM = pl.BlockSpec(memory_space=pltpu.VMEM)
SMEM = pl.BlockSpec(memory_space=pltpu.SMEM)
HBM = pl.BlockSpec(memory_space=pltpu.HBM)
VMEM_LIMIT = 57 << 20


def call(kernel, name, operands, out_shapes, scratch, flops=0, limit=VMEM_LIMIT):
    return pl.pallas_call(
        kernel,
        in_specs=[spec for spec, _ in operands],
        out_specs=[VMEM] * len(out_shapes),
        scratch_shapes=scratch,
        out_shape=[jax.ShapeDtypeStruct(shape, dtype) for shape, dtype in out_shapes],
        compiler_params=pltpu.CompilerParams(vmem_limit_bytes=limit),
        cost_estimate=pl.CostEstimate(flops=flops, bytes_accessed=flops // 256, transcendentals=0),
        name=name,
    )(*[array for _, array in operands])


def after(value, *others):
    return lax.optimization_barrier((value, *others))[0]


def hub_shards(
    queries,
    tree_keys,
    parents,
    node_live,
    lengths,
    start_device,
    cache_latent,
    cache_rope,
    up_weight,
):
    size = lax.axis_size("blk")
    head_size = lax.axis_size("head")
    request_count, width, columns = queries.shape
    page_rows, dim_lat = cache_latent.shape[1:]
    dim_rope = cache_rope.shape[1]
    dim_value = up_weight.shape[2]
    heads = up_weight.shape[0] // size
    nodes = columns // heads
    rows = columns + STAT_ROWS
    block = math.gcd(page_rows, 256)
    scale = 1.0 / math.sqrt(DN + dim_rope)
    most = request_count - 1
    bf16, f32 = jnp.bfloat16, jnp.float32
    dma = pltpu.SemaphoreType.DMA
    position = lax.axis_index("blk")
    here = jnp.stack([position, lax.axis_index("head") % 2, jnp.int32(size)]).astype(jnp.int32)
    scalars = [(SMEM, here), (SMEM, lengths), (SMEM, start_device)]
    pages = [(HBM, cache_latent), (HBM, cache_rope), (HBM, up_weight)]
    unit_flops = 2 * columns * page_rows * (width + dim_lat)

    long, apart = call(
        sort_kernel,
        "sort_queries",
        [(SMEM, lengths), (HBM, queries)],
        [((most, width, columns), bf16), ((1, width, columns), bf16)],
        [dma((request_count,))],
    )
    half = page_rows // 2
    pieces = rope_pieces(half, dim_lat)

    def answer(name, steps, query_groups, own=()):
        lanes = len(steps)
        count = request_count if own else most
        operands = scalars + [(VMEM, query) for group in query_groups for query in group]
        if own:
            operands += [(VMEM, own[0])]
        operands += pages
        if own:
            operands += [(VMEM, array) for array in own[1:]]
            outs = [((count, columns, dim_value), f32), ((count, columns), f32)]
        else:
            outs = [((count, rows, dim_value), bf16)] * lanes
        reach_size = request_count * nodes if own else 8
        return call(
            functools.partial(page_kernel, steps, bool(own), block, scale),
            name,
            operands,
            outs,
            [
                pltpu.VMEM((width, columns), bf16),
                pltpu.VMEM((count, page_rows, dim_lat), bf16),
                pltpu.VMEM((count, dim_rope, page_rows), bf16),
                pltpu.VMEM((lanes, heads, dim_lat, dim_value), bf16),
                pltpu.VMEM((lanes, heads, count * nodes, dim_lat), bf16),
                pltpu.VMEM((lanes, count, columns), f32),
                pltpu.VMEM((page_rows, columns), f32),
                pltpu.VMEM((reach_size, reach_size), f32),
                dma((count, 2)),
                dma((lanes,)),
            ],
            unit_flops * lanes * count,
        )

    def shift(value, pairs):
        return lax.ppermute(value, "blk", pairs)

    right1 = shift(long, [(i, i + 1) for i in range(size - 1)])
    left1 = shift(long, [(i, i - 1) for i in range(1, size)])
    (packed,) = call(
        pack_kernel,
        "pack_page",
        [(SMEM, here), (SMEM, lengths), (HBM, cache_latent), (HBM, cache_rope)],
        [((half + len(pieces) * dim_rope, dim_lat), bf16)],
        [dma((1 + len(pieces),))],
    )
    mine = shift(packed, [(0, 1), (size - 1, size - 2)])
    apart_right = shift(apart, [(i, i + 1) for i in range(size - 2)])
    apart_left = shift(apart, [(i, i - 1) for i in range(2, size)])
    parent_row = (parents + nodes * jnp.arange(request_count, dtype=jnp.int32)[:, None]).reshape(1, -1)
    live_rows = jnp.tile(node_live.astype(f32), (1, heads))
    part, stat = answer("own_pages", [[0]], [[long]], (apart, tree_keys, parent_row))
    right2 = shift(after(right1, part, apart_right, apart_left), [(i, i + 1) for i in range(1, size - 1)])
    left2 = shift(after(left1, part, apart_right, apart_left), [(i, i - 1) for i in range(1, size - 1)])
    first = answer("first_hop", [[-1], [1]], [[right1], [left1]])
    swapped = lax.ppermute(
        after(mine, *first),
        ("blk", "head"),
        [(i * head_size + j, i * head_size + (j ^ 1)) for i in (1, size - 2) for j in range(head_size)],
    )
    crossing = jnp.where(position * 2 < size, apart_right, apart_left)
    apart_far = shift(crossing, [(1, size - 2), (size - 2, 1)])
    right3 = shift(after(right2, *first), [(size - 2, size - 1)])
    left3 = shift(after(left2, *first), [(1, 0)])
    (second,) = answer("second_hop", [[-2, 2]], [[right2, left2]])
    to_left, to_right, to_far, apart_part, apart_stat = call(
        functools.partial(hub_kernel, block, scale),
        "hub_pages",
        scalars
        + [(VMEM, array) for array in (apart_right, apart_left, apart_far, apart, mine, swapped)]
        + pages
        + [(VMEM, array) for array in (*first, second)],
        [((request_count, rows, dim_value), bf16)] * 3
        + [((1, columns, dim_value), f32), ((1, columns), f32)],
        [
            pltpu.VMEM((width, columns), bf16),
            pltpu.VMEM((2, page_rows, dim_lat), bf16),
            pltpu.VMEM((2, dim_rope, page_rows), bf16),
            pltpu.VMEM((4, heads, dim_lat, dim_value), bf16),
            pltpu.VMEM((4, heads, nodes, dim_lat), bf16),
            pltpu.VMEM((4, 1, columns), f32),
            pltpu.VMEM((page_rows, columns), f32),
            pltpu.VMEM((8, columns), f32),
            pltpu.VMEM((dim_lat, columns), f32),
            dma((2,)),
            dma((4,)),
        ],
        unit_flops * 7,
    )
    from_right = shift(to_left, [(i, i - 1) for i in range(1, size)])
    from_left = shift(to_right, [(i, i + 1) for i in range(size - 1)])
    from_far = shift(to_far, [(i, i - 2) for i in range(2, size)] + [(i, i + 2) for i in range(size - 2)])
    (third,) = answer(
        "third_hop", [[1 - size, size - 1]], [[after(right3, to_far), left3]]
    )
    from_end = shift(third, [(0, size - 1), (size - 1, 0)])
    (verified,) = call(
        functools.partial(merge_kernel, [[1], [-1], [-2, 2], [1 - size, size - 1]], heads),
        "merge_parts",
        scalars
        + [
            (VMEM, array)
            for array in (
                part, stat, live_rows, apart_part, apart_stat, from_right, from_left, from_far, from_end
            )
        ],
        [((request_count, nodes, heads * dim_value), bf16)],
        [],
        limit=12 << 20,
    )
    return verified


def solution(mesh):
    size = mesh.shape["blk"]
    even = mesh.shape["head"] % 2 == 0

    def shards(queries, *rest):
        columns = queries.shape[2]
        cache_latent, _, up_weight = rest[-3:]
        wide = columns % up_weight.shape[2] == 0 and cache_latent.shape[1] % 256 == 0
        plan = hub_shards if wide and size == 4 and even and queries.shape[0] > 1 else gathered_shards
        return plan(queries, *rest)

    return jax.shard_map(
        shards,
        mesh=mesh,
        in_specs=(
            P("grp", None, ("head", "blk")),
            P("grp", None, None),
            P("grp", None),
            P("grp", None),
            P("grp"),
            P("grp"),
            P("grp", "blk", None),
            P("grp", None, "blk"),
            P("head", None, None),
        ),
        out_specs=P("grp", None, ("head", "blk")),
        check_vma=False,
    )
```

```python
import functools
import math

import jax
import jax.numpy as jnp
from jax import lax
from jax.experimental import pallas as pl
from jax.experimental.pallas import tpu as pltpu
from jax.sharding import PartitionSpec as P

DN = 128

NEGATIVE = -1e30
STAT_ROWS = 16


def merged(value, axis, join):
    pieces = jax.tree.map(lambda part: lax.all_gather(part, axis), value)
    head = jax.tree.map(lambda part: part[0], pieces)
    tail = jax.tree.map(lambda part: part[1:], pieces)
    subtotal, _ = lax.scan(lambda subtotal, slab: (join(subtotal, slab), None), head, tail)
    return subtotal


def ancestor_matrix(parent_list):
    node_count = parent_list.shape[0]
    ordering = jnp.arange(node_count, dtype=jnp.int32)
    one_hop = (parent_list[:, None] == ordering[None, :]).astype(jnp.float32)
    reached = jnp.maximum(one_hop, jnp.eye(node_count, dtype=jnp.float32))
    for repeat in range(max(node_count - 1, 1).bit_length()):
        reached = jnp.minimum(jnp.dot(reached, reached, precision=lax.Precision.HIGHEST), 1.0)
    return reached


def softmax_update(running, scores, visible, values):
    top_score, weight_sum, summed = running
    masked = jnp.where(visible, scores, -jnp.inf)
    new_top = jnp.maximum(top_score, jnp.max(masked, axis=1))
    factor = jnp.exp(top_score - new_top)
    expweights = jnp.exp(masked - new_top[:, None])
    summed = summed * factor[:, None] + jnp.dot(
        expweights.astype(jnp.bfloat16), values, preferred_element_type=jnp.float32
    )
    return (new_top, weight_sum * factor + jnp.sum(expweights, axis=1), summed)


def join_stats(first_stats, second_stats):
    top_one, sum_one = first_stats
    top_two, sum_two = second_stats
    top_both = jnp.maximum(top_one, top_two)
    return (top_both, sum_one * jnp.exp(top_one - top_both) + sum_two * jnp.exp(top_two - top_both))


def attend_page(running, query_block, lat_page, rope_page, live_count, score_scale):
    dim_lat = lat_page.shape[1]
    query_lat = query_block[:dim_lat]
    query_rope = query_block[dim_lat:]
    key_block = math.gcd(lat_page.shape[0], 512)

    def block_step(block_index, carried):
        first_key = block_index * key_block
        lat_rows = lax.dynamic_slice_in_dim(lat_page, first_key, key_block, 0)
        rope_rows = lax.dynamic_slice_in_dim(rope_page, first_key, key_block, 1)
        scores = lax.dot_general(
            query_lat, lat_rows, (((0,), (1,)), ((), ())), preferred_element_type=jnp.float32
        )
        scores = scores + lax.dot_general(
            query_rope, rope_rows, (((0,), (0,)), ((), ())), preferred_element_type=jnp.float32
        )
        scores = scores * score_scale
        visible = first_key + jnp.arange(key_block, dtype=jnp.int32) < live_count
        return softmax_update(carried, scores, visible[None, :], lat_rows)

    block_count = (live_count + key_block - 1) // key_block
    return lax.fori_loop(0, block_count, block_step, running)


def fresh_state(columns, dim_lat):
    return (
        jnp.full((columns,), NEGATIVE, jnp.float32),
        jnp.zeros((columns,), jnp.float32),
        jnp.zeros((columns, dim_lat), jnp.float32),
    )


def gathered_shards(
    queries,
    tree_keys,
    parents,
    node_live,
    lengths,
    start_device,
    cache_latent,
    cache_rope,
    up_weight,
):
    cycle_size = lax.axis_size("blk")
    position = lax.axis_index("blk")
    request_count = queries.shape[0]
    local_cols = queries.shape[2]
    node_count = tree_keys.shape[1]
    dim_lat = cache_latent.shape[2]
    dim_rope = cache_rope.shape[1]
    dim_value = up_weight.shape[2]
    page_rows = cache_latent.shape[1]
    own_heads = local_cols // node_count
    score_scale = 1.0 / math.sqrt(DN + dim_rope)
    page_index = (position - start_device) % cycle_size
    live_keys = jnp.clip(lengths - page_index * page_rows, 0, page_rows)
    piece = lax.all_gather(queries, "blk", axis=2, tiled=True)
    piece_cols = piece.shape[2]
    tops = []
    sums = []
    accs = []
    for fold_request in range(request_count):
        fold_outcome = attend_page(
            fresh_state(piece_cols, dim_lat),
            piece[fold_request],
            cache_latent[fold_request],
            cache_rope[fold_request],
            live_keys[fold_request],
            score_scale,
        )
        tops.append(fold_outcome[0])
        sums.append(fold_outcome[1])
        accs.append(fold_outcome[2])
    top_all = jnp.stack(tops)
    sum_all = jnp.stack(sums)
    acc_all = jnp.stack(accs)
    reached = jax.vmap(ancestor_matrix)(parents) > 0.5
    tree_tops, tree_sums, tree_accs = ([], [], [])
    for request in range(request_count):
        tree_scores = (
            lax.dot_general(
                queries[request],
                tree_keys[request],
                (((0,), (1,)), ((), ())),
                preferred_element_type=jnp.float32,
            )
            * score_scale
        )
        visible = jnp.tile(reached[request], (own_heads, 1))
        outcome = softmax_update(
            fresh_state(local_cols, dim_lat), tree_scores, visible, tree_keys[request][:, :dim_lat]
        )
        tree_tops.append(outcome[0])
        tree_sums.append(outcome[1])
        tree_accs.append(outcome[2])
    tree_top = jnp.stack(tree_tops)
    tree_sum = jnp.stack(tree_sums)
    tree_acc = jnp.stack(tree_accs)
    own_start = position * local_cols
    own_top = lax.dynamic_slice_in_dim(top_all, own_start, local_cols, 1)
    own_sum = lax.dynamic_slice_in_dim(sum_all, own_start, local_cols, 1)
    own_acc = lax.dynamic_slice_in_dim(acc_all, own_start, local_cols, 1)
    joined = jnp.maximum(own_top, tree_top)
    first_factor = jnp.exp(own_top - joined)
    second_factor = jnp.exp(tree_top - joined)
    top_all = lax.dynamic_update_slice_in_dim(top_all, joined, own_start, 1)
    sum_all = lax.dynamic_update_slice_in_dim(
        sum_all, own_sum * first_factor + tree_sum * second_factor, own_start, 1
    )
    acc_all = lax.dynamic_update_slice_in_dim(
        acc_all,
        own_acc * first_factor[:, :, None] + tree_acc * second_factor[:, :, None],
        own_start,
        1,
    )
    merged_top, merged_sum = merged((top_all, sum_all), "blk", join_stats)
    scaling = jnp.exp(top_all - merged_top) / merged_sum
    normed = acc_all * scaling[:, :, None]
    head_rows = lax.psum_scatter(
        normed.astype(jnp.bfloat16), "blk", scatter_dimension=1, tiled=True
    ).astype(jnp.float32)
    weight_own = lax.dynamic_slice_in_dim(up_weight, position * own_heads, own_heads, 0).astype(
        jnp.float32
    )
    projected = jnp.einsum(
        "rhnd,hdv->rnhv",
        head_rows.reshape(request_count, own_heads, node_count, dim_lat),
        weight_own,
        precision=lax.Precision.HIGHEST,
    )
    verified = projected.reshape(request_count, node_count, own_heads * dim_value)
    live_nodes = node_live.astype(jnp.float32)[:, :, None]
    return (verified * live_nodes).astype(jnp.bfloat16)


def dot_nn(left, right):
    return jnp.dot(left, right, preferred_element_type=jnp.float32)


def dot_tn(left, right):
    return lax.dot_general(
        left, right, (((0,), (0,)), ((), ())), preferred_element_type=jnp.float32
    )


def reach_closure(parent_row):
    count = parent_row.shape[1]
    row = lax.broadcasted_iota(jnp.int32, (count, count), 0)
    lane = lax.broadcasted_iota(jnp.int32, (count, count), 1)
    reached = jnp.where((row == parent_row) | (row == lane), 1.0, 0.0).astype(jnp.bfloat16)
    return reached


def page_softmax(query, lat_ref, rope_ref, page, keys, blocks, block, scale, score_ref, tree):
    dim_lat = lat_ref.shape[2]
    columns = query.shape[1]
    query_lat, query_rope = query[:dim_lat], query[dim_lat:]
    tops = []
    for index in range(blocks):
        span = slice(index * block, (index + 1) * block)
        scores = dot_nn(lat_ref[page, span, :], query_lat)
        scores = scores + dot_tn(rope_ref[page, :, span], query_rope)
        if index >= blocks - 2:
            place = index * block + lax.broadcasted_iota(jnp.int32, scores.shape, 0)
            scores = jnp.where(place < keys, scores, NEGATIVE)
        score_ref[span, :columns] = scores
        tops.append(jnp.max(scores, axis=0, keepdims=True))
    if tree is not None:
        tree_keys, visible = tree
        tree_scores = jnp.where(visible > 0.5, dot_nn(tree_keys, query), NEGATIVE)
        tops.append(jnp.max(tree_scores, axis=0, keepdims=True))
    top = functools.reduce(jnp.maximum, tops)
    base_two = scale * math.log2(math.e)
    shift = top * base_two
    total = summed = None
    for index in range(blocks):
        span = slice(index * block, (index + 1) * block)
        weights = jnp.exp2(score_ref[span, :columns] * base_two - shift)
        weight_sum = jnp.sum(weights, axis=0, keepdims=True)
        values = dot_tn(lat_ref[page, span, :], weights.astype(jnp.bfloat16))
        total = weight_sum if total is None else total + weight_sum
        summed = values if summed is None else summed + values
    if tree is not None:
        weights = jnp.exp2(tree_scores * base_two - shift)
        weight_sum = jnp.sum(weights, axis=0, keepdims=True)
        values = dot_tn(tree_keys[:, :dim_lat], weights.astype(jnp.bfloat16))
        total = weight_sum if total is None else total + weight_sum
        summed = values if summed is None else summed + values
    return summed, total, top * scale


class Book:
    def __init__(self, place_ref, length_ref, start_ref, page_rows):
        self.position, self.half = place_ref[0], place_ref[1]
        self.size = place_ref[2]
        self.lengths, self.starts = length_ref, start_ref
        self.page_rows = page_rows
        self.count = length_ref.shape[0]
        self.apart = shortest(length_ref)
        self.hub = ((self.position > 0) & (self.position < self.size - 1)).astype(jnp.int32)

    def request(self, place):
        moved = place + (place >= self.apart).astype(jnp.int32)
        return jnp.where(place == self.count - 1, self.apart, moved)

    def live(self, request, position):
        page = lax.rem(position - self.starts[request] + self.size, self.size)
        return jnp.clip(self.lengths[request] - page * self.page_rows, 0, self.page_rows)


def shortest(length_ref):
    best, index = length_ref[0], jnp.int32(0)
    for each in range(1, length_ref.shape[0]):
        less = length_ref[each] < best
        index = jnp.where(less, each, index)
        best = jnp.minimum(best, length_ref[each])
    return index


def sort_kernel(length_ref, query_ref, long_ref, apart_ref, held_ref, sems):
    apart = shortest(length_ref)
    most = long_ref.shape[0]
    stages = []
    for place in range(most + 1):
        if place < most:
            request, target = place + (place >= apart).astype(jnp.int32), long_ref.at[place]
        else:
            request, target = apart, apart_ref.at[0]
        held = held_ref.at[place]
        stages.append(
            (
                pltpu.make_async_copy(query_ref.at[request], held, sems.at[place, 0]),
                pltpu.make_async_copy(held, target, sems.at[place, 1]),
            )
        )
    for fetch, _ in stages:
        fetch.start()
    for fetch, put in stages:
        fetch.wait()
        put.start()
    for _, put in stages:
        put.wait()


def rope_pieces(half, width):
    return [(low, min(width, half - low)) for low in range(0, half, width)]


def pack_kernel(place_ref, length_ref, lat_ref, rope_ref, out_ref, sems):
    apart = shortest(length_ref)
    half = lat_ref.shape[1] // 2
    dim_rope = rope_ref.shape[1]
    width = lat_ref.shape[2]
    low = pl.multiple_of(place_ref[1] * half, 128)
    copies = [
        pltpu.make_async_copy(
            lat_ref.at[apart, pl.ds(low, half), :], out_ref.at[pl.ds(0, half), :], sems.at[0]
        )
    ]
    for index, (at, size) in enumerate(rope_pieces(half, width)):
        copies.append(
            pltpu.make_async_copy(
                rope_ref.at[apart, :, pl.ds(pl.multiple_of(low + at, 128), size)],
                out_ref.at[pl.ds(half + index * dim_rope, dim_rope), pl.ds(0, size)],
                sems.at[index + 1],
            )
        )
    for copy in copies:
        copy.start()
    for copy in copies:
        copy.wait()


def variants(keys, block_count, block, action):
    step = 2 if block_count % 2 == 0 else 1
    for blocks in range(step, block_count + 1, step):

        @pl.when((keys > (blocks - step) * block) & (keys <= blocks * block))
        def _():
            action(blocks)


def spans(place, nodes):
    if isinstance(place, int):
        return slice(place * nodes, (place + 1) * nodes), slice(place, place + 1)
    return pl.ds(pl.multiple_of(place * nodes, nodes), nodes), pl.ds(place, 1)


def store_value(rows_ref, level_ref, lane, place, nodes, summed, total, top):
    heads, _, dim_lat = rows_ref.shape[1:]
    span, line = spans(place, nodes)
    normed = (summed * (1.0 / total)).astype(jnp.bfloat16)
    rows_ref[lane, :, span, :] = normed.T.reshape(heads, nodes, dim_lat)
    level_ref[lane, line, :] = top + jnp.log(total)


def store_nothing(rows_ref, level_ref, lane, place, nodes):
    heads, _, dim_lat = rows_ref.shape[1:]
    span, line = spans(place, nodes)
    rows_ref[lane, :, span, :] = jnp.zeros((heads, nodes, dim_lat), jnp.bfloat16)
    level_ref[lane, line, :] = jnp.full((1, level_ref.shape[2]), NEGATIVE, jnp.float32)


def project(rows_ref, level_ref, weight_ref, lane, count, nodes, out_ref, stat_ref=None):
    heads = rows_ref.shape[1]
    columns, dim_value = level_ref.shape[2], weight_ref.shape[3]
    for head in range(heads):
        value = dot_nn(rows_ref[lane, head], weight_ref[lane, head])
        for each in range(count):
            piece = value[each * nodes : (each + 1) * nodes].astype(out_ref.dtype)
            out_ref[each, head * nodes : (head + 1) * nodes, :] = piece
    if stat_ref is not None:
        stat_ref[...] = level_ref[lane]
        return
    for each in range(count):
        out_ref[each, columns:, :] = level_rows(level_ref[lane, each : each + 1, :], dim_value)


def page_kernel(steps, own, block, scale, place_ref, length_ref, start_ref, *refs):
    refs = list(refs)
    query_hbm = [[refs.pop(0) for _ in group] for group in steps]
    if own:
        apart_hbm = refs.pop(0)
    lat_hbm, rope_hbm, weight_hbm = refs.pop(0), refs.pop(0), refs.pop(0)
    if own:
        tree_ref, parent_ref, part_ref, stat_ref = [refs.pop(0) for _ in range(4)]
        out_refs = [part_ref]
    else:
        out_refs = [refs.pop(0) for _ in steps]
    query_ref, lat_ref, rope_ref, weight_ref, rows_ref, level_ref, score_ref, reach_ref = refs[:8]
    page_sems, query_sems, weight_sems = refs[8:]
    page_rows = lat_ref.shape[1]
    book = Book(place_ref, length_ref, start_ref, page_rows)
    heads, columns = weight_ref.shape[1], level_ref.shape[2]
    nodes = columns // heads
    lanes = len(steps)
    count = book.count - (0 if own else 1)
    block_count = page_rows // block

    flags = []
    shards = []
    exist = []
    for group in steps:
        flag = shard = jnp.int32(0)
        each = []
        for step in group:
            there = book.position + step
            exists = ((there >= 0) & (there < book.size)).astype(jnp.int32)
            each.append(exists)
            flag = flag + exists
            shard = shard + exists * there
        flags.append(flag)
        shards.append(shard)
        exist.append(each)
    any_flag = jnp.minimum(functools.reduce(jnp.add, flags), 1)

    def keys_at(place):
        request = book.request(place)
        keys = book.live(request, book.position) * any_flag
        if own:
            keys = keys * jnp.where(place == count - 1, book.hub, 1)
        return request, keys

    def page_copies(place, request):
        return [
            pltpu.make_async_copy(lat_hbm.at[request], lat_ref.at[place], page_sems.at[place, 0]),
            pltpu.make_async_copy(rope_hbm.at[request], rope_ref.at[place], page_sems.at[place, 1]),
        ]

    def query_copy(ref, place, lane):
        target = query_ref.at[place, :, lane * columns : (lane + 1) * columns]
        return pltpu.make_async_copy(ref, target, query_sems.at[place, lane])

    def weight_copy(lane):
        low = pl.multiple_of(shards[lane] * heads, heads)
        return pltpu.make_async_copy(
            weight_hbm.at[pl.ds(low, heads)], weight_ref.at[lane], weight_sems.at[lane]
        )

    for place in range(count):
        request, keys = keys_at(jnp.int32(place))
        for lane, group in enumerate(query_hbm):
            for ref, exists in zip(group, exist[lane]):
                source = apart_hbm.at[0] if own and place == count - 1 else ref.at[place]

                @pl.when(exists * (keys + int(own)) > 0)
                def _():
                    query_copy(source, place, lane).start()

        @pl.when(keys > 0)
        def _():
            for copy in page_copies(place, request):
                copy.start()

    for lane in range(lanes):

        @pl.when(flags[lane] > 0)
        def _():
            weight_copy(lane).start()

    if own:
        reached = reach_closure(parent_ref[...])
        for _ in range(max(nodes - 1, 1).bit_length()):
            reached = jnp.minimum(dot_nn(reached, reached), 1.0).astype(jnp.bfloat16)
        reach_ref[...] = reached.astype(jnp.float32)

    def item_step(place, carry):
        request, keys = keys_at(place)
        for lane, group in enumerate(query_hbm):

            @pl.when(flags[lane] * (keys + int(own)) > 0)
            def _():
                query_copy(group[0].at[0], place, lane).wait()

        @pl.when(keys > 0)
        def _():
            for copy in page_copies(place, request):
                copy.wait()

        def attend(blocks, query):
            tree = None
            if own:
                base = pl.multiple_of(request * nodes, nodes)
                row = lax.broadcasted_iota(jnp.int32, (reach_ref.shape[1], columns), 0)
                along = lax.broadcasted_iota(jnp.int32, (reach_ref.shape[1], columns), 1)
                pick = jnp.where(row == base + along % nodes, 1.0, 0.0).astype(jnp.bfloat16)
                near = reach_ref[pl.ds(base, nodes), :].astype(jnp.bfloat16)
                tree = (tree_ref[request], dot_nn(near, pick))
            return page_softmax(
                query, lat_ref, rope_ref, place, keys, blocks, block, scale, score_ref, tree
            )

        def attend_one(lane):
            def action(blocks):
                if isinstance(lane, int):
                    query = query_ref[place, :, lane * columns : (lane + 1) * columns]
                else:
                    query = query_ref[place, :, pl.ds(pl.multiple_of(lane * columns, columns), columns)]
                store_value(rows_ref, level_ref, lane, place, nodes, *attend(blocks, query))

            return action

        def attend_all(blocks):
            summed, total, top = attend(blocks, query_ref[place])
            for lane in range(lanes):
                span = slice(lane * columns, (lane + 1) * columns)
                store_value(
                    rows_ref, level_ref, lane, place, nodes, summed[:, span], total[:, span], top[:, span]
                )

        if lanes == 1:
            variants(keys, block_count, block, attend_one(0))
        else:
            together = functools.reduce(jnp.multiply, flags)
            alone = functools.reduce(
                jnp.add, [lane * flag for lane, flag in enumerate(flags)]
            ) * (1 - together)
            variants(keys * together, block_count, block, attend_all)
            variants(keys * (1 - together), block_count, block, attend_one(alone))

        @pl.when(keys <= 0)
        def _():
            if own:
                attend_one(0)(0)
            else:
                for lane in range(lanes):
                    store_nothing(rows_ref, level_ref, lane, place, nodes)

        return carry

    lax.fori_loop(0, count * any_flag, item_step, 0)
    for lane in range(lanes):

        @pl.when(flags[lane] > 0)
        def _():
            weight_copy(lane).wait()
            project(
                rows_ref, level_ref, weight_ref, lane, count, nodes, out_refs[lane],
                stat_ref if own else None,
            )


def hub_kernel(block, scale, place_ref, length_ref, start_ref, *refs):
    refs = list(refs)
    query_hbm = [refs.pop(0) for _ in range(4)]
    mine_hbm, other_hbm, lat_hbm, rope_hbm, weight_hbm = [refs.pop(0) for _ in range(5)]
    held_hbm = [refs.pop(0) for _ in range(3)]
    out_refs = [refs.pop(0) for _ in range(3)]
    part_ref, stat_ref = refs.pop(0), refs.pop(0)
    query_ref, lat_ref, rope_ref, weight_ref, rows_ref, level_ref, score_ref = refs[:7]
    sum_ref, acc_ref, held_sems, query_sems, page_sems, end_sems, weight_sems = refs[7:]
    page_rows, dim_lat = lat_ref.shape[1:]
    dim_rope = rope_ref.shape[1]
    book = Book(place_ref, length_ref, start_ref, page_rows)
    heads, columns = weight_ref.shape[1], level_ref.shape[2]
    nodes = columns // heads
    half = page_rows // 2
    block_count = page_rows // block
    request = book.apart
    low_side = book.position * 2 < book.size
    end = jnp.where(low_side, 0, book.size - 1)
    far = jnp.where(low_side, book.position + 2, book.position - 2)
    shards = [book.position - 1, book.position + 1, far, book.position]
    live = [book.live(request, book.position), book.live(request, end)]

    held_copies = [
        pltpu.make_async_copy(held, out.at[pl.ds(0, held.shape[0])], held_sems.at[index])
        for index, (held, out) in enumerate(zip(held_hbm, out_refs))
    ]
    for copy in held_copies:
        copy.start()

    @pl.when(book.hub == 0)
    def _():
        for out_ref in out_refs:
            last = out_ref.shape[0] - 1
            out_ref[last, :columns, :] = jnp.zeros((columns, out_ref.shape[2]), out_ref.dtype)
            nothing = jnp.full((1, columns), NEGATIVE, jnp.float32)
            out_ref[last, columns:, :] = level_rows(nothing, out_ref.shape[2])
        part_ref[...] = jnp.zeros_like(part_ref)
        stat_ref[...] = jnp.full_like(stat_ref, NEGATIVE)

    @pl.when(book.hub > 0)
    def _():
        copies = [
            pltpu.make_async_copy(
                ref.at[0],
                query_ref.at[lane // 2, :, lane % 2 * columns : (lane % 2 + 1) * columns],
                query_sems.at[lane],
            )
            for lane, ref in enumerate(query_hbm)
        ]
        copies.append(pltpu.make_async_copy(lat_hbm.at[request], lat_ref.at[0], page_sems.at[0]))
        copies.append(pltpu.make_async_copy(rope_hbm.at[request], rope_ref.at[0], page_sems.at[1]))
        at_sem = 0
        for ref, part in ((mine_hbm, book.half), (other_hbm, 1 - book.half)):
            low = pl.multiple_of(part * half, 128)
            copies.append(
                pltpu.make_async_copy(
                    ref.at[pl.ds(0, half), :], lat_ref.at[1, pl.ds(low, half), :], end_sems.at[at_sem]
                )
            )
            at_sem += 1
            for index, (at, size) in enumerate(rope_pieces(half, dim_lat)):
                copies.append(
                    pltpu.make_async_copy(
                        ref.at[pl.ds(half + index * dim_rope, dim_rope), pl.ds(0, size)],
                        rope_ref.at[1, :, pl.ds(pl.multiple_of(low + at, 128), size)],
                        end_sems.at[at_sem],
                    )
                )
                at_sem += 1
        weight_copies = [
            pltpu.make_async_copy(
                weight_hbm.at[pl.ds(pl.multiple_of(shard * heads, heads), heads)],
                weight_ref.at[lane],
                weight_sems.at[lane],
            )
            for lane, shard in enumerate(shards)
        ]
        for copy in copies + weight_copies:
            copy.start()
        for copy in copies:
            copy.wait()

        def group_step(item, carry):
            group, page = lax.div(item, 2), lax.rem(item, 2)
            keys = jnp.where(page == 0, live[0], live[1])
            narrow = (group == 1) & (page == 0)

            @pl.when(page == 0)
            def _():
                sum_ref[0:1, :] = jnp.zeros((1, 2 * columns), jnp.float32)
                sum_ref[1:2, :] = jnp.full((1, 2 * columns), NEGATIVE, jnp.float32)
                acc_ref[...] = jnp.zeros_like(acc_ref)

            def attend(width):
                def action(blocks):
                    summed, total, top = page_softmax(
                        query_ref[group, :, :width], lat_ref, rope_ref, page, keys, blocks, block, scale,
                        score_ref, None,
                    )
                    old_top = sum_ref[1:2, :width]
                    new_top = jnp.maximum(old_top, top)
                    old_share, new_share = jnp.exp(old_top - new_top), jnp.exp(top - new_top)
                    sum_ref[0:1, :width] = sum_ref[0:1, :width] * old_share + total * new_share
                    sum_ref[1:2, :width] = new_top
                    acc_ref[:, :width] = acc_ref[:, :width] * old_share + summed * new_share

                return action

            variants(jnp.where(narrow, 0, keys), block_count, block, attend(2 * columns))
            variants(jnp.where(narrow, keys, 0), block_count, block, attend(columns))

            @pl.when(page == 1)
            def _():
                for side in range(2):
                    lane = group * 2 + side
                    span = slice(side * columns, (side + 1) * columns)
                    some = live[1] + (live[0] if side == 0 else jnp.where(group == 1, 0, live[0]))

                    @pl.when(some > 0)
                    def _():
                        outcome = acc_ref[:, span], sum_ref[0:1, span], sum_ref[1:2, span]
                        store_value(rows_ref, level_ref, lane, 0, nodes, *outcome)

                    @pl.when(some <= 0)
                    def _():
                        store_nothing(rows_ref, level_ref, lane, 0, nodes)

            return carry

        lax.fori_loop(0, 4, group_step, 0)
        for copy in weight_copies:
            copy.wait()
        for lane, out_ref in enumerate(out_refs):
            last = out_ref.shape[0] - 1
            project(rows_ref, level_ref, weight_ref, lane, 1, nodes, out_ref.at[last : last + 1])
        project(rows_ref, level_ref, weight_ref, 3, 1, nodes, part_ref, stat_ref)

    for copy in held_copies:
        copy.wait()


def level_rows(level, lanes):
    pieces = []
    rest = level
    for _ in range(3):
        piece = rest.astype(jnp.bfloat16).astype(jnp.float32)
        rest = rest - piece
        pieces.append(piece)
    rows = [
        piece[:, first : first + lanes] for piece in pieces for first in range(0, level.shape[1], lanes)
    ]
    rows.append(jnp.zeros((STAT_ROWS - len(rows), lanes), jnp.float32))
    return jnp.concatenate(rows, axis=0).astype(jnp.bfloat16)


def level_row(block, columns):
    per = columns // block.shape[1]
    block = block.astype(jnp.float32)
    return jnp.concatenate(
        [block[i : i + 1] + block[per + i : per + i + 1] + block[2 * per + i : 2 * per + i + 1] for i in range(per)],
        axis=1,
    )


def merge_kernel(layout, heads, place_ref, length_ref, start_ref, part_ref, stat_ref, live_ref,
                 apart_ref, apart_stat_ref, *refs):
    book = Book(place_ref, length_ref, start_ref, 1)
    request_count, columns, dim_value = part_ref.shape
    nodes = columns // heads
    remote_refs, out_ref = refs[: len(layout)], refs[len(layout)]
    nothing = jnp.full((1, columns), NEGATIVE, jnp.float32)
    requests = [book.request(jnp.int32(place)) for place in range(request_count)]
    levels = [stat_ref[...]]
    for steps, ref in zip(layout, remote_refs):
        held = ref.shape[0]
        level = jnp.concatenate(
            [level_row(ref[each, columns:, :], columns) for each in range(held)]
            + [nothing] * (request_count - held),
            axis=0,
        )
        exists = functools.reduce(
            jnp.logical_or,
            [(book.position + step >= 0) & (book.position + step < book.size) for step in steps],
        )
        levels.append(jnp.where(exists, level, NEGATIVE))
    levels.append(jnp.concatenate([nothing] * (request_count - 1) + [apart_stat_ref[...]], axis=0))
    top = functools.reduce(jnp.maximum, levels)
    weights = [jnp.exp(level - top) for level in levels]
    keep = jnp.concatenate([live_ref[pl.ds(request, 1), :] for request in requests], axis=0)
    total = keep / functools.reduce(jnp.add, weights)
    stacked = [weight * total for weight in weights]
    filler = -len(stacked) * request_count % 8
    if filler:
        stacked.append(jnp.zeros((filler, columns), jnp.float32))
    shares = jnp.concatenate(stacked, axis=0).T
    for place in range(request_count):
        value = part_ref[place] * shares[:, place : place + 1]
        for index, ref in enumerate(remote_refs):
            if place >= ref.shape[0]:
                continue
            at = (index + 1) * request_count + place
            value = value + ref[place, :columns, :].astype(jnp.float32) * shares[:, at : at + 1]
        if place == request_count - 1:
            at = (len(layout) + 1) * request_count + place
            value = value + apart_ref[0] * shares[:, at : at + 1]
        for head in range(heads):
            rows = value[head * nodes : (head + 1) * nodes].astype(jnp.bfloat16)
            out_ref[requests[place], :, head * dim_value : (head + 1) * dim_value] = rows


VMEM = pl.BlockSpec(memory_space=pltpu.VMEM)
SMEM = pl.BlockSpec(memory_space=pltpu.SMEM)
HBM = pl.BlockSpec(memory_space=pltpu.HBM)
VMEM_LIMIT = 57 << 20


def call(kernel, name, operands, out_shapes, scratch, flops=0, limit=VMEM_LIMIT, out_space=VMEM):
    return pl.pallas_call(
        kernel,
        in_specs=[spec for spec, _ in operands],
        out_specs=[out_space] * len(out_shapes),
        scratch_shapes=scratch,
        out_shape=[jax.ShapeDtypeStruct(shape, dtype) for shape, dtype in out_shapes],
        compiler_params=pltpu.CompilerParams(vmem_limit_bytes=limit),
        cost_estimate=pl.CostEstimate(flops=flops, bytes_accessed=flops // 256, transcendentals=0),
        name=name,
    )(*[array for _, array in operands])


def after(value, *others):
    return lax.optimization_barrier((value, *others))[0]


def hub_shards(
    queries,
    tree_keys,
    parents,
    node_live,
    lengths,
    start_device,
    cache_latent,
    cache_rope,
    up_weight,
):
    size = lax.axis_size("blk")
    head_size = lax.axis_size("head")
    request_count, width, columns = queries.shape
    page_rows, dim_lat = cache_latent.shape[1:]
    dim_rope = cache_rope.shape[1]
    dim_value = up_weight.shape[2]
    heads = up_weight.shape[0] // size
    nodes = columns // heads
    rows = columns + STAT_ROWS
    block = math.gcd(page_rows, 256)
    scale = 1.0 / math.sqrt(DN + dim_rope)
    most = request_count - 1
    bf16, f32 = jnp.bfloat16, jnp.float32
    dma = pltpu.SemaphoreType.DMA
    position = lax.axis_index("blk")
    here = jnp.stack([position, lax.axis_index("head") % 2, jnp.int32(size)]).astype(jnp.int32)
    scalars = [(SMEM, here), (SMEM, lengths), (SMEM, start_device)]
    pages = [(HBM, cache_latent), (HBM, cache_rope), (HBM, up_weight)]
    unit_flops = 2 * columns * page_rows * (width + dim_lat)

    long, apart = call(
        sort_kernel,
        "sort_queries",
        [(SMEM, lengths), (HBM, queries)],
        [((most, width, columns), bf16), ((1, width, columns), bf16)],
        [pltpu.VMEM((request_count, width, columns), bf16), dma((request_count, 2))],
        out_space=HBM,
    )
    half = page_rows // 2
    pieces = rope_pieces(half, dim_lat)

    def answer(name, steps, query_groups, own=()):
        lanes = len(steps)
        count = request_count if own else most
        operands = scalars + [(HBM, query) for group in query_groups for query in group]
        if own:
            operands += [(HBM, own[0])]
        operands += pages
        if own:
            operands += [(VMEM, array) for array in own[1:]]
            outs = [((count, columns, dim_value), f32), ((count, columns), f32)]
        else:
            outs = [((count, rows, dim_value), bf16)] * lanes
        reach_size = request_count * nodes if own else 8
        return call(
            functools.partial(page_kernel, steps, bool(own), block, scale),
            name,
            operands,
            outs,
            [
                pltpu.VMEM((count, width, lanes * columns), bf16),
                pltpu.VMEM((count, page_rows, dim_lat), bf16),
                pltpu.VMEM((count, dim_rope, page_rows), bf16),
                pltpu.VMEM((lanes, heads, dim_lat, dim_value), bf16),
                pltpu.VMEM((lanes, heads, count * nodes, dim_lat), bf16),
                pltpu.VMEM((lanes, count, columns), f32),
                pltpu.VMEM((page_rows, lanes * columns), f32),
                pltpu.VMEM((reach_size, reach_size), f32),
                dma((count, 2)),
                dma((count, lanes)),
                dma((lanes,)),
            ],
            unit_flops * lanes * count,
        )

    def shift(value, pairs):
        return lax.ppermute(value, "blk", pairs)

    right1 = shift(long, [(i, i + 1) for i in range(size - 1)])
    left1 = shift(long, [(i, i - 1) for i in range(1, size)])
    apart_right = shift(apart, [(i, i + 1) for i in range(size - 2)])
    apart_left = shift(apart, [(i, i - 1) for i in range(2, size)])
    parent_row = (parents + nodes * jnp.arange(request_count, dtype=jnp.int32)[:, None]).reshape(1, -1)
    live_rows = jnp.tile(node_live.astype(f32), (1, heads))
    part, stat = answer("own_pages", [[0]], [[long]], (apart, tree_keys, parent_row))
    right2 = shift(after(right1, part), [(i, i + 1) for i in range(1, size - 1)])
    left2 = shift(after(left1, part), [(i, i - 1) for i in range(1, size - 1)])
    (packed,) = call(
        pack_kernel,
        "pack_page",
        [(SMEM, here), (SMEM, lengths), (HBM, cache_latent), (HBM, cache_rope)],
        [((half + len(pieces) * dim_rope, dim_lat), bf16)],
        [dma((1 + len(pieces),))],
    )
    mine = shift(packed, [(0, 1), (size - 1, size - 2)])
    first = answer("first_hop", [[-1], [1]], [[after(right1, apart_right, apart_left)], [left1]])
    swapped = lax.ppermute(
        after(mine, *first),
        ("blk", "head"),
        [(i * head_size + j, i * head_size + (j ^ 1)) for i in (1, size - 2) for j in range(head_size)],
    )
    crossing = jnp.where(position * 2 < size, apart_right, apart_left)
    apart_far = shift(after(crossing, *first), [(1, size - 2), (size - 2, 1)])
    right3 = shift(after(right2, *first), [(size - 2, size - 1)])
    left3 = shift(after(left2, *first), [(1, 0)])
    (second,) = answer("second_hop", [[-2, 2]], [[right2, left2]])
    to_left, to_right, to_far, apart_part, apart_stat = call(
        functools.partial(hub_kernel, block, scale),
        "hub_pages",
        scalars
        + [(HBM, array) for array in (apart_right, apart_left, apart_far, apart, mine, swapped)]
        + pages
        + [(HBM, array) for array in (*first, second)],
        [((request_count, rows, dim_value), bf16)] * 3
        + [((1, columns, dim_value), f32), ((1, columns), f32)],
        [
            pltpu.VMEM((2, width, 2 * columns), bf16),
            pltpu.VMEM((2, page_rows, dim_lat), bf16),
            pltpu.VMEM((2, dim_rope, page_rows), bf16),
            pltpu.VMEM((4, heads, dim_lat, dim_value), bf16),
            pltpu.VMEM((4, heads, nodes, dim_lat), bf16),
            pltpu.VMEM((4, 1, columns), f32),
            pltpu.VMEM((page_rows, 2 * columns), f32),
            pltpu.VMEM((8, 2 * columns), f32),
            pltpu.VMEM((dim_lat, 2 * columns), f32),
            dma((3,)),
            dma((4,)),
            dma((2,)),
            dma((2 * (1 + len(pieces)),)),
            dma((4,)),
        ],
        unit_flops * 7,
    )
    (third,) = answer(
        "third_hop", [[1 - size, size - 1]], [[after(right3, to_far), left3]]
    )
    to_left, to_right, to_far = (after(value, third) for value in (to_left, to_right, to_far))
    from_right = shift(to_left, [(i, i - 1) for i in range(1, size)])
    from_left = shift(to_right, [(i, i + 1) for i in range(size - 1)])
    from_far = shift(to_far, [(i, i - 2) for i in range(2, size)] + [(i, i + 2) for i in range(size - 2)])
    from_end = shift(third, [(0, size - 1), (size - 1, 0)])
    (verified,) = call(
        functools.partial(merge_kernel, [[1], [-1], [-2, 2], [1 - size, size - 1]], heads),
        "merge_parts",
        scalars
        + [
            (VMEM, array)
            for array in (
                part, stat, live_rows, apart_part, apart_stat, from_right, from_left, from_far, from_end
            )
        ],
        [((request_count, nodes, heads * dim_value), bf16)],
        [],
        limit=12 << 20,
    )
    return verified


def solution(mesh):
    size = mesh.shape["blk"]
    even = mesh.shape["head"] % 2 == 0

    def shards(queries, *rest):
        columns = queries.shape[2]
        cache_latent, _, up_weight = rest[-3:]
        wide = columns % up_weight.shape[2] == 0 and cache_latent.shape[1] % 256 == 0
        plan = hub_shards if wide and size == 4 and even and queries.shape[0] > 1 else gathered_shards
        return plan(queries, *rest)

    return jax.shard_map(
        shards,
        mesh=mesh,
        in_specs=(
            P("grp", None, ("head", "blk")),
            P("grp", None, None),
            P("grp", None),
            P("grp", None),
            P("grp"),
            P("grp"),
            P("grp", "blk", None),
            P("grp", None, "blk"),
            P("head", None, None),
        ),
        out_specs=P("grp", None, ("head", "blk")),
        check_vma=False,
    )
```

```python
import functools
import math

import jax
import jax.numpy as jnp
from jax import lax
from jax.experimental import pallas as pl
from jax.experimental.pallas import tpu as pltpu
from jax.sharding import PartitionSpec as P

DN = 128

NEGATIVE = -1e30
STAT_ROWS = 16


def merged(value, axis, join):
    pieces = jax.tree.map(lambda part: lax.all_gather(part, axis), value)
    head = jax.tree.map(lambda part: part[0], pieces)
    tail = jax.tree.map(lambda part: part[1:], pieces)
    subtotal, _ = lax.scan(lambda subtotal, slab: (join(subtotal, slab), None), head, tail)
    return subtotal


def ancestor_matrix(parent_list):
    node_count = parent_list.shape[0]
    ordering = jnp.arange(node_count, dtype=jnp.int32)
    one_hop = (parent_list[:, None] == ordering[None, :]).astype(jnp.float32)
    reached = jnp.maximum(one_hop, jnp.eye(node_count, dtype=jnp.float32))
    for _ in range(max(node_count - 1, 1).bit_length()):
        reached = jnp.minimum(jnp.dot(reached, reached, precision=lax.Precision.HIGHEST), 1.0)
    return reached


def softmax_update(running, scores, visible, values):
    top_score, weight_sum, summed = running
    masked = jnp.where(visible, scores, -jnp.inf)
    new_top = jnp.maximum(top_score, jnp.max(masked, axis=1))
    factor = jnp.exp(top_score - new_top)
    expweights = jnp.exp(masked - new_top[:, None])
    summed = summed * factor[:, None] + jnp.dot(
        expweights.astype(jnp.bfloat16), values, preferred_element_type=jnp.float32
    )
    return (new_top, weight_sum * factor + jnp.sum(expweights, axis=1), summed)


def join_stats(first_stats, second_stats):
    top_one, sum_one = first_stats
    top_two, sum_two = second_stats
    top_both = jnp.maximum(top_one, top_two)
    return (top_both, sum_one * jnp.exp(top_one - top_both) + sum_two * jnp.exp(top_two - top_both))


def attend_page(running, query_block, lat_page, rope_page, live_count, score_scale):
    dim_lat = lat_page.shape[1]
    query_lat = query_block[:dim_lat]
    query_rope = query_block[dim_lat:]
    key_block = math.gcd(lat_page.shape[0], 512)

    def block_step(block_index, carried):
        first_key = block_index * key_block
        lat_rows = lax.dynamic_slice_in_dim(lat_page, first_key, key_block, 0)
        rope_rows = lax.dynamic_slice_in_dim(rope_page, first_key, key_block, 1)
        scores = lax.dot_general(
            query_lat, lat_rows, (((0,), (1,)), ((), ())), preferred_element_type=jnp.float32
        )
        scores = scores + lax.dot_general(
            query_rope, rope_rows, (((0,), (0,)), ((), ())), preferred_element_type=jnp.float32
        )
        scores = scores * score_scale
        visible = first_key + jnp.arange(key_block, dtype=jnp.int32) < live_count
        return softmax_update(carried, scores, visible[None, :], lat_rows)

    block_count = (live_count + key_block - 1) // key_block
    return lax.fori_loop(0, block_count, block_step, running)


def fresh_state(columns, dim_lat):
    return (
        jnp.full((columns,), NEGATIVE, jnp.float32),
        jnp.zeros((columns,), jnp.float32),
        jnp.zeros((columns, dim_lat), jnp.float32),
    )


def gathered_shards(
    queries,
    tree_keys,
    parents,
    node_live,
    lengths,
    start_device,
    cache_latent,
    cache_rope,
    up_weight,
):
    cycle_size = lax.axis_size("blk")
    position = lax.axis_index("blk")
    request_count = queries.shape[0]
    local_cols = queries.shape[2]
    node_count = tree_keys.shape[1]
    dim_lat = cache_latent.shape[2]
    dim_rope = cache_rope.shape[1]
    dim_value = up_weight.shape[2]
    page_rows = cache_latent.shape[1]
    own_heads = local_cols // node_count
    score_scale = 1.0 / math.sqrt(DN + dim_rope)
    page_index = (position - start_device) % cycle_size
    live_keys = jnp.clip(lengths - page_index * page_rows, 0, page_rows)
    piece = lax.all_gather(queries, "blk", axis=2, tiled=True)
    piece_cols = piece.shape[2]
    tops = []
    sums = []
    accs = []
    for fold_request in range(request_count):
        fold_outcome = attend_page(
            fresh_state(piece_cols, dim_lat),
            piece[fold_request],
            cache_latent[fold_request],
            cache_rope[fold_request],
            live_keys[fold_request],
            score_scale,
        )
        tops.append(fold_outcome[0])
        sums.append(fold_outcome[1])
        accs.append(fold_outcome[2])
    top_all = jnp.stack(tops)
    sum_all = jnp.stack(sums)
    acc_all = jnp.stack(accs)
    reached = jax.vmap(ancestor_matrix)(parents) > 0.5
    tree_tops, tree_sums, tree_accs = ([], [], [])
    for request in range(request_count):
        tree_scores = (
            lax.dot_general(
                queries[request],
                tree_keys[request],
                (((0,), (1,)), ((), ())),
                preferred_element_type=jnp.float32,
            )
            * score_scale
        )
        visible = jnp.tile(reached[request], (own_heads, 1))
        outcome = softmax_update(
            fresh_state(local_cols, dim_lat), tree_scores, visible, tree_keys[request][:, :dim_lat]
        )
        tree_tops.append(outcome[0])
        tree_sums.append(outcome[1])
        tree_accs.append(outcome[2])
    tree_top = jnp.stack(tree_tops)
    tree_sum = jnp.stack(tree_sums)
    tree_acc = jnp.stack(tree_accs)
    own_start = position * local_cols
    own_top = lax.dynamic_slice_in_dim(top_all, own_start, local_cols, 1)
    own_sum = lax.dynamic_slice_in_dim(sum_all, own_start, local_cols, 1)
    own_acc = lax.dynamic_slice_in_dim(acc_all, own_start, local_cols, 1)
    joined = jnp.maximum(own_top, tree_top)
    first_factor = jnp.exp(own_top - joined)
    second_factor = jnp.exp(tree_top - joined)
    top_all = lax.dynamic_update_slice_in_dim(top_all, joined, own_start, 1)
    sum_all = lax.dynamic_update_slice_in_dim(
        sum_all, own_sum * first_factor + tree_sum * second_factor, own_start, 1
    )
    acc_all = lax.dynamic_update_slice_in_dim(
        acc_all,
        own_acc * first_factor[:, :, None] + tree_acc * second_factor[:, :, None],
        own_start,
        1,
    )
    merged_top, merged_sum = merged((top_all, sum_all), "blk", join_stats)
    scaling = jnp.exp(top_all - merged_top) / merged_sum
    normed = acc_all * scaling[:, :, None]
    head_rows = lax.psum_scatter(
        normed.astype(jnp.bfloat16), "blk", scatter_dimension=1, tiled=True
    ).astype(jnp.float32)
    weight_own = lax.dynamic_slice_in_dim(up_weight, position * own_heads, own_heads, 0).astype(
        jnp.float32
    )
    projected = jnp.einsum(
        "rhnd,hdv->rnhv",
        head_rows.reshape(request_count, own_heads, node_count, dim_lat),
        weight_own,
        precision=lax.Precision.HIGHEST,
    )
    verified = projected.reshape(request_count, node_count, own_heads * dim_value)
    live_nodes = node_live.astype(jnp.float32)[:, :, None]
    return (verified * live_nodes).astype(jnp.bfloat16)


def dot_nn(left, right):
    return jnp.dot(left, right, preferred_element_type=jnp.float32)


def dot_tn(left, right):
    return lax.dot_general(
        left, right, (((0,), (0,)), ((), ())), preferred_element_type=jnp.float32
    )


def reach_closure(parent_row):
    count = parent_row.shape[1]
    row = lax.broadcasted_iota(jnp.int32, (count, count), 0)
    lane = lax.broadcasted_iota(jnp.int32, (count, count), 1)
    reached = jnp.where((row == parent_row) | (row == lane), 1.0, 0.0).astype(jnp.bfloat16)
    return reached


def page_softmax(query, lat_ref, rope_ref, page, keys, blocks, block, scale, score_ref, tree):
    dim_lat = lat_ref.shape[2]
    columns = query.shape[1]
    query_lat, query_rope = query[:dim_lat], query[dim_lat:]
    tops = []
    for index in range(blocks):
        span = slice(index * block, (index + 1) * block)
        scores = dot_nn(lat_ref[page, span, :], query_lat)
        scores = scores + dot_tn(rope_ref[page, :, span], query_rope)
        if index >= blocks - 2:
            place = index * block + lax.broadcasted_iota(jnp.int32, scores.shape, 0)
            scores = jnp.where(place < keys, scores, NEGATIVE)
        score_ref[span, :columns] = scores
        tops.append(jnp.max(scores, axis=0, keepdims=True))
    if tree is not None:
        tree_keys, visible = tree
        tree_scores = jnp.where(visible > 0.5, dot_nn(tree_keys, query), NEGATIVE)
        tops.append(jnp.max(tree_scores, axis=0, keepdims=True))
    top = functools.reduce(jnp.maximum, tops)
    base_two = scale * math.log2(math.e)
    shift = top * base_two
    total = summed = None
    for index in range(blocks):
        span = slice(index * block, (index + 1) * block)
        weights = jnp.exp2(score_ref[span, :columns] * base_two - shift)
        weight_sum = jnp.sum(weights, axis=0, keepdims=True)
        values = dot_tn(lat_ref[page, span, :], weights.astype(jnp.bfloat16))
        total = weight_sum if total is None else total + weight_sum
        summed = values if summed is None else summed + values
    if tree is not None:
        weights = jnp.exp2(tree_scores * base_two - shift)
        weight_sum = jnp.sum(weights, axis=0, keepdims=True)
        values = dot_tn(tree_keys[:, :dim_lat], weights.astype(jnp.bfloat16))
        total = weight_sum if total is None else total + weight_sum
        summed = values if summed is None else summed + values
    return summed, total, top * scale


class Book:
    def __init__(self, place_ref, length_ref, start_ref, page_rows):
        self.position, self.half = place_ref[0], place_ref[1]
        self.size = place_ref[2]
        self.lengths, self.starts = length_ref, start_ref
        self.page_rows = page_rows
        self.count = length_ref.shape[0]
        self.apart = shortest(length_ref)
        self.hub = ((self.position > 0) & (self.position < self.size - 1)).astype(jnp.int32)

    def request(self, place):
        moved = place + (place >= self.apart).astype(jnp.int32)
        return jnp.where(place == self.count - 1, self.apart, moved)

    def live(self, request, position):
        page = lax.rem(position - self.starts[request] + self.size, self.size)
        return jnp.clip(self.lengths[request] - page * self.page_rows, 0, self.page_rows)


def shortest(length_ref):
    best, index = length_ref[0], jnp.int32(0)
    for each in range(1, length_ref.shape[0]):
        less = length_ref[each] < best
        index = jnp.where(less, each, index)
        best = jnp.minimum(best, length_ref[each])
    return index


def sort_kernel(length_ref, query_ref, long_ref, apart_ref, held_ref, sems):
    apart = shortest(length_ref)
    most = long_ref.shape[0]
    stages = []
    for place in range(most + 1):
        if place < most:
            request, target = place + (place >= apart).astype(jnp.int32), long_ref.at[place]
        else:
            request, target = apart, apart_ref.at[0]
        held = held_ref.at[place]
        stages.append(
            (
                pltpu.make_async_copy(query_ref.at[request], held, sems.at[place, 0]),
                pltpu.make_async_copy(held, target, sems.at[place, 1]),
            )
        )
    for fetch, _ in stages:
        fetch.start()
    for fetch, put in stages:
        fetch.wait()
        put.start()
    for _, put in stages:
        put.wait()


def rope_pieces(half, width):
    return [(low, min(width, half - low)) for low in range(0, half, width)]


def pack_kernel(place_ref, length_ref, lat_ref, rope_ref, out_ref, sems):
    apart = shortest(length_ref)
    half = lat_ref.shape[1] // 2
    dim_rope = rope_ref.shape[1]
    width = lat_ref.shape[2]
    low = pl.multiple_of(place_ref[1] * half, 128)
    copies = [
        pltpu.make_async_copy(
            lat_ref.at[apart, pl.ds(low, half), :], out_ref.at[pl.ds(0, half), :], sems.at[0]
        )
    ]
    for index, (at, size) in enumerate(rope_pieces(half, width)):
        copies.append(
            pltpu.make_async_copy(
                rope_ref.at[apart, :, pl.ds(pl.multiple_of(low + at, 128), size)],
                out_ref.at[pl.ds(half + index * dim_rope, dim_rope), pl.ds(0, size)],
                sems.at[index + 1],
            )
        )
    for copy in copies:
        copy.start()
    for copy in copies:
        copy.wait()


def variants(keys, block_count, block, action):
    step = 2 if block_count % 2 == 0 else 1
    for blocks in range(step, block_count + 1, step):

        @pl.when((keys > (blocks - step) * block) & (keys <= blocks * block))
        def _():
            action(blocks)


def spans(place, nodes):
    if isinstance(place, int):
        return slice(place * nodes, (place + 1) * nodes), slice(place, place + 1)
    return pl.ds(pl.multiple_of(place * nodes, nodes), nodes), pl.ds(place, 1)


def store_value(rows_ref, level_ref, lane, place, nodes, summed, total, top):
    heads, _, dim_lat = rows_ref.shape[1:]
    span, line = spans(place, nodes)
    normed = (summed * (1.0 / total)).astype(jnp.bfloat16)
    rows_ref[lane, :, span, :] = normed.T.reshape(heads, nodes, dim_lat)
    level_ref[lane, line, :] = top + jnp.log(total)


def store_nothing(rows_ref, level_ref, lane, place, nodes):
    heads, _, dim_lat = rows_ref.shape[1:]
    span, line = spans(place, nodes)
    rows_ref[lane, :, span, :] = jnp.zeros((heads, nodes, dim_lat), jnp.bfloat16)
    level_ref[lane, line, :] = jnp.full((1, level_ref.shape[2]), NEGATIVE, jnp.float32)


def project(rows_ref, level_ref, weight_ref, lane, count, nodes, out_ref, stat_ref=None):
    heads = rows_ref.shape[1]
    columns, dim_value = level_ref.shape[2], weight_ref.shape[3]
    for head in range(heads):
        value = dot_nn(rows_ref[lane, head], weight_ref[lane, head])
        for each in range(count):
            piece = value[each * nodes : (each + 1) * nodes].astype(out_ref.dtype)
            out_ref[each, head * nodes : (head + 1) * nodes, :] = piece
    if stat_ref is not None:
        stat_ref[...] = level_ref[lane]
        return
    for each in range(count):
        out_ref[each, columns:, :] = level_rows(level_ref[lane, each : each + 1, :], dim_value)


def page_kernel(steps, own, block, scale, place_ref, length_ref, start_ref, *refs):
    refs = list(refs)
    query_hbm = [[refs.pop(0) for _ in group] for group in steps]
    if own:
        apart_hbm = refs.pop(0)
    lat_hbm, rope_hbm, weight_hbm = refs.pop(0), refs.pop(0), refs.pop(0)
    if own:
        tree_ref, parent_ref, part_ref, stat_ref = [refs.pop(0) for _ in range(4)]
        out_refs = [part_ref]
    else:
        out_refs = [refs.pop(0) for _ in steps]
    query_ref, lat_ref, rope_ref, weight_ref, rows_ref, level_ref, score_ref, reach_ref = refs[:8]
    page_sems, query_sems, weight_sems = refs[8:]
    page_rows = lat_ref.shape[1]
    book = Book(place_ref, length_ref, start_ref, page_rows)
    heads, columns = weight_ref.shape[1], level_ref.shape[2]
    nodes = columns // heads
    lanes = len(steps)
    count = book.count - (0 if own else 1)
    block_count = page_rows // block

    flags = []
    shards = []
    exist = []
    for group in steps:
        flag = shard = jnp.int32(0)
        each = []
        for step in group:
            there = book.position + step
            exists = ((there >= 0) & (there < book.size)).astype(jnp.int32)
            each.append(exists)
            flag = flag + exists
            shard = shard + exists * there
        flags.append(flag)
        shards.append(shard)
        exist.append(each)
    any_flag = jnp.minimum(functools.reduce(jnp.add, flags), 1)

    def keys_at(place):
        request = book.request(place)
        keys = book.live(request, book.position) * any_flag
        if own:
            keys = keys * jnp.where(place == count - 1, book.hub, 1)
        return request, keys

    def page_copies(place, request):
        return [
            pltpu.make_async_copy(lat_hbm.at[request], lat_ref.at[place], page_sems.at[place, 0]),
            pltpu.make_async_copy(rope_hbm.at[request], rope_ref.at[place], page_sems.at[place, 1]),
        ]

    def query_copy(ref, place, lane):
        target = query_ref.at[place, :, lane * columns : (lane + 1) * columns]
        return pltpu.make_async_copy(ref, target, query_sems.at[place, lane])

    def weight_copy(lane):
        low = pl.multiple_of(shards[lane] * heads, heads)
        return pltpu.make_async_copy(
            weight_hbm.at[pl.ds(low, heads)], weight_ref.at[lane], weight_sems.at[lane]
        )

    for place in range(count):
        request, keys = keys_at(jnp.int32(place))
        for lane, group in enumerate(query_hbm):
            for ref, exists in zip(group, exist[lane]):
                source = apart_hbm.at[0] if own and place == count - 1 else ref.at[place]

                @pl.when(exists * (keys + int(own)) > 0)
                def _():
                    query_copy(source, place, lane).start()

        @pl.when(keys > 0)
        def _():
            for copy in page_copies(place, request):
                copy.start()

    for lane in range(lanes):

        @pl.when(flags[lane] > 0)
        def _():
            weight_copy(lane).start()

    if own:
        reached = reach_closure(parent_ref[...])
        for _ in range(max(nodes - 1, 1).bit_length()):
            reached = jnp.minimum(dot_nn(reached, reached), 1.0).astype(jnp.bfloat16)
        reach_ref[...] = reached.astype(jnp.float32)

    def item_step(place, carry):
        request, keys = keys_at(place)
        for lane, group in enumerate(query_hbm):

            @pl.when(flags[lane] * (keys + int(own)) > 0)
            def _():
                query_copy(group[0].at[0], place, lane).wait()

        @pl.when(keys > 0)
        def _():
            for copy in page_copies(place, request):
                copy.wait()

        def attend(blocks, query):
            tree = None
            if own:
                base = pl.multiple_of(request * nodes, nodes)
                row = lax.broadcasted_iota(jnp.int32, (reach_ref.shape[1], columns), 0)
                along = lax.broadcasted_iota(jnp.int32, (reach_ref.shape[1], columns), 1)
                pick = jnp.where(row == base + along % nodes, 1.0, 0.0).astype(jnp.bfloat16)
                near = reach_ref[pl.ds(base, nodes), :].astype(jnp.bfloat16)
                tree = (tree_ref[request], dot_nn(near, pick))
            return page_softmax(
                query, lat_ref, rope_ref, place, keys, blocks, block, scale, score_ref, tree
            )

        def attend_one(lane):
            def action(blocks):
                if isinstance(lane, int):
                    query = query_ref[place, :, lane * columns : (lane + 1) * columns]
                else:
                    query = query_ref[place, :, pl.ds(pl.multiple_of(lane * columns, columns), columns)]
                store_value(rows_ref, level_ref, lane, place, nodes, *attend(blocks, query))

            return action

        def attend_all(blocks):
            summed, total, top = attend(blocks, query_ref[place])
            for lane in range(lanes):
                span = slice(lane * columns, (lane + 1) * columns)
                store_value(
                    rows_ref, level_ref, lane, place, nodes, summed[:, span], total[:, span], top[:, span]
                )

        if lanes == 1:
            variants(keys, block_count, block, attend_one(0))
        else:
            together = functools.reduce(jnp.multiply, flags)
            alone = functools.reduce(
                jnp.add, [lane * flag for lane, flag in enumerate(flags)]
            ) * (1 - together)
            variants(keys * together, block_count, block, attend_all)
            variants(keys * (1 - together), block_count, block, attend_one(alone))

        @pl.when(keys <= 0)
        def _():
            if own:
                attend_one(0)(0)
            else:
                for lane in range(lanes):
                    store_nothing(rows_ref, level_ref, lane, place, nodes)

        return carry

    lax.fori_loop(0, count * any_flag, item_step, 0)
    for lane in range(lanes):

        @pl.when(flags[lane] > 0)
        def _():
            weight_copy(lane).wait()
            project(
                rows_ref, level_ref, weight_ref, lane, count, nodes, out_refs[lane],
                stat_ref if own else None,
            )


def hub_kernel(block, scale, place_ref, length_ref, start_ref, *refs):
    refs = list(refs)
    query_hbm = [refs.pop(0) for _ in range(4)]
    mine_hbm, other_hbm, lat_hbm, rope_hbm, weight_hbm = [refs.pop(0) for _ in range(5)]
    out_refs = [refs.pop(0) for _ in range(3)]
    part_ref, stat_ref = refs.pop(0), refs.pop(0)
    query_ref, lat_ref, rope_ref, weight_ref, rows_ref, level_ref, score_ref = refs[:7]
    sum_ref, acc_ref, query_sems, page_sems, end_sems, weight_sems = refs[7:]
    page_rows, dim_lat = lat_ref.shape[1:]
    dim_rope = rope_ref.shape[1]
    book = Book(place_ref, length_ref, start_ref, page_rows)
    heads, columns = weight_ref.shape[1], level_ref.shape[2]
    nodes = columns // heads
    half = page_rows // 2
    block_count = page_rows // block
    request = book.apart
    low_side = book.position * 2 < book.size
    end = jnp.where(low_side, 0, book.size - 1)
    far = jnp.where(low_side, book.position + 2, book.position - 2)
    shards = [book.position - 1, book.position + 1, far, book.position]
    live = [book.live(request, book.position), book.live(request, end)]

    @pl.when(book.hub == 0)
    def _():
        nothing = level_rows(jnp.full((1, columns), NEGATIVE, jnp.float32), part_ref.shape[2])
        for out_ref in out_refs:
            out_ref[0, :columns, :] = jnp.zeros((columns, out_ref.shape[2]), out_ref.dtype)
            out_ref[0, columns:, :] = nothing
        part_ref[...] = jnp.zeros_like(part_ref)
        stat_ref[...] = jnp.full_like(stat_ref, NEGATIVE)

    @pl.when(book.hub > 0)
    def _():
        copies = [
            pltpu.make_async_copy(
                ref.at[0],
                query_ref.at[lane // 2, :, lane % 2 * columns : (lane % 2 + 1) * columns],
                query_sems.at[lane],
            )
            for lane, ref in enumerate(query_hbm)
        ]
        copies.append(pltpu.make_async_copy(lat_hbm.at[request], lat_ref.at[0], page_sems.at[0]))
        copies.append(pltpu.make_async_copy(rope_hbm.at[request], rope_ref.at[0], page_sems.at[1]))
        at_sem = 0
        for ref, part in ((mine_hbm, book.half), (other_hbm, 1 - book.half)):
            low = pl.multiple_of(part * half, 128)
            copies.append(
                pltpu.make_async_copy(
                    ref.at[pl.ds(0, half), :], lat_ref.at[1, pl.ds(low, half), :], end_sems.at[at_sem]
                )
            )
            at_sem += 1
            for index, (at, size) in enumerate(rope_pieces(half, dim_lat)):
                copies.append(
                    pltpu.make_async_copy(
                        ref.at[pl.ds(half + index * dim_rope, dim_rope), pl.ds(0, size)],
                        rope_ref.at[1, :, pl.ds(pl.multiple_of(low + at, 128), size)],
                        end_sems.at[at_sem],
                    )
                )
                at_sem += 1
        weight_copies = [
            pltpu.make_async_copy(
                weight_hbm.at[pl.ds(pl.multiple_of(shard * heads, heads), heads)],
                weight_ref.at[lane],
                weight_sems.at[lane],
            )
            for lane, shard in enumerate(shards)
        ]
        for copy in copies + weight_copies:
            copy.start()
        for copy in copies:
            copy.wait()

        def group_step(item, carry):
            group, page = lax.div(item, 2), lax.rem(item, 2)
            keys = jnp.where(page == 0, live[0], live[1])
            narrow = (group == 1) & (page == 0)

            @pl.when(page == 0)
            def _():
                sum_ref[0:1, :] = jnp.zeros((1, 2 * columns), jnp.float32)
                sum_ref[1:2, :] = jnp.full((1, 2 * columns), NEGATIVE, jnp.float32)
                acc_ref[...] = jnp.zeros_like(acc_ref)

            def attend(width):
                def action(blocks):
                    summed, total, top = page_softmax(
                        query_ref[group, :, :width], lat_ref, rope_ref, page, keys, blocks, block, scale,
                        score_ref, None,
                    )
                    old_top = sum_ref[1:2, :width]
                    new_top = jnp.maximum(old_top, top)
                    old_share, new_share = jnp.exp(old_top - new_top), jnp.exp(top - new_top)
                    sum_ref[0:1, :width] = sum_ref[0:1, :width] * old_share + total * new_share
                    sum_ref[1:2, :width] = new_top
                    acc_ref[:, :width] = acc_ref[:, :width] * old_share + summed * new_share

                return action

            variants(jnp.where(narrow, 0, keys), block_count, block, attend(2 * columns))
            variants(jnp.where(narrow, keys, 0), block_count, block, attend(columns))

            @pl.when(page == 1)
            def _():
                for side in range(2):
                    lane = group * 2 + side
                    span = slice(side * columns, (side + 1) * columns)
                    some = live[1] + (live[0] if side == 0 else jnp.where(group == 1, 0, live[0]))

                    @pl.when(some > 0)
                    def _():
                        outcome = acc_ref[:, span], sum_ref[0:1, span], sum_ref[1:2, span]
                        store_value(rows_ref, level_ref, lane, 0, nodes, *outcome)

                    @pl.when(some <= 0)
                    def _():
                        store_nothing(rows_ref, level_ref, lane, 0, nodes)

            return carry

        lax.fori_loop(0, 4, group_step, 0)
        for copy in weight_copies:
            copy.wait()
        outer = jnp.where(low_side, 0, 1)
        for lane, out_ref in zip((outer, 1 - outer, 2), out_refs):
            project(rows_ref, level_ref, weight_ref, lane, 1, nodes, out_ref)
        project(rows_ref, level_ref, weight_ref, 3, 1, nodes, part_ref, stat_ref)


def level_rows(level, lanes):
    pieces = []
    rest = level
    for _ in range(3):
        piece = rest.astype(jnp.bfloat16).astype(jnp.float32)
        rest = rest - piece
        pieces.append(piece)
    rows = [
        piece[:, first : first + lanes] for piece in pieces for first in range(0, level.shape[1], lanes)
    ]
    rows.append(jnp.zeros((STAT_ROWS - len(rows), lanes), jnp.float32))
    return jnp.concatenate(rows, axis=0).astype(jnp.bfloat16)


def level_row(block, columns):
    per = columns // block.shape[1]
    block = block.astype(jnp.float32)
    return jnp.concatenate(
        [block[i : i + 1] + block[per + i : per + i + 1] + block[2 * per + i : 2 * per + i + 1] for i in range(per)],
        axis=1,
    )


def merge_kernel(layout, heads, place_ref, length_ref, start_ref, part_ref, stat_ref, live_ref,
                 apart_ref, apart_stat_ref, *refs):
    book = Book(place_ref, length_ref, start_ref, 1)
    request_count, columns, dim_value = part_ref.shape
    nodes = columns // heads
    remote_refs, out_ref = refs[: len(layout)], refs[len(layout)]
    nothing = jnp.full((1, columns), NEGATIVE, jnp.float32)
    requests = [book.request(jnp.int32(place)) for place in range(request_count)]
    levels = [[stat_ref[place : place + 1, :]] for place in range(request_count)]
    values = [[part_ref[place]] for place in range(request_count)]
    for kind, ref in zip(layout, remote_refs):
        if isinstance(kind, bool):
            exists = book.hub == int(kind)
        else:
            exists = functools.reduce(
                jnp.logical_or,
                [(book.position + step >= 0) & (book.position + step < book.size) for step in kind],
            )
        first = request_count - 1 if isinstance(kind, bool) else 0
        for each in range(ref.shape[0]):
            level = level_row(ref[each, columns:, :], columns)
            levels[first + each].append(jnp.where(exists, level, NEGATIVE))
            values[first + each].append(ref[each, :columns, :].astype(jnp.float32))
    levels[-1].append(apart_stat_ref[...])
    values[-1].append(apart_ref[0])
    rows = []
    for request, request_levels in zip(requests, levels):
        top = functools.reduce(jnp.maximum, request_levels)
        weights = [jnp.exp(level - top) for level in request_levels]
        total = live_ref[pl.ds(request, 1), :] / functools.reduce(jnp.add, weights)
        rows += [weight * total for weight in weights]
    rows += [nothing] * (-len(rows) % 8)
    shares = jnp.concatenate(rows, axis=0).T
    at = 0
    for request, request_values in zip(requests, values):
        value = None
        for each in request_values:
            term = each * shares[:, at : at + 1]
            value = term if value is None else value + term
            at += 1
        for head in range(heads):
            piece = value[head * nodes : (head + 1) * nodes].astype(jnp.bfloat16)
            out_ref[request, :, head * dim_value : (head + 1) * dim_value] = piece


VMEM = pl.BlockSpec(memory_space=pltpu.VMEM)
SMEM = pl.BlockSpec(memory_space=pltpu.SMEM)
HBM = pl.BlockSpec(memory_space=pltpu.HBM)
VMEM_LIMIT = 57 << 20


def call(kernel, operands, out_shapes, scratch, flops=0, limit=VMEM_LIMIT, out_space=VMEM):
    return pl.pallas_call(
        kernel,
        in_specs=[spec for spec, _ in operands],
        out_specs=[out_space] * len(out_shapes),
        scratch_shapes=scratch,
        out_shape=[jax.ShapeDtypeStruct(shape, dtype) for shape, dtype in out_shapes],
        compiler_params=pltpu.CompilerParams(vmem_limit_bytes=limit),
        cost_estimate=pl.CostEstimate(flops=flops, bytes_accessed=flops // 256, transcendentals=0),
    )(*[array for _, array in operands])


def after(value, *others):
    return lax.optimization_barrier((value, *others))[0]


def hub_shards(
    queries,
    tree_keys,
    parents,
    node_live,
    lengths,
    start_device,
    cache_latent,
    cache_rope,
    up_weight,
):
    size = lax.axis_size("blk")
    head_size = lax.axis_size("head")
    request_count, width, columns = queries.shape
    page_rows, dim_lat = cache_latent.shape[1:]
    dim_rope = cache_rope.shape[1]
    dim_value = up_weight.shape[2]
    heads = up_weight.shape[0] // size
    nodes = columns // heads
    rows = columns + STAT_ROWS
    block = math.gcd(page_rows, 256)
    scale = 1.0 / math.sqrt(DN + dim_rope)
    most = request_count - 1
    bf16, f32 = jnp.bfloat16, jnp.float32
    dma = pltpu.SemaphoreType.DMA
    position = lax.axis_index("blk")
    here = jnp.stack([position, lax.axis_index("head") % 2, jnp.int32(size)]).astype(jnp.int32)
    scalars = [(SMEM, here), (SMEM, lengths), (SMEM, start_device)]
    pages = [(HBM, cache_latent), (HBM, cache_rope), (HBM, up_weight)]
    unit_flops = 2 * columns * page_rows * (width + dim_lat)

    long, apart = call(
        sort_kernel,
        [(SMEM, lengths), (HBM, queries)],
        [((most, width, columns), bf16), ((1, width, columns), bf16)],
        [pltpu.VMEM((request_count, width, columns), bf16), dma((request_count, 2))],
        out_space=HBM,
    )
    half = page_rows // 2
    pieces = rope_pieces(half, dim_lat)

    def answer(steps, query_groups, own=(), space=HBM, limit=VMEM_LIMIT):
        lanes = len(steps)
        count = request_count if own else most
        operands = scalars + [(space, query) for group in query_groups for query in group]
        if own:
            operands += [(HBM, own[0])]
        operands += pages
        if own:
            operands += [(VMEM, array) for array in own[1:]]
            outs = [((count, columns, dim_value), f32), ((count, columns), f32)]
        else:
            outs = [((count, rows, dim_value), bf16)] * lanes
        reach_size = request_count * nodes if own else 8
        return call(
            functools.partial(page_kernel, steps, bool(own), block, scale),
            operands,
            outs,
            [
                pltpu.VMEM((count, width, lanes * columns), bf16),
                pltpu.VMEM((count, page_rows, dim_lat), bf16),
                pltpu.VMEM((count, dim_rope, page_rows), bf16),
                pltpu.VMEM((lanes, heads, dim_lat, dim_value), bf16),
                pltpu.VMEM((lanes, heads, count * nodes, dim_lat), bf16),
                pltpu.VMEM((lanes, count, columns), f32),
                pltpu.VMEM((page_rows, lanes * columns), f32),
                pltpu.VMEM((reach_size, reach_size), f32),
                dma((count, 2)),
                dma((count, lanes)),
                dma((lanes,)),
            ],
            unit_flops * lanes * count,
            limit,
        )

    def shift(value, pairs):
        return lax.ppermute(value, "blk", pairs)

    right1 = shift(long, [(i, i + 1) for i in range(size - 1)])
    left1 = shift(long, [(i, i - 1) for i in range(1, size)])
    apart_right = shift(apart, [(i, i + 1) for i in range(size - 2)])
    apart_left = shift(apart, [(i, i - 1) for i in range(2, size)])
    parent_row = (parents + nodes * jnp.arange(request_count, dtype=jnp.int32)[:, None]).reshape(1, -1)
    live_rows = jnp.tile(node_live.astype(f32), (1, heads))
    part, stat = answer([[0]], [[long]], (apart, tree_keys, parent_row))
    right2 = shift(after(right1, part), [(i, i + 1) for i in range(1, size - 1)])
    left2 = shift(after(left1, part), [(i, i - 1) for i in range(1, size - 1)])
    (packed,) = call(
        pack_kernel,
        [(SMEM, here), (SMEM, after(lengths, right1, left1)), (HBM, cache_latent), (HBM, cache_rope)],
        [((half + len(pieces) * dim_rope, dim_lat), bf16)],
        [dma((1 + len(pieces),))],
    )
    mine = shift(packed, [(0, 1), (size - 1, size - 2)])
    first = answer([[-1], [1]], [[after(right1, apart_right, apart_left)], [left1]])
    from_right = shift(first[0], [(i, i - 1) for i in range(1, size)])
    from_left = shift(first[1], [(i, i + 1) for i in range(size - 1)])
    swapped = lax.ppermute(
        after(mine, *first),
        ("blk", "head"),
        [(i * head_size + j, i * head_size + (j ^ 1)) for i in (1, size - 2) for j in range(head_size)],
    )
    crossing = jnp.where(position * 2 < size, apart_right, apart_left)
    apart_far = shift(after(crossing, *first), [(1, size - 2), (size - 2, 1)])
    right3 = shift(after(right2, *first), [(size - 2, size - 1)])
    left3 = shift(after(left2, *first), [(1, 0)])
    (second,) = answer([[-2, 2]], [[after(right2, from_right, from_left), left2]])
    from_far = shift(second, [(i, i - 2) for i in range(2, size)] + [(i, i + 2) for i in range(size - 2)])
    outer, inner, distant, apart_part, apart_stat = call(
        functools.partial(hub_kernel, block, scale),
        scalars
        + [
            (HBM, array)
            for array in (
                apart_right, apart_left, after(apart_far, second), apart, mine, swapped
            )
        ]
        + pages,
        [((1, rows, dim_value), bf16)] * 3 + [((1, columns, dim_value), f32), ((1, columns), f32)],
        [
            pltpu.VMEM((2, width, 2 * columns), bf16),
            pltpu.VMEM((2, page_rows, dim_lat), bf16),
            pltpu.VMEM((2, dim_rope, page_rows), bf16),
            pltpu.VMEM((4, heads, dim_lat, dim_value), bf16),
            pltpu.VMEM((4, heads, nodes, dim_lat), bf16),
            pltpu.VMEM((4, 1, columns), f32),
            pltpu.VMEM((page_rows, 2 * columns), f32),
            pltpu.VMEM((8, 2 * columns), f32),
            pltpu.VMEM((dim_lat, 2 * columns), f32),
            dma((4,)),
            dma((2,)),
            dma((2 * (1 + len(pieces)),)),
            dma((4,)),
        ],
        unit_flops * 7,
    )
    from_hub = shift(outer, [(1, 0), (size - 2, size - 1)])
    from_other = shift(inner, [(1, size - 2), (size - 2, 1)])
    from_distant = shift(distant, [(size - 2, 0), (1, size - 1)])
    (third,) = answer(
        [[1 - size, size - 1]], [[after(right3, outer, from_far), left3]], space=VMEM, limit=44 << 20
    )
    from_end = shift(third, [(0, size - 1), (size - 1, 0)])
    layout = [[1], [-1], [-2, 2], [1 - size, size - 1], False, True, False]
    arrays = (
        part, stat, live_rows, apart_part, apart_stat, from_right, from_left, from_far, from_end,
        from_hub, from_other, from_distant,
    )
    (verified,) = call(
        functools.partial(merge_kernel, layout, heads),
        scalars + [(VMEM, array) for array in arrays],
        [((request_count, nodes, heads * dim_value), bf16)],
        [],
        limit=12 << 20,
    )
    return verified


def solution(mesh):
    size = mesh.shape["blk"]
    hubs = size == 4 and mesh.shape["head"] % 2 == 0

    def shards(queries, *rest):
        columns = queries.shape[2]
        cache_latent, _, up_weight = rest[-3:]
        wide = columns % up_weight.shape[2] == 0 and cache_latent.shape[1] % 256 == 0
        if hubs and wide and queries.shape[0] > 1:
            return hub_shards(queries, *rest)
        return gathered_shards(queries, *rest)

    return jax.shard_map(
        shards,
        mesh=mesh,
        in_specs=(
            P("grp", None, ("head", "blk")),
            P("grp", None, None),
            P("grp", None),
            P("grp", None),
            P("grp"),
            P("grp"),
            P("grp", "blk", None),
            P("grp", None, "blk"),
            P("head", None, None),
        ),
        out_specs=P("grp", None, ("head", "blk")),
        check_vma=False,
    )
```

```python
import functools
import math

import jax
import jax.numpy as jnp
from jax import lax
from jax.experimental import pallas as pl
from jax.experimental.pallas import tpu as pltpu
from jax.sharding import PartitionSpec as P

DN = 128

NEGATIVE = -1e30
STAT_ROWS = 16


def merged(value, axis, join):
    pieces = jax.tree.map(lambda part: lax.all_gather(part, axis), value)
    head = jax.tree.map(lambda part: part[0], pieces)
    tail = jax.tree.map(lambda part: part[1:], pieces)
    subtotal, _ = lax.scan(lambda subtotal, slab: (join(subtotal, slab), None), head, tail)
    return subtotal


def ancestor_matrix(parent_list):
    node_count = parent_list.shape[0]
    ordering = jnp.arange(node_count, dtype=jnp.int32)
    one_hop = (parent_list[:, None] == ordering[None, :]).astype(jnp.float32)
    reached = jnp.maximum(one_hop, jnp.eye(node_count, dtype=jnp.float32))
    for _ in range(max(node_count - 1, 1).bit_length()):
        reached = jnp.minimum(jnp.dot(reached, reached, precision=lax.Precision.HIGHEST), 1.0)
    return reached


def softmax_update(running, scores, visible, values):
    top_score, weight_sum, summed = running
    masked = jnp.where(visible, scores, -jnp.inf)
    new_top = jnp.maximum(top_score, jnp.max(masked, axis=1))
    factor = jnp.exp(top_score - new_top)
    expweights = jnp.exp(masked - new_top[:, None])
    summed = summed * factor[:, None] + jnp.dot(
        expweights.astype(jnp.bfloat16), values, preferred_element_type=jnp.float32
    )
    return (new_top, weight_sum * factor + jnp.sum(expweights, axis=1), summed)


def join_stats(first_stats, second_stats):
    top_one, sum_one = first_stats
    top_two, sum_two = second_stats
    top_both = jnp.maximum(top_one, top_two)
    return (top_both, sum_one * jnp.exp(top_one - top_both) + sum_two * jnp.exp(top_two - top_both))


def attend_page(running, query_block, lat_page, rope_page, live_count, score_scale):
    dim_lat = lat_page.shape[1]
    query_lat = query_block[:dim_lat]
    query_rope = query_block[dim_lat:]
    key_block = math.gcd(lat_page.shape[0], 512)

    def block_step(block_index, carried):
        first_key = block_index * key_block
        lat_rows = lax.dynamic_slice_in_dim(lat_page, first_key, key_block, 0)
        rope_rows = lax.dynamic_slice_in_dim(rope_page, first_key, key_block, 1)
        scores = lax.dot_general(
            query_lat, lat_rows, (((0,), (1,)), ((), ())), preferred_element_type=jnp.float32
        )
        scores = scores + lax.dot_general(
            query_rope, rope_rows, (((0,), (0,)), ((), ())), preferred_element_type=jnp.float32
        )
        scores = scores * score_scale
        visible = first_key + jnp.arange(key_block, dtype=jnp.int32) < live_count
        return softmax_update(carried, scores, visible[None, :], lat_rows)

    block_count = (live_count + key_block - 1) // key_block
    return lax.fori_loop(0, block_count, block_step, running)


def fresh_state(columns, dim_lat):
    return (
        jnp.full((columns,), NEGATIVE, jnp.float32),
        jnp.zeros((columns,), jnp.float32),
        jnp.zeros((columns, dim_lat), jnp.float32),
    )


def gathered_shards(
    queries,
    tree_keys,
    parents,
    node_live,
    lengths,
    start_device,
    cache_latent,
    cache_rope,
    up_weight,
):
    cycle_size = lax.axis_size("blk")
    position = lax.axis_index("blk")
    request_count = queries.shape[0]
    local_cols = queries.shape[2]
    node_count = tree_keys.shape[1]
    dim_lat = cache_latent.shape[2]
    dim_rope = cache_rope.shape[1]
    dim_value = up_weight.shape[2]
    page_rows = cache_latent.shape[1]
    own_heads = local_cols // node_count
    score_scale = 1.0 / math.sqrt(DN + dim_rope)
    page_index = (position - start_device) % cycle_size
    live_keys = jnp.clip(lengths - page_index * page_rows, 0, page_rows)
    piece = lax.all_gather(queries, "blk", axis=2, tiled=True)
    piece_cols = piece.shape[2]
    tops = []
    sums = []
    accs = []
    for fold_request in range(request_count):
        fold_outcome = attend_page(
            fresh_state(piece_cols, dim_lat),
            piece[fold_request],
            cache_latent[fold_request],
            cache_rope[fold_request],
            live_keys[fold_request],
            score_scale,
        )
        tops.append(fold_outcome[0])
        sums.append(fold_outcome[1])
        accs.append(fold_outcome[2])
    top_all = jnp.stack(tops)
    sum_all = jnp.stack(sums)
    acc_all = jnp.stack(accs)
    reached = jax.vmap(ancestor_matrix)(parents) > 0.5
    tree_tops, tree_sums, tree_accs = ([], [], [])
    for request in range(request_count):
        tree_scores = (
            lax.dot_general(
                queries[request],
                tree_keys[request],
                (((0,), (1,)), ((), ())),
                preferred_element_type=jnp.float32,
            )
            * score_scale
        )
        visible = jnp.tile(reached[request], (own_heads, 1))
        outcome = softmax_update(
            fresh_state(local_cols, dim_lat), tree_scores, visible, tree_keys[request][:, :dim_lat]
        )
        tree_tops.append(outcome[0])
        tree_sums.append(outcome[1])
        tree_accs.append(outcome[2])
    tree_top = jnp.stack(tree_tops)
    tree_sum = jnp.stack(tree_sums)
    tree_acc = jnp.stack(tree_accs)
    own_start = position * local_cols
    own_top = lax.dynamic_slice_in_dim(top_all, own_start, local_cols, 1)
    own_sum = lax.dynamic_slice_in_dim(sum_all, own_start, local_cols, 1)
    own_acc = lax.dynamic_slice_in_dim(acc_all, own_start, local_cols, 1)
    joined = jnp.maximum(own_top, tree_top)
    first_factor = jnp.exp(own_top - joined)
    second_factor = jnp.exp(tree_top - joined)
    top_all = lax.dynamic_update_slice_in_dim(top_all, joined, own_start, 1)
    sum_all = lax.dynamic_update_slice_in_dim(
        sum_all, own_sum * first_factor + tree_sum * second_factor, own_start, 1
    )
    acc_all = lax.dynamic_update_slice_in_dim(
        acc_all,
        own_acc * first_factor[:, :, None] + tree_acc * second_factor[:, :, None],
        own_start,
        1,
    )
    merged_top, merged_sum = merged((top_all, sum_all), "blk", join_stats)
    scaling = jnp.exp(top_all - merged_top) / merged_sum
    normed = acc_all * scaling[:, :, None]
    head_rows = lax.psum_scatter(
        normed.astype(jnp.bfloat16), "blk", scatter_dimension=1, tiled=True
    ).astype(jnp.float32)
    weight_own = lax.dynamic_slice_in_dim(up_weight, position * own_heads, own_heads, 0).astype(
        jnp.float32
    )
    projected = jnp.einsum(
        "rhnd,hdv->rnhv",
        head_rows.reshape(request_count, own_heads, node_count, dim_lat),
        weight_own,
        precision=lax.Precision.HIGHEST,
    )
    verified = projected.reshape(request_count, node_count, own_heads * dim_value)
    live_nodes = node_live.astype(jnp.float32)[:, :, None]
    return (verified * live_nodes).astype(jnp.bfloat16)


def dot_nn(left, right):
    return jnp.dot(left, right, preferred_element_type=jnp.float32)


def dot_tn(left, right):
    return lax.dot_general(
        left, right, (((0,), (0,)), ((), ())), preferred_element_type=jnp.float32
    )


def reach_closure(parent_row):
    count = parent_row.shape[1]
    row = lax.broadcasted_iota(jnp.int32, (count, count), 0)
    lane = lax.broadcasted_iota(jnp.int32, (count, count), 1)
    reached = jnp.where((row == parent_row) | (row == lane), 1.0, 0.0).astype(jnp.bfloat16)
    return reached


def page_softmax(query, lat_ref, rope_ref, page, keys, blocks, block, scale, score_ref, tree):
    dim_lat = lat_ref.shape[2]
    columns = query.shape[1]
    query_lat, query_rope = query[:dim_lat], query[dim_lat:]
    tops = []
    for index in range(blocks):
        span = slice(index * block, (index + 1) * block)
        scores = dot_nn(lat_ref[page, span, :], query_lat)
        scores = scores + dot_tn(rope_ref[page, :, span], query_rope)
        if index >= blocks - 2:
            place = index * block + lax.broadcasted_iota(jnp.int32, scores.shape, 0)
            scores = jnp.where(place < keys, scores, NEGATIVE)
        score_ref[span, :columns] = scores
        tops.append(jnp.max(scores, axis=0, keepdims=True))
    if tree is not None:
        tree_keys, visible = tree
        tree_scores = jnp.where(visible > 0.5, dot_nn(tree_keys, query), NEGATIVE)
        tops.append(jnp.max(tree_scores, axis=0, keepdims=True))
    top = functools.reduce(jnp.maximum, tops)
    base_two = scale * math.log2(math.e)
    shift = top * base_two
    total = summed = None
    for index in range(blocks):
        span = slice(index * block, (index + 1) * block)
        weights = jnp.exp2(score_ref[span, :columns] * base_two - shift)
        weight_sum = jnp.sum(weights, axis=0, keepdims=True)
        values = dot_tn(lat_ref[page, span, :], weights.astype(jnp.bfloat16))
        total = weight_sum if total is None else total + weight_sum
        summed = values if summed is None else summed + values
    if tree is not None:
        weights = jnp.exp2(tree_scores * base_two - shift)
        weight_sum = jnp.sum(weights, axis=0, keepdims=True)
        values = dot_tn(tree_keys[:, :dim_lat], weights.astype(jnp.bfloat16))
        total = weight_sum if total is None else total + weight_sum
        summed = values if summed is None else summed + values
    return summed, total, top * scale


class Book:
    def __init__(self, place_ref, length_ref, start_ref, page_rows):
        self.position, self.half = place_ref[0], place_ref[1]
        self.size = place_ref[2]
        self.lengths, self.starts = length_ref, start_ref
        self.page_rows = page_rows
        self.count = length_ref.shape[0]
        self.apart = shortest(length_ref)
        self.hub = ((self.position > 0) & (self.position < self.size - 1)).astype(jnp.int32)

    def request(self, place):
        moved = place + (place >= self.apart).astype(jnp.int32)
        return jnp.where(place == self.count - 1, self.apart, moved)

    def live(self, request, position):
        page = lax.rem(position - self.starts[request] + self.size, self.size)
        return jnp.clip(self.lengths[request] - page * self.page_rows, 0, self.page_rows)


def shortest(length_ref):
    best, index = length_ref[0], jnp.int32(0)
    for each in range(1, length_ref.shape[0]):
        less = length_ref[each] < best
        index = jnp.where(less, each, index)
        best = jnp.minimum(best, length_ref[each])
    return index


def sort_kernel(length_ref, query_ref, long_ref, apart_ref, held_ref, sems):
    apart = shortest(length_ref)
    most = long_ref.shape[0]
    stages = []
    for place in range(most + 1):
        if place < most:
            request, target = place + (place >= apart).astype(jnp.int32), long_ref.at[place]
        else:
            request, target = apart, apart_ref.at[0]
        held = held_ref.at[place]
        stages.append(
            (
                pltpu.make_async_copy(query_ref.at[request], held, sems.at[place, 0]),
                pltpu.make_async_copy(held, target, sems.at[place, 1]),
            )
        )
    for fetch, _ in stages:
        fetch.start()
    for fetch, put in stages:
        fetch.wait()
        put.start()
    for _, put in stages:
        put.wait()


def rope_pieces(half, width):
    return [(low, min(width, half - low)) for low in range(0, half, width)]


def pack_kernel(place_ref, length_ref, lat_ref, rope_ref, out_ref, sems):
    apart = shortest(length_ref)
    half = lat_ref.shape[1] // 2
    dim_rope = rope_ref.shape[1]
    width = lat_ref.shape[2]
    low = pl.multiple_of(place_ref[1] * half, 128)
    copies = [
        pltpu.make_async_copy(
            lat_ref.at[apart, pl.ds(low, half), :], out_ref.at[pl.ds(0, half), :], sems.at[0]
        )
    ]
    for index, (at, size) in enumerate(rope_pieces(half, width)):
        copies.append(
            pltpu.make_async_copy(
                rope_ref.at[apart, :, pl.ds(pl.multiple_of(low + at, 128), size)],
                out_ref.at[pl.ds(half + index * dim_rope, dim_rope), pl.ds(0, size)],
                sems.at[index + 1],
            )
        )
    for copy in copies:
        copy.start()
    for copy in copies:
        copy.wait()


def variants(keys, block_count, block, action):
    step = 2 if block_count % 2 == 0 else 1
    for blocks in range(step, block_count + 1, step):

        @pl.when((keys > (blocks - step) * block) & (keys <= blocks * block))
        def _():
            action(blocks)


def spans(place, nodes):
    if isinstance(place, int):
        return slice(place * nodes, (place + 1) * nodes), slice(place, place + 1)
    return pl.ds(pl.multiple_of(place * nodes, nodes), nodes), pl.ds(place, 1)


def store_value(rows_ref, level_ref, lane, place, nodes, summed, total, top):
    heads, _, dim_lat = rows_ref.shape[1:]
    span, line = spans(place, nodes)
    normed = (summed * (1.0 / total)).astype(jnp.bfloat16)
    rows_ref[lane, :, span, :] = normed.T.reshape(heads, nodes, dim_lat)
    level_ref[lane, line, :] = top + jnp.log(total)


def store_nothing(rows_ref, level_ref, lane, place, nodes):
    heads, _, dim_lat = rows_ref.shape[1:]
    span, line = spans(place, nodes)
    rows_ref[lane, :, span, :] = jnp.zeros((heads, nodes, dim_lat), jnp.bfloat16)
    level_ref[lane, line, :] = jnp.full((1, level_ref.shape[2]), NEGATIVE, jnp.float32)


def project(rows_ref, level_ref, weight_ref, lane, count, nodes, out_ref, stat_ref=None):
    heads = rows_ref.shape[1]
    columns, dim_value = level_ref.shape[2], weight_ref.shape[3]
    for head in range(heads):
        value = dot_nn(rows_ref[lane, head], weight_ref[lane, head])
        for each in range(count):
            piece = value[each * nodes : (each + 1) * nodes].astype(out_ref.dtype)
            out_ref[each, head * nodes : (head + 1) * nodes, :] = piece
    if stat_ref is not None:
        stat_ref[...] = level_ref[lane]
        return
    for each in range(count):
        out_ref[each, columns:, :] = level_rows(level_ref[lane, each : each + 1, :], dim_value)


def page_kernel(steps, own, block, scale, place_ref, length_ref, start_ref, *refs):
    refs = list(refs)
    query_hbm = [[refs.pop(0) for _ in group] for group in steps]
    if own:
        apart_hbm = refs.pop(0)
    lat_hbm, rope_hbm, weight_hbm = refs.pop(0), refs.pop(0), refs.pop(0)
    if own:
        tree_ref, parent_ref, part_ref, stat_ref = [refs.pop(0) for _ in range(4)]
        out_refs = [part_ref]
    else:
        out_refs = [refs.pop(0) for _ in steps]
    query_ref, lat_ref, rope_ref, weight_ref, rows_ref, level_ref, score_ref, reach_ref = refs[:8]
    page_sems, query_sems, weight_sems = refs[8:]
    page_rows = lat_ref.shape[1]
    book = Book(place_ref, length_ref, start_ref, page_rows)
    heads, columns = weight_ref.shape[1], level_ref.shape[2]
    nodes = columns // heads
    lanes = len(steps)
    count = book.count - (0 if own else 1)
    block_count = page_rows // block

    flags = []
    shards = []
    exist = []
    for group in steps:
        flag = shard = jnp.int32(0)
        each = []
        for step in group:
            there = book.position + step
            exists = ((there >= 0) & (there < book.size)).astype(jnp.int32)
            each.append(exists)
            flag = flag + exists
            shard = shard + exists * there
        flags.append(flag)
        shards.append(shard)
        exist.append(each)
    any_flag = jnp.minimum(functools.reduce(jnp.add, flags), 1)

    def keys_at(place):
        request = book.request(place)
        keys = book.live(request, book.position) * any_flag
        if own:
            keys = keys * jnp.where(place == count - 1, book.hub, 1)
        return request, keys

    def page_copies(place, request):
        return [
            pltpu.make_async_copy(lat_hbm.at[request], lat_ref.at[place], page_sems.at[place, 0]),
            pltpu.make_async_copy(rope_hbm.at[request], rope_ref.at[place], page_sems.at[place, 1]),
        ]

    def query_copy(ref, place, lane):
        target = query_ref.at[place, :, lane * columns : (lane + 1) * columns]
        return pltpu.make_async_copy(ref, target, query_sems.at[place, lane])

    def weight_copy(lane):
        low = pl.multiple_of(shards[lane] * heads, heads)
        return pltpu.make_async_copy(
            weight_hbm.at[pl.ds(low, heads)], weight_ref.at[lane], weight_sems.at[lane]
        )

    for place in range(count):
        request, keys = keys_at(jnp.int32(place))
        for lane, group in enumerate(query_hbm):
            for ref, exists in zip(group, exist[lane]):
                source = apart_hbm.at[0] if own and place == count - 1 else ref.at[place]

                @pl.when(exists * (keys + int(own)) > 0)
                def _():
                    query_copy(source, place, lane).start()

        @pl.when(keys > 0)
        def _():
            for copy in page_copies(place, request):
                copy.start()

    for lane in range(lanes):

        @pl.when(flags[lane] > 0)
        def _():
            weight_copy(lane).start()

    if own:
        reached = reach_closure(parent_ref[...])
        for _ in range(max(nodes - 1, 1).bit_length()):
            reached = jnp.minimum(dot_nn(reached, reached), 1.0).astype(jnp.bfloat16)
        reach_ref[...] = reached.astype(jnp.float32)

    def item_step(place, carry):
        request, keys = keys_at(place)
        for lane, group in enumerate(query_hbm):

            @pl.when(flags[lane] * (keys + int(own)) > 0)
            def _():
                query_copy(group[0].at[0], place, lane).wait()

        @pl.when(keys > 0)
        def _():
            for copy in page_copies(place, request):
                copy.wait()

        def attend(blocks, query):
            tree = None
            if own:
                base = pl.multiple_of(request * nodes, nodes)
                row = lax.broadcasted_iota(jnp.int32, (reach_ref.shape[1], columns), 0)
                along = lax.broadcasted_iota(jnp.int32, (reach_ref.shape[1], columns), 1)
                pick = jnp.where(row == base + along % nodes, 1.0, 0.0).astype(jnp.bfloat16)
                near = reach_ref[pl.ds(base, nodes), :].astype(jnp.bfloat16)
                tree = (tree_ref[request], dot_nn(near, pick))
            return page_softmax(
                query, lat_ref, rope_ref, place, keys, blocks, block, scale, score_ref, tree
            )

        def attend_one(lane):
            def action(blocks):
                if isinstance(lane, int):
                    query = query_ref[place, :, lane * columns : (lane + 1) * columns]
                else:
                    query = query_ref[place, :, pl.ds(pl.multiple_of(lane * columns, columns), columns)]
                store_value(rows_ref, level_ref, lane, place, nodes, *attend(blocks, query))

            return action

        def attend_all(blocks):
            summed, total, top = attend(blocks, query_ref[place])
            for lane in range(lanes):
                span = slice(lane * columns, (lane + 1) * columns)
                store_value(
                    rows_ref, level_ref, lane, place, nodes, summed[:, span], total[:, span], top[:, span]
                )

        if lanes == 1:
            variants(keys, block_count, block, attend_one(0))
        else:
            together = functools.reduce(jnp.multiply, flags)
            alone = functools.reduce(
                jnp.add, [lane * flag for lane, flag in enumerate(flags)]
            ) * (1 - together)
            variants(keys * together, block_count, block, attend_all)
            variants(keys * (1 - together), block_count, block, attend_one(alone))

        @pl.when(keys <= 0)
        def _():
            if own:
                attend_one(0)(0)
            else:
                for lane in range(lanes):
                    store_nothing(rows_ref, level_ref, lane, place, nodes)

        return carry

    lax.fori_loop(0, count * any_flag, item_step, 0)
    for lane in range(lanes):

        @pl.when(flags[lane] > 0)
        def _():
            weight_copy(lane).wait()
            project(
                rows_ref, level_ref, weight_ref, lane, count, nodes, out_refs[lane],
                stat_ref if own else None,
            )


def hub_kernel(block, scale, place_ref, length_ref, start_ref, *refs):
    refs = list(refs)
    query_hbm = [refs.pop(0) for _ in range(4)]
    mine_hbm, other_hbm, lat_hbm, rope_hbm, weight_hbm = [refs.pop(0) for _ in range(5)]
    out_refs = [refs.pop(0) for _ in range(3)]
    part_ref, stat_ref = refs.pop(0), refs.pop(0)
    query_ref, lat_ref, rope_ref, weight_ref, rows_ref, level_ref, score_ref = refs[:7]
    sum_ref, acc_ref, query_sems, page_sems, end_sems, weight_sems = refs[7:]
    page_rows, dim_lat = lat_ref.shape[1:]
    dim_rope = rope_ref.shape[1]
    book = Book(place_ref, length_ref, start_ref, page_rows)
    heads, columns = weight_ref.shape[1], level_ref.shape[2]
    nodes = columns // heads
    half = page_rows // 2
    block_count = page_rows // block
    request = book.apart
    low_side = book.position * 2 < book.size
    end = jnp.where(low_side, 0, book.size - 1)
    far = jnp.where(low_side, book.position + 2, book.position - 2)
    shards = [book.position - 1, book.position + 1, far, book.position]
    live = [book.live(request, book.position), book.live(request, end)]

    @pl.when(book.hub == 0)
    def _():
        nothing = level_rows(jnp.full((1, columns), NEGATIVE, jnp.float32), part_ref.shape[2])
        for out_ref in out_refs:
            out_ref[0, :columns, :] = jnp.zeros((columns, out_ref.shape[2]), out_ref.dtype)
            out_ref[0, columns:, :] = nothing
        part_ref[...] = jnp.zeros_like(part_ref)
        stat_ref[...] = jnp.full_like(stat_ref, NEGATIVE)

    @pl.when(book.hub > 0)
    def _():
        copies = [
            pltpu.make_async_copy(
                ref.at[0],
                query_ref.at[lane // 2, :, lane % 2 * columns : (lane % 2 + 1) * columns],
                query_sems.at[lane],
            )
            for lane, ref in enumerate(query_hbm)
        ]
        copies.append(pltpu.make_async_copy(lat_hbm.at[request], lat_ref.at[0], page_sems.at[0]))
        copies.append(pltpu.make_async_copy(rope_hbm.at[request], rope_ref.at[0], page_sems.at[1]))
        at_sem = 0
        for ref, part in ((mine_hbm, book.half), (other_hbm, 1 - book.half)):
            low = pl.multiple_of(part * half, 128)
            copies.append(
                pltpu.make_async_copy(
                    ref.at[pl.ds(0, half), :], lat_ref.at[1, pl.ds(low, half), :], end_sems.at[at_sem]
                )
            )
            at_sem += 1
            for index, (at, size) in enumerate(rope_pieces(half, dim_lat)):
                copies.append(
                    pltpu.make_async_copy(
                        ref.at[pl.ds(half + index * dim_rope, dim_rope), pl.ds(0, size)],
                        rope_ref.at[1, :, pl.ds(pl.multiple_of(low + at, 128), size)],
                        end_sems.at[at_sem],
                    )
                )
                at_sem += 1
        weight_copies = [
            pltpu.make_async_copy(
                weight_hbm.at[pl.ds(pl.multiple_of(shard * heads, heads), heads)],
                weight_ref.at[lane],
                weight_sems.at[lane],
            )
            for lane, shard in enumerate(shards)
        ]
        for copy in copies + weight_copies:
            copy.start()
        for copy in copies:
            copy.wait()

        def group_step(item, carry):
            group, page = lax.div(item, 2), lax.rem(item, 2)
            keys = jnp.where(page == 0, live[0], live[1])
            narrow = (group == 1) & (page == 0)

            @pl.when(page == 0)
            def _():
                sum_ref[0:1, :] = jnp.zeros((1, 2 * columns), jnp.float32)
                sum_ref[1:2, :] = jnp.full((1, 2 * columns), NEGATIVE, jnp.float32)
                acc_ref[...] = jnp.zeros_like(acc_ref)

            def attend(width):
                def action(blocks):
                    summed, total, top = page_softmax(
                        query_ref[group, :, :width], lat_ref, rope_ref, page, keys, blocks, block, scale,
                        score_ref, None,
                    )
                    old_top = sum_ref[1:2, :width]
                    new_top = jnp.maximum(old_top, top)
                    old_share, new_share = jnp.exp(old_top - new_top), jnp.exp(top - new_top)
                    sum_ref[0:1, :width] = sum_ref[0:1, :width] * old_share + total * new_share
                    sum_ref[1:2, :width] = new_top
                    acc_ref[:, :width] = acc_ref[:, :width] * old_share + summed * new_share

                return action

            variants(jnp.where(narrow, 0, keys), block_count, block, attend(2 * columns))
            variants(jnp.where(narrow, keys, 0), block_count, block, attend(columns))

            @pl.when(page == 1)
            def _():
                for side in range(2):
                    lane = group * 2 + side
                    span = slice(side * columns, (side + 1) * columns)
                    some = live[1] + (live[0] if side == 0 else jnp.where(group == 1, 0, live[0]))

                    @pl.when(some > 0)
                    def _():
                        outcome = acc_ref[:, span], sum_ref[0:1, span], sum_ref[1:2, span]
                        store_value(rows_ref, level_ref, lane, 0, nodes, *outcome)

                    @pl.when(some <= 0)
                    def _():
                        store_nothing(rows_ref, level_ref, lane, 0, nodes)

            return carry

        lax.fori_loop(0, 4, group_step, 0)
        for copy in weight_copies:
            copy.wait()
        outer = jnp.where(low_side, 0, 1)
        for lane, out_ref in zip((outer, 1 - outer, 2), out_refs):
            project(rows_ref, level_ref, weight_ref, lane, 1, nodes, out_ref)
        project(rows_ref, level_ref, weight_ref, 3, 1, nodes, part_ref, stat_ref)


def level_rows(level, lanes):
    pieces = []
    rest = level
    for _ in range(3):
        piece = rest.astype(jnp.bfloat16).astype(jnp.float32)
        rest = rest - piece
        pieces.append(piece)
    rows = [
        piece[:, first : first + lanes] for piece in pieces for first in range(0, level.shape[1], lanes)
    ]
    rows.append(jnp.zeros((STAT_ROWS - len(rows), lanes), jnp.float32))
    return jnp.concatenate(rows, axis=0).astype(jnp.bfloat16)


def level_row(block, columns):
    per = columns // block.shape[1]
    block = block.astype(jnp.float32)
    return jnp.concatenate(
        [block[i : i + 1] + block[per + i : per + i + 1] + block[2 * per + i : 2 * per + i + 1] for i in range(per)],
        axis=1,
    )


def merge_kernel(layout, heads, place_ref, length_ref, start_ref, part_ref, stat_ref, live_ref,
                 apart_ref, apart_stat_ref, *refs):
    book = Book(place_ref, length_ref, start_ref, 1)
    request_count, columns, dim_value = part_ref.shape
    nodes = columns // heads
    remote_refs, out_ref = refs[: len(layout)], refs[len(layout)]
    nothing = jnp.full((1, columns), NEGATIVE, jnp.float32)
    requests = [book.request(jnp.int32(place)) for place in range(request_count)]
    levels = [[stat_ref[place : place + 1, :]] for place in range(request_count)]
    values = [[part_ref[place]] for place in range(request_count)]
    for kind, ref in zip(layout, remote_refs):
        if isinstance(kind, bool):
            exists = book.hub == int(kind)
        else:
            exists = functools.reduce(
                jnp.logical_or,
                [(book.position + step >= 0) & (book.position + step < book.size) for step in kind],
            )
        first = request_count - 1 if isinstance(kind, bool) else 0
        for each in range(ref.shape[0]):
            level = level_row(ref[each, columns:, :], columns)
            levels[first + each].append(jnp.where(exists, level, NEGATIVE))
            values[first + each].append(ref[each, :columns, :].astype(jnp.float32))
    levels[-1].append(apart_stat_ref[...])
    values[-1].append(apart_ref[0])
    rows = []
    for request, request_levels in zip(requests, levels):
        top = functools.reduce(jnp.maximum, request_levels)
        weights = [jnp.exp(level - top) for level in request_levels]
        total = live_ref[pl.ds(request, 1), :] / functools.reduce(jnp.add, weights)
        rows += [weight * total for weight in weights]
    rows += [nothing] * (-len(rows) % 8)
    shares = jnp.concatenate(rows, axis=0).T
    at = 0
    for request, request_values in zip(requests, values):
        value = None
        for each in request_values:
            term = each * shares[:, at : at + 1]
            value = term if value is None else value + term
            at += 1
        for head in range(heads):
            piece = value[head * nodes : (head + 1) * nodes].astype(jnp.bfloat16)
            out_ref[request, :, head * dim_value : (head + 1) * dim_value] = piece


VMEM = pl.BlockSpec(memory_space=pltpu.VMEM)
SMEM = pl.BlockSpec(memory_space=pltpu.SMEM)
HBM = pl.BlockSpec(memory_space=pltpu.HBM)
VMEM_LIMIT = 57 << 20


def call(kernel, operands, out_shapes, scratch, flops=0, limit=VMEM_LIMIT, out_space=VMEM):
    return pl.pallas_call(
        kernel,
        in_specs=[spec for spec, _ in operands],
        out_specs=[out_space] * len(out_shapes),
        scratch_shapes=scratch,
        out_shape=[jax.ShapeDtypeStruct(shape, dtype) for shape, dtype in out_shapes],
        compiler_params=pltpu.CompilerParams(vmem_limit_bytes=limit),
        cost_estimate=pl.CostEstimate(flops=flops, bytes_accessed=flops // 256, transcendentals=0),
    )(*[array for _, array in operands])


def after(value, *others):
    return lax.optimization_barrier((value, *others))[0]


def hub_shards(
    queries,
    tree_keys,
    parents,
    node_live,
    lengths,
    start_device,
    cache_latent,
    cache_rope,
    up_weight,
):
    size = lax.axis_size("blk")
    head_size = lax.axis_size("head")
    request_count, width, columns = queries.shape
    page_rows, dim_lat = cache_latent.shape[1:]
    dim_rope = cache_rope.shape[1]
    dim_value = up_weight.shape[2]
    heads = up_weight.shape[0] // size
    nodes = columns // heads
    rows = columns + STAT_ROWS
    block = math.gcd(page_rows, 256)
    scale = 1.0 / math.sqrt(DN + dim_rope)
    most = request_count - 1
    bf16, f32 = jnp.bfloat16, jnp.float32
    dma = pltpu.SemaphoreType.DMA
    position = lax.axis_index("blk")
    here = jnp.stack([position, lax.axis_index("head") % 2, jnp.int32(size)]).astype(jnp.int32)
    scalars = [(SMEM, here), (SMEM, lengths), (SMEM, start_device)]
    pages = [(HBM, cache_latent), (HBM, cache_rope), (HBM, up_weight)]
    unit_flops = 2 * columns * page_rows * (width + dim_lat)

    long, apart = call(
        sort_kernel,
        [(SMEM, lengths), (HBM, queries)],
        [((most, width, columns), bf16), ((1, width, columns), bf16)],
        [pltpu.VMEM((request_count, width, columns), bf16), dma((request_count, 2))],
        out_space=HBM,
    )
    half = page_rows // 2
    pieces = rope_pieces(half, dim_lat)

    def answer(steps, query_groups, own=()):
        lanes = len(steps)
        count = request_count if own else most
        operands = scalars + [(HBM, query) for group in query_groups for query in group]
        if own:
            operands += [(HBM, own[0])]
        operands += pages
        if own:
            operands += [(VMEM, array) for array in own[1:]]
            outs = [((count, columns, dim_value), f32), ((count, columns), f32)]
        else:
            outs = [((count, rows, dim_value), bf16)] * lanes
        reach_size = request_count * nodes if own else 8
        return call(
            functools.partial(page_kernel, steps, bool(own), block, scale),
            operands,
            outs,
            [
                pltpu.VMEM((count, width, lanes * columns), bf16),
                pltpu.VMEM((count, page_rows, dim_lat), bf16),
                pltpu.VMEM((count, dim_rope, page_rows), bf16),
                pltpu.VMEM((lanes, heads, dim_lat, dim_value), bf16),
                pltpu.VMEM((lanes, heads, count * nodes, dim_lat), bf16),
                pltpu.VMEM((lanes, count, columns), f32),
                pltpu.VMEM((page_rows, lanes * columns), f32),
                pltpu.VMEM((reach_size, reach_size), f32),
                dma((count, 2)),
                dma((count, lanes)),
                dma((lanes,)),
            ],
            unit_flops * lanes * count,
        )

    def shift(value, pairs):
        return lax.ppermute(value, "blk", pairs)

    right1 = shift(long, [(i, i + 1) for i in range(size - 1)])
    left1 = shift(long, [(i, i - 1) for i in range(1, size)])
    apart_right = shift(apart, [(i, i + 1) for i in range(size - 2)])
    apart_left = shift(apart, [(i, i - 1) for i in range(2, size)])
    parent_row = (parents + nodes * jnp.arange(request_count, dtype=jnp.int32)[:, None]).reshape(1, -1)
    live_rows = jnp.tile(node_live.astype(f32), (1, heads))
    part, stat = answer([[0]], [[long]], (apart, tree_keys, parent_row))
    right2 = shift(after(right1, part), [(i, i + 1) for i in range(1, size - 1)])
    left2 = shift(after(left1, part), [(i, i - 1) for i in range(1, size - 1)])
    (packed,) = call(
        pack_kernel,
        [(SMEM, here), (SMEM, after(lengths, right1, left1)), (HBM, cache_latent), (HBM, cache_rope)],
        [((half + len(pieces) * dim_rope, dim_lat), bf16)],
        [dma((1 + len(pieces),))],
    )
    mine = shift(packed, [(0, 1), (size - 1, size - 2)])
    first = answer([[-1], [1]], [[after(right1, apart_right, apart_left)], [left1]])
    from_right = shift(first[0], [(i, i - 1) for i in range(1, size)])
    from_left = shift(first[1], [(i, i + 1) for i in range(size - 1)])
    swapped = lax.ppermute(
        after(mine, *first),
        ("blk", "head"),
        [(i * head_size + j, i * head_size + (j ^ 1)) for i in (1, size - 2) for j in range(head_size)],
    )
    crossing = jnp.where(position * 2 < size, apart_right, apart_left)
    apart_far = shift(after(crossing, *first), [(1, size - 2), (size - 2, 1)])
    right3 = shift(after(right2, *first), [(size - 2, size - 1)])
    left3 = shift(after(left2, *first), [(1, 0)])
    (second,) = answer([[-2, 2]], [[right2, left2]])
    from_far = shift(second, [(i, i - 2) for i in range(2, size)] + [(i, i + 2) for i in range(size - 2)])
    outer, inner, distant, apart_part, apart_stat = call(
        functools.partial(hub_kernel, block, scale),
        scalars
        + [
            (HBM, array)
            for array in (
                apart_right, apart_left, after(apart_far, second), apart, mine, swapped
            )
        ]
        + pages,
        [((1, rows, dim_value), bf16)] * 3 + [((1, columns, dim_value), f32), ((1, columns), f32)],
        [
            pltpu.VMEM((2, width, 2 * columns), bf16),
            pltpu.VMEM((2, page_rows, dim_lat), bf16),
            pltpu.VMEM((2, dim_rope, page_rows), bf16),
            pltpu.VMEM((4, heads, dim_lat, dim_value), bf16),
            pltpu.VMEM((4, heads, nodes, dim_lat), bf16),
            pltpu.VMEM((4, 1, columns), f32),
            pltpu.VMEM((page_rows, 2 * columns), f32),
            pltpu.VMEM((8, 2 * columns), f32),
            pltpu.VMEM((dim_lat, 2 * columns), f32),
            dma((4,)),
            dma((2,)),
            dma((2 * (1 + len(pieces)),)),
            dma((4,)),
        ],
        unit_flops * 7,
    )
    from_hub = shift(outer, [(1, 0), (size - 2, size - 1)])
    from_other = shift(inner, [(1, size - 2), (size - 2, 1)])
    from_distant = shift(distant, [(size - 2, 0), (1, size - 1)])
    (third,) = answer([[1 - size, size - 1]], [[after(right3, outer), left3]])
    from_end = shift(third, [(0, size - 1), (size - 1, 0)])
    layout = [[1], [-1], [-2, 2], [1 - size, size - 1], False, True, False]
    arrays = (
        part, stat, live_rows, apart_part, apart_stat, from_right, from_left, from_far, from_end,
        from_hub, from_other, from_distant,
    )
    (verified,) = call(
        functools.partial(merge_kernel, layout, heads),
        scalars + [(VMEM, array) for array in arrays],
        [((request_count, nodes, heads * dim_value), bf16)],
        [],
        limit=12 << 20,
    )
    return verified


def solution(mesh):
    size = mesh.shape["blk"]
    hubs = size == 4 and mesh.shape["head"] % 2 == 0

    def shards(queries, *rest):
        columns = queries.shape[2]
        cache_latent, _, up_weight = rest[-3:]
        wide = columns % up_weight.shape[2] == 0 and cache_latent.shape[1] % 256 == 0
        if hubs and wide and queries.shape[0] > 1:
            return hub_shards(queries, *rest)
        return gathered_shards(queries, *rest)

    return jax.shard_map(
        shards,
        mesh=mesh,
        in_specs=(
            P("grp", None, ("head", "blk")),
            P("grp", None, None),
            P("grp", None),
            P("grp", None),
            P("grp"),
            P("grp"),
            P("grp", "blk", None),
            P("grp", None, "blk"),
            P("head", None, None),
        ),
        out_specs=P("grp", None, ("head", "blk")),
        check_vma=False,
    )
```
